32 devices in a mesh: groups: 1, patch: 32 (over z, y, x, core), level: 1.
Axes of the slice: x: 2, y: 2, z: 4, core: 2. Of those that a mesh axis runs over, the one named last changes fastest.
Arguments:
- layer_input: bfloat16 [1, 4096, 1536], P('groups', 'patch', 'level'), may hold values from -24 to 24, as said below
- cotangent: bfloat16 [1, 4096, 1536], P('groups', 'patch', 'level'), may hold values from -6 to 6
- neighbours: int32 [4096, 6], P('patch'), may hold values from 0 to 192, as said below
- boundary: int32 [32, 64], P('patch'), may hold values from 0 to 127, as said below
- gauge_index: int32 [4096, 6], P('patch'), may hold values from 0 to 1023
- gauge_angles: float32 [1024], replicated, may hold values from -3.140625 to 3.140625
- norm_gain: float32 [1536], replicated, may hold values from 0.5 to 1.5
- up_weight: bfloat16 [1536, 2048], P('patch', 'level'), may hold values from -0.15625 to 0.15625
- down_weight: bfloat16 [1536, 2048], P('patch', 'level'), may hold values from -0.125 to 0.125
- self_real: bfloat16 [32, 32], replicated, may hold values from -0.75 to 0.75
- self_imag: bfloat16 [32, 32], replicated, may hold values from -0.75 to 0.75
- near_real: bfloat16 [32, 32], replicated, may hold values from -1.5 to 1.5
- near_imag: bfloat16 [32, 32], replicated, may hold values from -1.5 to 1.5
Outputs:
- layer_grad: bfloat16 [1, 4096, 1536], P('groups', 'patch', 'level')
The draws below stay inside these ranges and needn't reach their ends.
Inputs may be any that keep to these rules, and one draw needn't show every extreme that they name: `layer_input`: the layer input is a real field; rows and features carry differing scales. `neighbours`: entry i of a column's row refers to its patch's extended rows: i < 128 is the patch's own column i, then 32 boundary columns of the previous patch in the cycle, then 32 of the next one; 192 appears only in the last entry and marks an absent neighbour. `boundary`: row p holds 64 distinct local columns of patch p: the first 32 are seen by patch p - 1, the rest by patch p + 1 (patches form a cycle).
All inputs are finite; a program needn't handle non-finite values.
Results may differ from the reference program's by a relative error of at most 0.014.
Values may be sent and summed in bfloat16 or wider, within the bound.
No kernel may reach another device: no remote copies, remote signals or barrier semaphores. Data moves between devices by JAX's collectives and lax.ppermute only.
A program may use at most 64 MiB of HBM per device.

```python
import math
import jax
import jax.numpy as jnp
from jax import lax

CH = 64
HID = 2048
CW = 1536
COLS_DEV = 128
BATCH = 1
NB = 32
NANG = 1024
COLUMNS = 4096
EXT = 192
N_PATCH = 32


def draw_layer_input(key, part):
    keys = jax.random.split(key, 3)
    row_scale = jnp.exp(jax.random.uniform(keys[1], (BATCH, COLUMNS, 1), jnp.float32, math.log(0.3), math.log(3.0)))
    feature_scale = jnp.exp(jax.random.uniform(keys[2], (1, 1, CW), jnp.float32, math.log(0.5), math.log(2.0)))
    base_values = jnp.clip(jax.random.normal(keys[0], (BATCH, COLUMNS, CW), jnp.float32), -4.0, 4.0)
    return (base_values * row_scale * feature_scale).astype(jnp.bfloat16)


def draw_neighbours(key, part):
    first_key, second_key = jax.random.split(key)
    drawn_ids = jax.random.randint(first_key, (COLUMNS, 6), 0, COLS_DEV + 2 * NB)
    lacking = jax.random.randint(second_key, (COLUMNS,), 0, 16) == 0
    lacking = lacking | (jnp.arange(COLUMNS) == 0)
    final_entry = jnp.where(lacking, COLS_DEV + 2 * NB, drawn_ids[:, 5])
    return jnp.concatenate([drawn_ids[:, :5], final_entry[:, None]], axis=1).astype(jnp.int32)


def draw_boundary(key, part):
    row_keys = jax.random.split(key, N_PATCH)

    def one_row(row_key):
        return jax.random.permutation(row_key, COLS_DEV)[:2 * NB]
    return jax.vmap(one_row)(row_keys).astype(jnp.int32)


def place_ends(values, key, low, largest):
    dims = values.shape
    index_at = [jax.random.randint(jax.random.fold_in(key, axis), (), 0, dims[axis]) for axis in range(len(dims))]
    values = values.at[tuple(index_at)].set(low)
    longest = dims.index(max(dims))
    index_at[longest] = (index_at[longest] + 1) % dims[longest]
    return values.at[tuple(index_at)].set(largest)


def levels(own_key, dims, pieces, least, top_value):
    def one(dim, shards_of):
        steps = jax.random.uniform(jax.random.fold_in(jax.random.fold_in(own_key, 6), dim), (shards_of,), jnp.float32, least / len(pieces), top_value / len(pieces))
        return jnp.repeat(jnp.exp(steps), dims[dim] // shards_of).reshape((-1,) + (1,) * (len(dims) - dim - 1))

    level = one(*pieces[0])
    for cut in pieces[1:]:
        level = level * one(*cut)
    return level


def normal_values(own_key, shape, scale, bound, shards=(), kind=jnp.bfloat16):
    values = scale * jax.random.normal(own_key, shape, jnp.float32)
    if shards:
        values = values * levels(own_key, shape, shards, -0.22, 0.18)
    return jnp.clip(values, -bound, bound).astype(kind)


def setup_inputs(seed: int = 0, part: int = 0) -> dict:
    streams_of = jax.random.split(jax.random.key(seed), 14)
    own_keys = jax.random.split(jax.random.fold_in(streams_of[13], part), 14)
    return {
        "layer_input": draw_layer_input(jax.random.fold_in(jax.random.fold_in(streams_of[13], part), 71), part),
        "cotangent": normal_values(own_keys[1], (BATCH, COLUMNS, CW), 1.0, 6.0, ((1, 32),)),
        "neighbours": draw_neighbours(jax.random.fold_in(streams_of[13], 71), part),
        "boundary": draw_boundary(jax.random.fold_in(streams_of[13], 71), part),
        "gauge_index": place_ends(jax.random.randint(streams_of[4], (COLUMNS, 6), 0, NANG), jax.random.fold_in(streams_of[4], 1), 0, NANG - 1).astype(jnp.int32),
        "gauge_angles": jnp.clip(jax.random.uniform(streams_of[5], (NANG,), jnp.float32, -3.140625, 3.140625), -3.140625, 3.140625),
        "norm_gain": jnp.clip(jax.random.uniform(streams_of[6], (CW,), jnp.float32, 0.5, 1.5), 0.5, 1.5),
        "up_weight": normal_values(streams_of[7], (CW, HID), CW ** -0.5, 0.15625, ((0, 32),)),
        "down_weight": normal_values(streams_of[8], (CW, HID), HID ** -0.5, 0.125, ((0, 32),)),
        "self_real": normal_values(streams_of[9], (CH // 2, CH // 2), CH ** -0.5, 0.75),
        "self_imag": normal_values(streams_of[10], (CH // 2, CH // 2), CH ** -0.5, 0.75),
        "near_real": normal_values(streams_of[11], (CH // 2, CH // 2), (CH // 4) ** -0.5, 1.5),
        "near_imag": normal_values(streams_of[12], (CH // 2, CH // 2), (CH // 4) ** -0.5, 1.5),
    }


def real_form(real_part, imag_part):
    upper = jnp.concatenate([real_part, imag_part], axis=1)
    lower = jnp.concatenate([-imag_part, real_part], axis=1)
    return jnp.concatenate([upper, lower], axis=0)

def rotate_quarter(values, channels):
    shape = values.shape
    split = values.reshape(shape[:-1] + (shape[-1] // channels, 2, channels // 2))
    turned = jnp.stack([-split[..., 1, :], split[..., 0, :]], axis=-2)
    return turned.reshape(shape)

def per_level(values, form, channels):
    shape = values.shape
    split = values.reshape(shape[:-1] + (shape[-1] // channels, channels)).astype(jnp.float32)
    result = jnp.einsum('clw,wv->clv', split, form.astype(jnp.float32))
    return result.reshape(shape)

def mlp_back(columns_in, grads, norm_gain, up_weight, down_weight):
    values = columns_in.astype(jnp.float32)
    root_scale = lax.rsqrt(lax.optimization_barrier(jnp.mean(values * values, axis=-1, keepdims=True)) + 1e-05)
    normed = (values * root_scale * norm_gain).astype(jnp.bfloat16)
    pre_act = jnp.dot(normed, up_weight, preferred_element_type=jnp.float32)
    back_hidden = jnp.dot(grads, down_weight, preferred_element_type=jnp.float32)
    sigmoid_pre = jax.nn.sigmoid(pre_act)
    grad_pre = (back_hidden * sigmoid_pre * (1.0 + pre_act * (1.0 - sigmoid_pre))).astype(jnp.bfloat16)
    grad_normed = jnp.dot(grad_pre, up_weight.T, preferred_element_type=jnp.float32)
    mixed_mean = lax.optimization_barrier(jnp.mean(norm_gain * grad_normed * values, axis=-1, keepdims=True))
    return root_scale * norm_gain * grad_normed - values * root_scale * root_scale * root_scale * mixed_mean

def reference(layer_input, cotangent, neighbours, boundary, gauge_index, gauge_angles, norm_gain, up_weight, down_weight, self_real, self_imag, near_real, near_imag):
    position = jnp.arange(COLUMNS, dtype=jnp.int32)
    patch_of = position // COLS_DEV
    before = ((patch_of - 1) % N_PATCH)[:, None]
    after = ((patch_of + 1) % N_PATCH)[:, None]
    own_source = patch_of[:, None] * COLS_DEV + neighbours
    from_before = before * COLS_DEV + boundary[before, NB + jnp.clip(neighbours - COLS_DEV, 0, NB - 1)]
    from_after = after * COLS_DEV + boundary[after, jnp.clip(neighbours - COLS_DEV - NB, 0, NB - 1)]
    source = jnp.where(neighbours < COLS_DEV, own_source, jnp.where(neighbours < COLS_DEV + NB, from_before, jnp.where(neighbours < EXT, from_after, 0))).astype(jnp.int32)
    present = (neighbours < EXT).astype(jnp.float32)
    edge_weight = present / lax.optimization_barrier(jnp.sum(present, axis=1, keepdims=True))
    phase = gauge_angles[gauge_index]
    cosine = jnp.cos(phase)
    sine = jnp.sin(phase)
    near_form = real_form(near_real, near_imag)
    self_form = real_form(self_real, self_imag)
    block_rows = math.gcd(COLUMNS, 2048)

    def mlp_block(pair):
        return mlp_back(pair[0], pair[1], norm_gain, up_weight, down_weight)

    def one_sample(pair):
        inputs, grads = pair
        gathered = jnp.zeros((COLUMNS, CW), jnp.float32)
        for entry in range(6):
            near = inputs[source[:, entry]].astype(jnp.float32)
            turned = rotate_quarter(near, CH)
            gathered = gathered + (cosine[:, entry:entry + 1] * near + sine[:, entry:entry + 1] * turned) * edge_weight[:, entry:entry + 1]
        gathered = gathered.astype(jnp.bfloat16)
        convolved = per_level(gathered, near_form, CH) + per_level(inputs, self_form, CH)
        conv_out = (inputs.astype(jnp.float32) + convolved).astype(jnp.bfloat16)
        conv_out = lax.optimization_barrier(conv_out)
        terms = lax.map(mlp_block, (conv_out.reshape(-1, block_rows, CW), grads.reshape(-1, block_rows, CW)))
        grad_conv = (grads.astype(jnp.float32) + terms.reshape(COLUMNS, CW)).astype(jnp.bfloat16)
        grad_conv = lax.optimization_barrier(grad_conv)
        pulled = per_level(grad_conv, near_form.T, CH)
        own_back = per_level(grad_conv, self_form.T, CH)
        pulled_turn = rotate_quarter(pulled, CH)
        spread = jnp.zeros((COLUMNS, CW), jnp.float32)
        for entry in range(6):
            edges = (cosine[:, entry:entry + 1] * pulled - sine[:, entry:entry + 1] * pulled_turn) * edge_weight[:, entry:entry + 1]
            spread = spread.at[source[:, entry]].add(edges)
        return (grad_conv.astype(jnp.float32) + own_back + spread).astype(jnp.bfloat16)
    return lax.map(one_sample, (layer_input, cotangent))
```

```python
import jax
import jax.numpy as jnp
from jax import lax
from jax.experimental import pallas as pl
from jax.experimental.pallas import tpu as pltpu
from jax.sharding import PartitionSpec as P

CH = 64


def padded(shard, sides, width):
    for axis, dim in sides:
        devices, length = (lax.axis_size(axis), shard.shape[dim])
        up = [(i, (i + 1) % devices) for i in range(devices)]
        down = [(j, i) for i, j in up]
        last = lax.slice_in_dim(shard, length - width, length, axis=dim)
        leading = lax.slice_in_dim(shard, 0, width, axis=dim)
        before = lax.ppermute(last, axis, up)
        after = lax.ppermute(leading, axis, down)
        shard = jnp.concatenate([before, shard, after], axis=dim)
    return shard


def real_form(real_part, imag_part):
    upper = jnp.concatenate([real_part, imag_part], axis=1)
    lower = jnp.concatenate([-imag_part, real_part], axis=1)
    return jnp.concatenate([upper, lower], axis=0)


def rotate_quarter(values, channels):
    shape = values.shape
    split = values.reshape(shape[:-1] + (shape[-1] // channels, 2, channels // 2))
    turned = jnp.stack([-split[..., 1, :], split[..., 0, :]], axis=-2)
    return turned.reshape(shape)


def per_level(values, form, channels):
    shape = values.shape
    split = values.reshape(shape[:-1] + (shape[-1] // channels, channels))
    result = jnp.einsum("bclw,wv->bclv", split, form, preferred_element_type=jnp.float32)
    return result.reshape(shape)


def mlp_back(columns_in, grads, norm_gain, up_mat, down_mat):
    values = columns_in.astype(jnp.float32)
    root_scale = lax.rsqrt(jnp.mean(values * values, axis=-1, keepdims=True) + 1e-05)
    normed = (values * root_scale * norm_gain).astype(jnp.bfloat16)
    pre_act = jnp.einsum("brw,wh->brh", normed, up_mat, preferred_element_type=jnp.float32)
    back_hidden = jnp.einsum("brw,wh->brh", grads, down_mat, preferred_element_type=jnp.float32)
    sigmoid_pre = jax.nn.sigmoid(pre_act)
    grad_pre = (back_hidden * sigmoid_pre * (1.0 + pre_act * (1.0 - sigmoid_pre))).astype(
        jnp.bfloat16
    )
    grad_normed = jnp.einsum("brh,wh->brw", grad_pre, up_mat, preferred_element_type=jnp.float32)
    mixed_mean = jnp.mean(norm_gain * grad_normed * values, axis=-1, keepdims=True)
    return (
        root_scale * norm_gain * grad_normed
        - values * root_scale * root_scale * root_scale * mixed_mean
    )


def general(
    layer_input,
    cotangent,
    neighbours,
    boundary,
    gauge_index,
    gauge_angles,
    norm_gain,
    up_weight,
    down_weight,
    self_real,
    self_imag,
    near_real,
    near_imag,
):
    samples, columns, width = layer_input.shape
    border = boundary.shape[1] // 2
    low_rows = boundary[0, :border]
    high_rows = boundary[0, border:]
    sent = jnp.stack([layer_input[:, low_rows], layer_input[:, high_rows]])
    cycle = padded(sent, (("patch", 0),), 1)
    extended = jnp.concatenate(
        [layer_input, cycle[0], cycle[3], jnp.zeros((samples, 1, width), jnp.bfloat16)], axis=1
    )
    sentinel = columns + 2 * border
    present = (neighbours < sentinel).astype(jnp.float32)
    edge_weight = present / jnp.sum(present, axis=1, keepdims=True)
    phase = gauge_angles[gauge_index]
    cosine = jnp.cos(phase)
    sine = jnp.sin(phase)
    near_form = real_form(near_real, near_imag)
    self_form = real_form(self_real, self_imag)
    gathered = jnp.zeros((samples, columns, width), jnp.float32)
    for entry in range(6):
        near = extended[:, neighbours[:, entry]].astype(jnp.float32)
        turned = rotate_quarter(near, CH)
        gathered = (
            gathered
            + (
                cosine[None, :, entry : entry + 1] * near
                + sine[None, :, entry : entry + 1] * turned
            )
            * edge_weight[None, :, entry : entry + 1]
        )
    gathered = gathered.astype(jnp.bfloat16)
    convolved = per_level(gathered, near_form, CH) + per_level(layer_input, self_form, CH)
    conv_out = (layer_input.astype(jnp.float32) + convolved).astype(jnp.bfloat16)
    conv_out = lax.optimization_barrier(conv_out)
    up_part, down_part = (
        lax.all_gather(up_weight, "patch", axis=0, tiled=True),
        lax.all_gather(down_weight, "patch", axis=0, tiled=True),
    )
    up_whole, down_whole = (
        lax.all_gather(up_part, "level", axis=1, tiled=True),
        lax.all_gather(down_part, "level", axis=1, tiled=True),
    )
    half_cols, half_grads = (
        lax.all_to_all(conv_out, "level", split_axis=1, concat_axis=2, tiled=True),
        lax.all_to_all(cotangent, "level", split_axis=1, concat_axis=2, tiled=True),
    )
    terms = mlp_back(half_cols, half_grads, norm_gain, up_whole, down_whole)
    column_grad = (half_grads.astype(jnp.float32) + terms).astype(jnp.bfloat16)
    grad_conv = lax.all_to_all(column_grad, "level", split_axis=2, concat_axis=1, tiled=True)
    grad_conv = lax.optimization_barrier(grad_conv)
    pulled = per_level(grad_conv, near_form.T, CH)
    own_back = per_level(grad_conv, self_form.T, CH)
    pulled_turn = rotate_quarter(pulled, CH)
    spread = jnp.zeros((samples, sentinel + 1, width), jnp.float32)
    for entry in range(6):
        edges = (
            cosine[None, :, entry : entry + 1] * pulled
            - sine[None, :, entry : entry + 1] * pulled_turn
        ) * edge_weight[None, :, entry : entry + 1]
        spread = spread.at[:, neighbours[:, entry]].add(edges)
    back_sent = jnp.stack(
        [spread[:, columns : columns + border], spread[:, columns + border : sentinel]]
    )
    back_cycle = padded(back_sent.astype(jnp.bfloat16), (("patch", 0),), 1).astype(back_sent.dtype)
    local_terms = (
        spread[:, :columns].at[:, low_rows].add(back_cycle[0]).at[:, high_rows].add(back_cycle[3])
    )
    return (grad_conv.astype(jnp.float32) + own_back + local_terms).astype(jnp.bfloat16)


BLOCK = 256
TEAM = 4


def iota(shape, dim):
    return lax.broadcasted_iota(jnp.int32, shape, dim)


def mm(a, b, dims=((1,), (0,))):
    return lax.dot_general(a, b, (dims, ((), ())), preferred_element_type=jnp.float32)


def turn(values):
    width = values.shape[1]
    half = CH // 2
    later = pltpu.roll(values, width - half, 1)
    earlier = pltpu.roll(values, half, 1)
    return jnp.where(iota(values.shape, 1) % CH < half, -later, earlier)


def call(body, outs, args, scratch=(), specs=None):
    vmem = pl.BlockSpec(memory_space=pltpu.VMEM)
    return pl.pallas_call(
        body,
        out_shape=outs,
        in_specs=specs or [vmem] * len(args),
        out_specs=jax.tree.map(lambda _: vmem, outs),
        scratch_shapes=scratch,
        compiler_params=pltpu.CompilerParams(vmem_limit_bytes=56 << 20),
    )(*args)


def struct(shape, dtype=jnp.bfloat16):
    return jax.ShapeDtypeStruct(shape, dtype)


def picked(bound_ref, columns):
    count = bound_ref.shape[1]
    return (iota((columns, count), 0) == bound_ref[...]).astype(jnp.bfloat16)


def pack_body(x_ref, bound_ref, up_ref, down_ref, low_ref, high_ref, *parts):
    border = low_ref.shape[0]
    rows = mm(picked(bound_ref, x_ref.shape[0]), x_ref[...], ((0,), (0,))).astype(jnp.bfloat16)
    low_ref[...] = rows[:border]
    high_ref[...] = rows[border:]
    mine = lax.axis_index("patch") % TEAM
    span = parts[0].shape[2]
    for k in range(TEAM):
        at = pl.multiple_of((mine ^ k) * span, span)
        parts[k][0] = up_ref[:, pl.ds(at, span)]
        parts[k][1] = down_ref[:, pl.ds(at, span)]


def spread_form(real_ref, imag_ref):
    half = real_ref.shape[0]
    tall = (iota((BLOCK, half), 0) % half == iota((BLOCK, half), 1)).astype(jnp.bfloat16)

    def tiled(ref):
        rows = mm(tall, ref[...]).astype(jnp.bfloat16)
        return mm(rows, tall, ((1,), (1,)))

    real, imag = tiled(real_ref), tiled(imag_ref)
    row, col = iota((BLOCK, BLOCK), 0), iota((BLOCK, BLOCK), 1)
    row_real = row % CH < half
    col_real = col % CH < half
    form = jnp.where(row_real == col_real, real, jnp.where(row_real, imag, -imag))
    return jnp.where(row // CH == col // CH, form, 0.0).astype(jnp.bfloat16)


def prep_body(sentinel, near_ref, index_ref, angle_ref, nr, ni, sr, si, mix_ref, form_ref):
    columns, entries = near_ref.shape
    count = angle_ref.shape[1]
    place = iota((columns, count), 1)
    angles = angle_ref[...]
    phases = [
        jnp.sum(
            jnp.where(index_ref[:, k : k + 1] == place, angles, 0.0), axis=1, keepdims=True
        )
        for k in range(entries)
    ]
    lane = iota((columns, 128), 1)
    phase = jnp.zeros((columns, 128), jnp.float32)
    for k in range(entries):
        phase = jnp.where(lane == k, phases[k], phase)
    cosine, sine = jnp.cos(phase), jnp.sin(phase)
    present = [(near_ref[:, k : k + 1] < sentinel).astype(jnp.float32) for k in range(entries)]
    total = sum(present)
    width = mix_ref.shape[2]
    place = iota((columns, width), 1)
    mix_cos = jnp.zeros((columns, width), jnp.float32)
    mix_sin = jnp.zeros((columns, width), jnp.float32)
    for k in range(entries):
        weight = present[k] / total
        hit = near_ref[:, k : k + 1] == place
        mix_cos = mix_cos + jnp.where(hit, cosine[:, k : k + 1] * weight, 0.0)
        mix_sin = mix_sin + jnp.where(hit, sine[:, k : k + 1] * weight, 0.0)
    mix_ref[0] = mix_cos.astype(jnp.bfloat16)
    mix_ref[1] = mix_sin.astype(jnp.bfloat16)
    form_ref[0] = spread_form(nr, ni)
    form_ref[1] = spread_form(sr, si)


def conv_body(x_ref, before_ref, after_ref, mix_ref, form_ref, gain_ref, conv_ref, norm_ref, ext):
    columns, width = x_ref.shape
    border = before_ref.shape[0]
    ext[:columns] = x_ref[...]
    ext[columns : columns + border] = before_ref[...]
    ext[columns + border : columns + 2 * border] = after_ref[...]
    rest = ext.shape[0] - columns - 2 * border
    if rest:
        ext[columns + 2 * border :] = jnp.zeros((rest, width), jnp.bfloat16)
    source = ext[...]
    gathered = (mm(mix_ref[0], source) + turn(mm(mix_ref[1], source))).astype(jnp.bfloat16)
    square = jnp.zeros((columns, BLOCK), jnp.float32)
    for b in range(width // BLOCK):
        at = slice(b * BLOCK, (b + 1) * BLOCK)
        x = x_ref[:, at]
        out = x.astype(jnp.float32) + (mm(gathered[:, at], form_ref[0]) + mm(x, form_ref[1]))
        out = out.astype(jnp.bfloat16)
        conv_ref[:, at] = out
        out = out.astype(jnp.float32)
        square = square + out * out
    scale = lax.rsqrt(jnp.sum(square, axis=1, keepdims=True) / width + 1e-05)
    norm_ref[...] = (conv_ref[...].astype(jnp.float32) * scale * gain_ref[...]).astype(jnp.bfloat16)


def ring_place(group, groups):
    return jnp.where(group % 2 == 0, group // 2, groups - 1 - group // 2)


def ring_group(place, groups):
    return jnp.where(place < groups // 2, 2 * place, 2 * (groups - 1 - place) + 1)


def column_body(steps, groups, *refs):
    norms, grads, chunks = refs[:TEAM], refs[TEAM : 2 * TEAM], refs[2 * TEAM : 2 * TEAM + len(steps)]
    mine_ref, cross_ref, send_ref, xs, gs, ups, downs, sem = refs[2 * TEAM + len(steps) :]
    columns = norms[0].shape[0]
    me = lax.axis_index("patch")
    group, member = me // TEAM, me % TEAM
    place = ring_place(group, groups)
    copies = []

    def copy(src, dst):
        copies.append(pltpu.make_async_copy(src, dst, sem.at[len(copies)]))
        copies[-1].start()

    for k in range(TEAM):
        copy(norms[k], xs.at[pl.ds(k * columns, columns)])
        copy(grads[k], gs.at[pl.ds(k * columns, columns)])
    for (shift, first), ref in zip(steps, chunks):
        rows = ref.shape[1] // 2
        owner = ring_group((place + shift + groups) % groups, groups)
        for half in range(2):
            at = pl.multiple_of((owner * TEAM + (member ^ (first + half))) * rows, 16)
            span = pl.ds(half * rows, rows)
            copy(ref.at[0, span], ups.at[pl.ds(at, rows)])
            copy(ref.at[1, span], downs.at[pl.ds(at, rows)])
    for one in copies:
        one.wait()
    pre_act = mm(xs[...], ups[...])
    back = mm(gs[...], downs[...])
    gate = jax.nn.sigmoid(pre_act)
    grad_pre = (back * gate * (1.0 + pre_act * (1.0 - gate))).astype(jnp.bfloat16)
    up = ups[...]
    for k, (ref, slot) in enumerate(((mine_ref, None), (send_ref, 0), (cross_ref, None), (send_ref, 1))):
        rows = mm(grad_pre[k * columns : (k + 1) * columns], up, ((1,), (1,)))
        if slot is None:
            ref[...] = rows
        else:
            ref[slot] = rows.astype(jnp.bfloat16)


def shifted_back(mix, form, grads):
    spread = mm(mix[0], grads, ((0,), (0,))) - turn(mm(mix[1], grads, ((0,), (0,))))
    spread = spread.astype(jnp.bfloat16)
    width = grads.shape[1]
    return [
        mm(spread[:, b * BLOCK : (b + 1) * BLOCK], form, ((1,), (1,)))
        for b in range(width // BLOCK)
    ]


def grad_body(mine_ref, part_ref, cross_ref, conv_ref, cot_ref, gain_ref, mix_ref, form_ref, grad_ref, prev_ref, next_ref):
    columns, width = conv_ref.shape
    border = prev_ref.shape[0]
    grad_normed = mine_ref[...] + part_ref[0].astype(jnp.float32) + cross_ref[...].astype(jnp.float32)
    values = conv_ref[...].astype(jnp.float32)
    scaled = gain_ref[...] * grad_normed
    scale = lax.rsqrt(jnp.sum(values * values, axis=1, keepdims=True) / width + 1e-05)
    mixed = jnp.sum(scaled * values, axis=1, keepdims=True) / width
    grads = cot_ref[...].astype(jnp.float32) + (
        scale * scaled - values * (scale * scale * scale * mixed)
    )
    grads = grads.astype(jnp.bfloat16)
    grad_ref[...] = grads
    outer = [mix_ref[i, :, columns:] for i in range(2)]
    for b, rows in enumerate(shifted_back(outer, form_ref[0], grads)):
        at = slice(b * BLOCK, (b + 1) * BLOCK)
        rows = rows.astype(jnp.bfloat16)
        prev_ref[:, at] = rows[:border]
        next_ref[:, at] = rows[border : 2 * border]


def own_body(grad_ref, mix_ref, form_ref, local_ref):
    columns, width = grad_ref.shape
    grads = grad_ref[...]
    inner = [mix_ref[i, :, :columns] for i in range(2)]
    for b, rows in enumerate(shifted_back(inner, form_ref[0], grads)):
        at = slice(b * BLOCK, (b + 1) * BLOCK)
        own = grads[:, at]
        local_ref[:, at] = own.astype(jnp.float32) + (mm(own, form_ref[1], ((1,), (1,))) + rows)


def last_body(local_ref, low_ref, high_ref, bound_ref, out_ref):
    border = low_ref.shape[0]
    chosen = picked(bound_ref, local_ref.shape[0]).astype(jnp.float32)
    low = chosen[:, :border].astype(jnp.bfloat16)
    high = chosen[:, border:].astype(jnp.bfloat16)
    out_ref[...] = (local_ref[...] + mm(low, low_ref[...]) + mm(high, high_ref[...])).astype(jnp.bfloat16)


def per_device(
    layer_input,
    cotangent,
    neighbours,
    boundary,
    gauge_index,
    gauge_angles,
    norm_gain,
    up_weight,
    down_weight,
    self_real,
    self_imag,
    near_real,
    near_imag,
):
    samples, columns, width = layer_input.shape
    devices = lax.axis_size("patch")
    rows, hidden = up_weight.shape
    border = boundary.shape[1] // 2
    span = hidden // TEAM
    fits = (
        lax.axis_size("level") == 1
        and samples == 1
        and devices % (2 * TEAM) == 0
        and width % BLOCK == 0
        and hidden % (TEAM * 128) == 0
        and rows % 16 == 0
        and columns % 128 == 0
        and border % 16 == 0
        and 2 * border <= columns
        and width * span <= 1 << 20
    )
    if not fits:
        return general(
            layer_input,
            cotangent,
            neighbours,
            boundary,
            gauge_index,
            gauge_angles,
            norm_gain,
            up_weight,
            down_weight,
            self_real,
            self_imag,
            near_real,
            near_imag,
        )
    groups = devices // TEAM
    sentinel = columns + 2 * border
    extent = -(-sentinel // 128) * 128
    x = layer_input[0]
    cot = cotangent[0]
    angles = gauge_angles.reshape(1, -1)
    gain = norm_gain.reshape(1, -1)

    def swap(value, bits):
        return lax.ppermute(value, "patch", [(i, i ^ bits) for i in range(devices)])

    def step(value, shift):
        return lax.ppermute(value, "patch", [(i, (i + shift) % devices) for i in range(devices)])

    order = list(range(0, groups, 2)) + list(range(groups - 1, 0, -2))

    def around(value, shift):
        pairs = [
            (order[k] * TEAM + j, order[(k + shift) % groups] * TEAM + j)
            for k in range(groups)
            for j in range(TEAM)
        ]
        return lax.ppermute(value, "patch", pairs)

    low, high, *parts = call(
        pack_body,
        [struct((border, width))] * 2 + [struct((2, rows, span))] * TEAM,
        [x, boundary, up_weight, down_weight],
    )
    near_part = swap(parts[1], 1)
    far_parts = [swap(parts[2], 2), swap(parts[3], 3)]
    first = jnp.concatenate([parts[0], near_part], axis=1)
    second = jnp.concatenate(far_parts, axis=1)
    before = step(high, 1)
    after = step(low, -1)
    steps, chunks = [(0, 0), (0, 2)], [first, second]
    forth = [first, second]
    back = [first, second]
    half = groups // 2
    for s in range(1, half + 1):
        for which in range(2):
            if s < half or which == 0:
                forth[which] = around(forth[which], 1)
                steps.append((-s, 2 * which))
                chunks.append(forth[which])
            if s < half or which == 1:
                back[which] = around(back[which], -1)
                steps.append((s, 2 * which))
                chunks.append(back[which])

    cot_near = swap(cot, 1)
    cot_far = swap(cot, 2)
    cot_cross = swap(cot_far, 1)

    mix, form = call(
        lambda *refs: prep_body(sentinel, *refs),
        [struct((2, columns, extent)), struct((2, BLOCK, BLOCK))],
        [neighbours, gauge_index, angles, near_real, near_imag, self_real, self_imag],
    )
    conv, norm = call(
        conv_body,
        [struct((columns, width))] * 2,
        [x, before, after, mix, form, gain],
        [pltpu.VMEM((extent, width), jnp.bfloat16)],
    )
    norm_near = swap(norm, 1)
    norm_far = swap(norm, 2)
    norm_cross = swap(norm_far, 1)

    operands = [norm, norm_near, norm_far, norm_cross, cot, cot_near, cot_far, cot_cross, *chunks]
    wide = struct((columns, width), jnp.float32)
    mine, cross, send = call(
        lambda *refs: column_body(steps, groups, *refs),
        [wide, wide, struct((2, columns, width))],
        operands,
        [
            pltpu.VMEM((TEAM * columns, width), jnp.bfloat16),
            pltpu.VMEM((TEAM * columns, width), jnp.bfloat16),
            pltpu.VMEM((width, span), jnp.bfloat16),
            pltpu.VMEM((width, span), jnp.bfloat16),
            pltpu.SemaphoreType.DMA((2 * TEAM + 4 * len(steps),)),
        ],
        [pl.BlockSpec(memory_space=pl.ANY)] * len(operands),
    )
    received = swap(send, 1)
    crossing = (cross + received[1].astype(jnp.float32)).astype(jnp.bfloat16)
    crossed = swap(crossing, 2)
    grads, to_prev, to_next = call(
        grad_body,
        [struct((columns, width)), struct((border, width)), struct((border, width))],
        [mine, received, crossed, conv, cot, gain, mix, form],
    )
    from_prev = step(to_next, 1)
    from_next = step(to_prev, -1)
    local = call(own_body, wide, [grads, mix, form])
    out = call(last_body, struct((columns, width)), [local, from_prev, from_next, boundary])
    return out[None]


def solution(mesh):
    in_specs = (
        P("groups", "patch", "level"),
        P("groups", "patch", "level"),
        P("patch", None),
        P("patch", None),
        P("patch", None),
        P(),
        P(),
        P("patch", "level"),
        P("patch", "level"),
        P(),
        P(),
        P(),
        P(),
    )
    out_specs = P("groups", "patch", "level")
    return jax.shard_map(
        per_device, mesh=mesh, in_specs=in_specs, out_specs=out_specs, check_vma=False
    )
```

```python
import jax
import jax.numpy as jnp
from jax import lax
from jax.experimental import pallas as pl
from jax.experimental.pallas import tpu as pltpu
from jax.sharding import PartitionSpec as P


CH = 64


def padded(shard, sides, width):
    for axis, dim in sides:
        devices, length = (lax.axis_size(axis), shard.shape[dim])
        up = [(i, (i + 1) % devices) for i in range(devices)]
        down = [(j, i) for i, j in up]
        last = lax.slice_in_dim(shard, length - width, length, axis=dim)
        leading = lax.slice_in_dim(shard, 0, width, axis=dim)
        before = lax.ppermute(last, axis, up)
        after = lax.ppermute(leading, axis, down)
        shard = jnp.concatenate([before, shard, after], axis=dim)
    return shard


def real_form(real_part, imag_part):
    upper = jnp.concatenate([real_part, imag_part], axis=1)
    lower = jnp.concatenate([-imag_part, real_part], axis=1)
    return jnp.concatenate([upper, lower], axis=0)


def rotate_quarter(values, channels):
    shape = values.shape
    split = values.reshape(shape[:-1] + (shape[-1] // channels, 2, channels // 2))
    turned = jnp.stack([-split[..., 1, :], split[..., 0, :]], axis=-2)
    return turned.reshape(shape)


def per_level(values, form, channels):
    shape = values.shape
    split = values.reshape(shape[:-1] + (shape[-1] // channels, channels))
    result = jnp.einsum("bclw,wv->bclv", split, form, preferred_element_type=jnp.float32)
    return result.reshape(shape)


def mlp_back(columns_in, grads, norm_gain, up_mat, down_mat):
    values = columns_in.astype(jnp.float32)
    root_scale = lax.rsqrt(jnp.mean(values * values, axis=-1, keepdims=True) + 1e-05)
    normed = (values * root_scale * norm_gain).astype(jnp.bfloat16)
    pre_act = jnp.einsum("brw,wh->brh", normed, up_mat, preferred_element_type=jnp.float32)
    back_hidden = jnp.einsum("brw,wh->brh", grads, down_mat, preferred_element_type=jnp.float32)
    sigmoid_pre = jax.nn.sigmoid(pre_act)
    grad_pre = (back_hidden * sigmoid_pre * (1.0 + pre_act * (1.0 - sigmoid_pre))).astype(
        jnp.bfloat16
    )
    grad_normed = jnp.einsum("brh,wh->brw", grad_pre, up_mat, preferred_element_type=jnp.float32)
    mixed_mean = jnp.mean(norm_gain * grad_normed * values, axis=-1, keepdims=True)
    return (
        root_scale * norm_gain * grad_normed
        - values * root_scale * root_scale * root_scale * mixed_mean
    )


def general(
    layer_input,
    cotangent,
    neighbours,
    boundary,
    gauge_index,
    gauge_angles,
    norm_gain,
    up_weight,
    down_weight,
    self_real,
    self_imag,
    near_real,
    near_imag,
):
    samples, columns, width = layer_input.shape
    border = boundary.shape[1] // 2
    low_rows = boundary[0, :border]
    high_rows = boundary[0, border:]
    sent = jnp.stack([layer_input[:, low_rows], layer_input[:, high_rows]])
    cycle = padded(sent, (("patch", 0),), 1)
    extended = jnp.concatenate(
        [layer_input, cycle[0], cycle[3], jnp.zeros((samples, 1, width), jnp.bfloat16)], axis=1
    )
    sentinel = columns + 2 * border
    present = (neighbours < sentinel).astype(jnp.float32)
    edge_weight = present / jnp.sum(present, axis=1, keepdims=True)
    phase = gauge_angles[gauge_index]
    cosine = jnp.cos(phase)
    sine = jnp.sin(phase)
    near_form = real_form(near_real, near_imag)
    self_form = real_form(self_real, self_imag)
    gathered = jnp.zeros((samples, columns, width), jnp.float32)
    for entry in range(6):
        near = extended[:, neighbours[:, entry]].astype(jnp.float32)
        turned = rotate_quarter(near, CH)
        gathered = (
            gathered
            + (
                cosine[None, :, entry : entry + 1] * near
                + sine[None, :, entry : entry + 1] * turned
            )
            * edge_weight[None, :, entry : entry + 1]
        )
    gathered = gathered.astype(jnp.bfloat16)
    convolved = per_level(gathered, near_form, CH) + per_level(layer_input, self_form, CH)
    conv_out = (layer_input.astype(jnp.float32) + convolved).astype(jnp.bfloat16)
    conv_out = lax.optimization_barrier(conv_out)
    up_part, down_part = (
        lax.all_gather(up_weight, "patch", axis=0, tiled=True),
        lax.all_gather(down_weight, "patch", axis=0, tiled=True),
    )
    up_whole, down_whole = (
        lax.all_gather(up_part, "level", axis=1, tiled=True),
        lax.all_gather(down_part, "level", axis=1, tiled=True),
    )
    half_cols, half_grads = (
        lax.all_to_all(conv_out, "level", split_axis=1, concat_axis=2, tiled=True),
        lax.all_to_all(cotangent, "level", split_axis=1, concat_axis=2, tiled=True),
    )
    terms = mlp_back(half_cols, half_grads, norm_gain, up_whole, down_whole)
    column_grad = (half_grads.astype(jnp.float32) + terms).astype(jnp.bfloat16)
    grad_conv = lax.all_to_all(column_grad, "level", split_axis=2, concat_axis=1, tiled=True)
    grad_conv = lax.optimization_barrier(grad_conv)
    pulled = per_level(grad_conv, near_form.T, CH)
    own_back = per_level(grad_conv, self_form.T, CH)
    pulled_turn = rotate_quarter(pulled, CH)
    spread = jnp.zeros((samples, sentinel + 1, width), jnp.float32)
    for entry in range(6):
        edges = (
            cosine[None, :, entry : entry + 1] * pulled
            - sine[None, :, entry : entry + 1] * pulled_turn
        ) * edge_weight[None, :, entry : entry + 1]
        spread = spread.at[:, neighbours[:, entry]].add(edges)
    back_sent = jnp.stack(
        [spread[:, columns : columns + border], spread[:, columns + border : sentinel]]
    )
    back_cycle = padded(back_sent.astype(jnp.bfloat16), (("patch", 0),), 1).astype(back_sent.dtype)
    local_terms = (
        spread[:, :columns].at[:, low_rows].add(back_cycle[0]).at[:, high_rows].add(back_cycle[3])
    )
    return (grad_conv.astype(jnp.float32) + own_back + local_terms).astype(jnp.bfloat16)


BLOCK = 256
TEAM = 4


def iota(shape, dim):
    return lax.broadcasted_iota(jnp.int32, shape, dim)


def mm(a, b, dims=((1,), (0,))):
    return lax.dot_general(a, b, (dims, ((), ())), preferred_element_type=jnp.float32)


def turn(values):
    width = values.shape[1]
    half = CH // 2
    later = pltpu.roll(values, width - half, 1)
    earlier = pltpu.roll(values, half, 1)
    return jnp.where(iota(values.shape, 1) % CH < half, -later, earlier)


def call(body, outs, args, scratch=(), raw=()):
    vmem = pl.BlockSpec(memory_space=pltpu.VMEM)
    args = [
        value if i in raw else pltpu.with_memory_space_constraint(value, pltpu.VMEM)
        for i, value in enumerate(args)
    ]
    specs = [pl.BlockSpec(memory_space=pl.ANY) if i in raw else vmem for i in range(len(args))]
    return pl.pallas_call(
        body,
        out_shape=outs,
        in_specs=specs,
        out_specs=jax.tree.map(lambda _: vmem, outs),
        scratch_shapes=scratch,
        compiler_params=pltpu.CompilerParams(vmem_limit_bytes=24 << 20),
    )(*args)


def struct(shape, dtype=jnp.bfloat16):
    return pltpu.VMEM(shape, dtype)


def picked(bound_ref, columns):
    count = bound_ref.shape[1]
    return (iota((columns, count), 0) == bound_ref[...]).astype(jnp.bfloat16)


def weights_body(up_ref, down_ref, *refs):
    *parts, sem = refs
    mine = lax.axis_index("patch") % TEAM
    span = parts[0].shape[2]
    copies = []
    for k in range(TEAM):
        at = pl.multiple_of((mine ^ k) * span, 128)
        for which, ref in enumerate((up_ref, down_ref)):
            copies.append(
                pltpu.make_async_copy(
                    ref.at[:, pl.ds(at, span)], parts[k].at[which], sem.at[2 * k + which]
                )
            )
            copies[-1].start()
    for one in copies:
        one.wait()


def border_body(x_ref, bound_ref, low_ref, high_ref):
    border = low_ref.shape[0]
    rows = mm(picked(bound_ref, x_ref.shape[0]), x_ref[...], ((0,), (0,))).astype(jnp.bfloat16)
    low_ref[...] = rows[:border]
    high_ref[...] = rows[border:]


def spread_form(real_ref, imag_ref):
    half = real_ref.shape[0]
    tall = (iota((BLOCK, half), 0) % half == iota((BLOCK, half), 1)).astype(jnp.bfloat16)

    def tiled(ref):
        rows = mm(tall, ref[...]).astype(jnp.bfloat16)
        return mm(rows, tall, ((1,), (1,)))

    real, imag = tiled(real_ref), tiled(imag_ref)
    row, col = iota((BLOCK, BLOCK), 0), iota((BLOCK, BLOCK), 1)
    row_real = row % CH < half
    col_real = col % CH < half
    form = jnp.where(row_real == col_real, real, jnp.where(row_real, imag, -imag))
    return jnp.where(row // CH == col // CH, form, 0.0).astype(jnp.bfloat16)


def prep_body(sentinel, near_ref, index_ref, angle_ref, nr, ni, sr, si, mix_ref, form_ref):
    entries, columns = near_ref.shape
    table = angle_ref[...]
    index = index_ref[...]
    phases = []
    for k in range(entries):
        spot = jnp.broadcast_to(index[k : k + 1], (table.shape[0], columns))
        found = jnp.take_along_axis(table, spot % 128, axis=1)
        hit = iota(found.shape, 0) == spot // 128
        phases.append(jnp.sum(jnp.where(hit, found, 0.0), axis=0, keepdims=True))
    phase = jnp.concatenate(phases, axis=0)
    near = near_ref[...]
    present = (near < sentinel).astype(jnp.float32)
    weight = present / jnp.sum(present, axis=0, keepdims=True)
    cosine, sine = jnp.cos(phase) * weight, jnp.sin(phase) * weight
    height = mix_ref.shape[1]
    place = iota((height, columns), 0)
    mix_cos = jnp.zeros((height, columns), jnp.float32)
    mix_sin = jnp.zeros((height, columns), jnp.float32)
    for k in range(entries):
        hit = near[k : k + 1] == place
        mix_cos = mix_cos + jnp.where(hit, cosine[k : k + 1], 0.0)
        mix_sin = mix_sin + jnp.where(hit, sine[k : k + 1], 0.0)
    mix_ref[0] = mix_cos.astype(jnp.bfloat16)
    mix_ref[1] = mix_sin.astype(jnp.bfloat16)
    form_ref[0] = spread_form(nr, ni)
    form_ref[1] = spread_form(sr, si)


def conv_body(x_ref, before_ref, after_ref, mix_ref, form_ref, gain_ref, conv_ref, norm_ref, ext):
    columns, width = x_ref.shape
    border = before_ref.shape[0]
    ext[:columns] = x_ref[...]
    ext[columns : columns + border] = before_ref[...]
    ext[columns + border : columns + 2 * border] = after_ref[...]
    rest = ext.shape[0] - columns - 2 * border
    if rest:
        ext[columns + 2 * border :] = jnp.zeros((rest, width), jnp.bfloat16)
    source = ext[...]
    over = ((0,), (0,))
    gathered = mm(mix_ref[0], source, over) + turn(mm(mix_ref[1], source, over))
    gathered = gathered.astype(jnp.bfloat16)
    square = jnp.zeros((columns, BLOCK), jnp.float32)
    for b in range(width // BLOCK):
        at = slice(b * BLOCK, (b + 1) * BLOCK)
        x = x_ref[:, at]
        out = x.astype(jnp.float32) + (mm(gathered[:, at], form_ref[0]) + mm(x, form_ref[1]))
        out = out.astype(jnp.bfloat16)
        conv_ref[:, at] = out
        out = out.astype(jnp.float32)
        square = square + out * out
    scale = lax.rsqrt(jnp.sum(square, axis=1, keepdims=True) / width + 1e-05)
    norm_ref[...] = (conv_ref[...].astype(jnp.float32) * scale * gain_ref[...]).astype(jnp.bfloat16)


def ring_place(group, groups):
    return jnp.where(group % 2 == 0, group // 2, groups - 1 - group // 2)


def ring_group(place, groups):
    return jnp.where(place < groups // 2, 2 * place, 2 * (groups - 1 - place) + 1)


def column_body(steps, groups, *refs):
    norms, grads, chunks = refs[:TEAM], refs[TEAM : 2 * TEAM], refs[2 * TEAM : 2 * TEAM + len(steps)]
    mine_ref, cross_ref, send_ref, xs, gs, ups, downs = refs[2 * TEAM + len(steps) :]
    columns = norms[0].shape[0]
    me = lax.axis_index("patch")
    group, member = me // TEAM, me % TEAM
    place = ring_place(group, groups)
    for k in range(TEAM):
        xs[k * columns : (k + 1) * columns] = norms[k][...]
        gs[k * columns : (k + 1) * columns] = grads[k][...]
    for (shift, first), ref in zip(steps, chunks):
        rows = ref.shape[1] // 2
        owner = ring_group((place + shift + groups) % groups, groups)
        for half in range(2):
            at = pl.multiple_of((owner * TEAM + (member ^ (first + half))) * rows, 16)
            span = slice(half * rows, (half + 1) * rows)
            ups[pl.ds(at, rows)] = ref[0, span]
            downs[pl.ds(at, rows)] = ref[1, span]
    pre_act = mm(xs[...], ups[...])
    back = mm(gs[...], downs[...])
    gate = jax.nn.sigmoid(pre_act)
    grad_pre = (back * gate * (1.0 + pre_act * (1.0 - gate))).astype(jnp.bfloat16)
    up = ups[...]
    for k, (ref, slot) in enumerate(((mine_ref, None), (send_ref, 0), (cross_ref, None), (send_ref, 1))):
        rows = mm(grad_pre[k * columns : (k + 1) * columns], up, ((1,), (1,)))
        if slot is None:
            ref[...] = rows
        else:
            ref[slot] = rows.astype(jnp.bfloat16)


def shifted_back(mix, form, grads):
    spread = mm(mix[0], grads) - turn(mm(mix[1], grads))
    spread = spread.astype(jnp.bfloat16)
    width = grads.shape[1]
    return [
        mm(spread[:, b * BLOCK : (b + 1) * BLOCK], form, ((1,), (1,)))
        for b in range(width // BLOCK)
    ]


def join_body(cross_ref, part_ref, out_ref):
    out_ref[...] = (cross_ref[...] + part_ref[1].astype(jnp.float32)).astype(jnp.bfloat16)


def grad_body(mine_ref, part_ref, cross_ref, conv_ref, cot_ref, gain_ref, mix_ref, form_ref, grad_ref, prev_ref, next_ref):
    columns, width = conv_ref.shape
    border = prev_ref.shape[0]
    grad_normed = mine_ref[...] + part_ref[0].astype(jnp.float32) + cross_ref[...].astype(jnp.float32)
    values = conv_ref[...].astype(jnp.float32)
    scaled = gain_ref[...] * grad_normed
    scale = lax.rsqrt(jnp.sum(values * values, axis=1, keepdims=True) / width + 1e-05)
    mixed = jnp.sum(scaled * values, axis=1, keepdims=True) / width
    grads = cot_ref[...].astype(jnp.float32) + (
        scale * scaled - values * (scale * scale * scale * mixed)
    )
    grads = grads.astype(jnp.bfloat16)
    grad_ref[...] = grads
    outer = [mix_ref[i, columns:] for i in range(2)]
    for b, rows in enumerate(shifted_back(outer, form_ref[0], grads)):
        at = slice(b * BLOCK, (b + 1) * BLOCK)
        rows = rows.astype(jnp.bfloat16)
        prev_ref[:, at] = rows[:border]
        next_ref[:, at] = rows[border : 2 * border]


def own_body(grad_ref, mix_ref, form_ref, local_ref):
    columns, _ = grad_ref.shape
    grads = grad_ref[...]
    inner = [mix_ref[i, :columns] for i in range(2)]
    for b, rows in enumerate(shifted_back(inner, form_ref[0], grads)):
        at = slice(b * BLOCK, (b + 1) * BLOCK)
        own = grads[:, at]
        local_ref[:, at] = own.astype(jnp.float32) + (mm(own, form_ref[1], ((1,), (1,))) + rows)


def last_body(local_ref, low_ref, high_ref, bound_ref, out_ref):
    border = low_ref.shape[0]
    chosen = picked(bound_ref, local_ref.shape[0]).astype(jnp.float32)
    low = chosen[:, :border].astype(jnp.bfloat16)
    high = chosen[:, border:].astype(jnp.bfloat16)
    out_ref[...] = (local_ref[...] + mm(low, low_ref[...]) + mm(high, high_ref[...])).astype(jnp.bfloat16)


def per_device(
    layer_input,
    cotangent,
    neighbours,
    boundary,
    gauge_index,
    gauge_angles,
    norm_gain,
    up_weight,
    down_weight,
    self_real,
    self_imag,
    near_real,
    near_imag,
):
    samples, columns, width = layer_input.shape
    devices = lax.axis_size("patch")
    rows, hidden = up_weight.shape
    border = boundary.shape[1] // 2
    span = hidden // TEAM
    fits = (
        lax.axis_size("level") == 1
        and samples == 1
        and devices % (2 * TEAM) == 0
        and width % BLOCK == 0
        and hidden % (TEAM * 128) == 0
        and rows % 16 == 0
        and border % 16 == 0
        and 2 * border <= columns
        and width * span <= 1 << 20
        and gauge_angles.shape[0] % 128 == 0
        and columns == 128
    )
    if not fits:
        return general(
            layer_input,
            cotangent,
            neighbours,
            boundary,
            gauge_index,
            gauge_angles,
            norm_gain,
            up_weight,
            down_weight,
            self_real,
            self_imag,
            near_real,
            near_imag,
        )
    groups = devices // TEAM
    sentinel = columns + 2 * border
    extent = -(-sentinel // 128) * 128
    x = layer_input[0]
    cot = cotangent[0]
    angles = gauge_angles.reshape(-1, 128)
    gain = norm_gain.reshape(1, -1)

    def permute(value, pairs):
        return lax.ppermute(value, "patch", pairs)

    def swap(value, bits):
        return permute(value, [(i, i ^ bits) for i in range(devices)])

    def step(value, shift):
        return permute(value, [(i, (i + shift) % devices) for i in range(devices)])

    order = list(range(0, groups, 2)) + list(range(groups - 1, 0, -2))

    def around(value, shift):
        pairs = [
            (order[k] * TEAM + j, order[(k + shift) % groups] * TEAM + j)
            for k in range(groups)
            for j in range(TEAM)
        ]
        return permute(value, pairs)

    parts = call(
        weights_body,
        [struct((2, rows, span))] * TEAM,
        [up_weight, down_weight],
        [pltpu.SemaphoreType.DMA((2 * TEAM,))],
        (0, 1),
    )
    near_part = swap(parts[1], 1)
    far_parts = [swap(parts[2], 2), swap(parts[3], 3)]
    first = jnp.concatenate([parts[0], near_part], axis=1)
    second = jnp.concatenate(far_parts, axis=1)
    steps, chunks = [(0, 0), (0, 2)], [first, second]
    forth = [first, second]
    back = [first, second]
    half = groups // 2
    for s in range(1, half + 1):
        for which in range(2):
            if s < half or which == 0:
                forth[which] = around(forth[which], 1)
                steps.append((-s, 2 * which))
                chunks.append(forth[which])
            if s < half or which == 1:
                back[which] = around(back[which], -1)
                steps.append((s, 2 * which))
                chunks.append(back[which])

    low, high = call(border_body, [struct((border, width))] * 2, [x, boundary])
    before = step(high, 1)
    after = step(low, -1)
    cot_near = swap(cot, 1)
    cot_far = swap(cot, 2)
    cot_cross = swap(cot_far, 1)

    mix, form = call(
        lambda *refs: prep_body(sentinel, *refs),
        [struct((2, extent, columns)), struct((2, BLOCK, BLOCK))],
        [neighbours.T, gauge_index.T, angles, near_real, near_imag, self_real, self_imag],
    )
    conv, norm = call(
        conv_body,
        [struct((columns, width))] * 2,
        [x, before, after, mix, form, gain],
        [pltpu.VMEM((extent, width), jnp.bfloat16)],
    )
    norm_near = swap(norm, 1)
    norm_far = swap(norm, 2)
    norm_cross = swap(norm_far, 1)

    wide = struct((columns, width), jnp.float32)
    mine, cross, send = call(
        lambda *refs: column_body(steps, groups, *refs),
        [wide, wide, struct((2, columns, width))],
        [norm, norm_near, norm_far, norm_cross, cot, cot_near, cot_far, cot_cross, *chunks],
        [
            pltpu.VMEM((TEAM * columns, width), jnp.bfloat16),
            pltpu.VMEM((TEAM * columns, width), jnp.bfloat16),
            pltpu.VMEM((width, span), jnp.bfloat16),
            pltpu.VMEM((width, span), jnp.bfloat16),
        ],
    )
    received = swap(send, 1)
    crossing = call(join_body, struct((columns, width)), [cross, received])
    crossed = swap(crossing, 2)
    grads, to_prev, to_next = call(
        grad_body,
        [struct((columns, width)), struct((border, width)), struct((border, width))],
        [mine, received, crossed, conv, cot, gain, mix, form],
    )
    from_prev = step(to_next, 1)
    from_next = step(to_prev, -1)
    local = call(own_body, wide, [grads, mix, form])
    out = pl.pallas_call(
        last_body, out_shape=jax.ShapeDtypeStruct((columns, width), jnp.bfloat16)
    )(*(pltpu.with_memory_space_constraint(v, pltpu.VMEM) for v in (local, from_prev, from_next, boundary)))
    return out[None]


def solution(mesh):
    in_specs = (
        P("groups", "patch", "level"),
        P("groups", "patch", "level"),
        P("patch", None),
        P("patch", None),
        P("patch", None),
        P(),
        P(),
        P("patch", "level"),
        P("patch", "level"),
        P(),
        P(),
        P(),
        P(),
    )
    out_specs = P("groups", "patch", "level")

    return jax.shard_map(
        per_device, mesh=mesh, in_specs=in_specs, out_specs=out_specs, check_vma=False
    )
```

```python
import jax
import jax.numpy as jnp
from jax import lax
from jax.experimental import pallas as pl
from jax.experimental.pallas import tpu as pltpu
from jax.sharding import PartitionSpec as P


CH = 64


def padded(shard, sides, width):
    for axis, dim in sides:
        devices, length = (lax.axis_size(axis), shard.shape[dim])
        up = [(i, (i + 1) % devices) for i in range(devices)]
        down = [(j, i) for i, j in up]
        last = lax.slice_in_dim(shard, length - width, length, axis=dim)
        leading = lax.slice_in_dim(shard, 0, width, axis=dim)
        before = lax.ppermute(last, axis, up)
        after = lax.ppermute(leading, axis, down)
        shard = jnp.concatenate([before, shard, after], axis=dim)
    return shard


def real_form(real_part, imag_part):
    upper = jnp.concatenate([real_part, imag_part], axis=1)
    lower = jnp.concatenate([-imag_part, real_part], axis=1)
    return jnp.concatenate([upper, lower], axis=0)


def rotate_quarter(values, channels):
    shape = values.shape
    split = values.reshape(shape[:-1] + (shape[-1] // channels, 2, channels // 2))
    turned = jnp.stack([-split[..., 1, :], split[..., 0, :]], axis=-2)
    return turned.reshape(shape)


def per_level(values, form, channels):
    shape = values.shape
    split = values.reshape(shape[:-1] + (shape[-1] // channels, channels))
    result = jnp.einsum("bclw,wv->bclv", split, form, preferred_element_type=jnp.float32)
    return result.reshape(shape)


def mlp_back(columns_in, grads, norm_gain, up_mat, down_mat):
    values = columns_in.astype(jnp.float32)
    root_scale = lax.rsqrt(jnp.mean(values * values, axis=-1, keepdims=True) + 1e-05)
    normed = (values * root_scale * norm_gain).astype(jnp.bfloat16)
    pre_act = jnp.einsum("brw,wh->brh", normed, up_mat, preferred_element_type=jnp.float32)
    back_hidden = jnp.einsum("brw,wh->brh", grads, down_mat, preferred_element_type=jnp.float32)
    sigmoid_pre = jax.nn.sigmoid(pre_act)
    grad_pre = (back_hidden * sigmoid_pre * (1.0 + pre_act * (1.0 - sigmoid_pre))).astype(
        jnp.bfloat16
    )
    grad_normed = jnp.einsum("brh,wh->brw", grad_pre, up_mat, preferred_element_type=jnp.float32)
    mixed_mean = jnp.mean(norm_gain * grad_normed * values, axis=-1, keepdims=True)
    return (
        root_scale * norm_gain * grad_normed
        - values * root_scale * root_scale * root_scale * mixed_mean
    )


def general(
    layer_input,
    cotangent,
    neighbours,
    boundary,
    gauge_index,
    gauge_angles,
    norm_gain,
    up_weight,
    down_weight,
    self_real,
    self_imag,
    near_real,
    near_imag,
):
    samples, columns, width = layer_input.shape
    border = boundary.shape[1] // 2
    low_rows = boundary[0, :border]
    high_rows = boundary[0, border:]
    sent = jnp.stack([layer_input[:, low_rows], layer_input[:, high_rows]])
    cycle = padded(sent, (("patch", 0),), 1)
    extended = jnp.concatenate(
        [layer_input, cycle[0], cycle[3], jnp.zeros((samples, 1, width), jnp.bfloat16)], axis=1
    )
    sentinel = columns + 2 * border
    present = (neighbours < sentinel).astype(jnp.float32)
    edge_weight = present / jnp.sum(present, axis=1, keepdims=True)
    phase = gauge_angles[gauge_index]
    cosine = jnp.cos(phase)
    sine = jnp.sin(phase)
    near_form = real_form(near_real, near_imag)
    self_form = real_form(self_real, self_imag)
    gathered = jnp.zeros((samples, columns, width), jnp.float32)
    for entry in range(6):
        near = extended[:, neighbours[:, entry]].astype(jnp.float32)
        turned = rotate_quarter(near, CH)
        gathered = (
            gathered
            + (
                cosine[None, :, entry : entry + 1] * near
                + sine[None, :, entry : entry + 1] * turned
            )
            * edge_weight[None, :, entry : entry + 1]
        )
    gathered = gathered.astype(jnp.bfloat16)
    convolved = per_level(gathered, near_form, CH) + per_level(layer_input, self_form, CH)
    conv_out = (layer_input.astype(jnp.float32) + convolved).astype(jnp.bfloat16)
    conv_out = lax.optimization_barrier(conv_out)
    up_part, down_part = (
        lax.all_gather(up_weight, "patch", axis=0, tiled=True),
        lax.all_gather(down_weight, "patch", axis=0, tiled=True),
    )
    up_whole, down_whole = (
        lax.all_gather(up_part, "level", axis=1, tiled=True),
        lax.all_gather(down_part, "level", axis=1, tiled=True),
    )
    half_cols, half_grads = (
        lax.all_to_all(conv_out, "level", split_axis=1, concat_axis=2, tiled=True),
        lax.all_to_all(cotangent, "level", split_axis=1, concat_axis=2, tiled=True),
    )
    terms = mlp_back(half_cols, half_grads, norm_gain, up_whole, down_whole)
    column_grad = (half_grads.astype(jnp.float32) + terms).astype(jnp.bfloat16)
    grad_conv = lax.all_to_all(column_grad, "level", split_axis=2, concat_axis=1, tiled=True)
    grad_conv = lax.optimization_barrier(grad_conv)
    pulled = per_level(grad_conv, near_form.T, CH)
    own_back = per_level(grad_conv, self_form.T, CH)
    pulled_turn = rotate_quarter(pulled, CH)
    spread = jnp.zeros((samples, sentinel + 1, width), jnp.float32)
    for entry in range(6):
        edges = (
            cosine[None, :, entry : entry + 1] * pulled
            - sine[None, :, entry : entry + 1] * pulled_turn
        ) * edge_weight[None, :, entry : entry + 1]
        spread = spread.at[:, neighbours[:, entry]].add(edges)
    back_sent = jnp.stack(
        [spread[:, columns : columns + border], spread[:, columns + border : sentinel]]
    )
    back_cycle = padded(back_sent.astype(jnp.bfloat16), (("patch", 0),), 1).astype(back_sent.dtype)
    local_terms = (
        spread[:, :columns].at[:, low_rows].add(back_cycle[0]).at[:, high_rows].add(back_cycle[3])
    )
    return (grad_conv.astype(jnp.float32) + own_back + local_terms).astype(jnp.bfloat16)


BLOCK = 256
TEAM = 4


def iota(shape, dim):
    return lax.broadcasted_iota(jnp.int32, shape, dim)


def mm(a, b, dims=((1,), (0,))):
    return lax.dot_general(a, b, (dims, ((), ())), preferred_element_type=jnp.float32)


def turn(values):
    width = values.shape[1]
    half = CH // 2
    later = pltpu.roll(values, width - half, 1)
    earlier = pltpu.roll(values, half, 1)
    return jnp.where(iota(values.shape, 1) % CH < half, -later, earlier)


def call(body, outs, args, scratch=(), raw=(), aliases=()):
    vmem = pl.BlockSpec(memory_space=pltpu.VMEM)
    args = [
        pltpu.with_memory_space_constraint(value, pltpu.HBM if i in raw else pltpu.VMEM)
        for i, value in enumerate(args)
    ]
    specs = [pl.BlockSpec(memory_space=pl.ANY) if i in raw else vmem for i in range(len(args))]
    return pl.pallas_call(
        body,
        out_shape=outs,
        in_specs=specs,
        out_specs=jax.tree.map(lambda _: vmem, outs),
        scratch_shapes=scratch,
        input_output_aliases=dict(aliases),
        compiler_params=pltpu.CompilerParams(vmem_limit_bytes=24 << 20),
    )(*args)


def struct(shape, dtype=jnp.bfloat16):
    return pltpu.VMEM(shape, dtype)


def picked(bound_ref, columns):
    count = bound_ref.shape[1]
    return (iota((columns, count), 0) == bound_ref[...]).astype(jnp.bfloat16)


def load_body(count, *refs):
    up_ref, down_ref, *sources = refs[: 2 + count]
    parts = refs[2 + count : 2 + count + TEAM]
    *targets, sem = refs[2 + count + TEAM :]
    mine = lax.axis_index("patch") % TEAM
    span = parts[0].shape[2]
    pairs = []
    for k in range(TEAM):
        at = pl.multiple_of((mine ^ k) * span, 128)
        for which, ref in enumerate((up_ref, down_ref)):
            pairs.append((ref.at[:, pl.ds(at, span)], parts[k].at[which]))
    pairs += zip(sources, targets)
    copies = [pltpu.make_async_copy(src, dst, sem.at[i]) for i, (src, dst) in enumerate(pairs)]
    for one in copies:
        one.start()
    for one in copies:
        one.wait()


def is_even():
    return lax.axis_index("patch") % 2 == 0


def border_body(x_ref, bound_ref, inner_ref, outer_ref):
    border = inner_ref.shape[0]
    rows = mm(picked(bound_ref, x_ref.shape[0]), x_ref[...], ((0,), (0,))).astype(jnp.bfloat16)
    low, high = rows[:border], rows[border:]
    inner_ref[...] = jnp.where(is_even(), high, low)
    outer_ref[...] = jnp.where(is_even(), low, high)


def spread_form(real_ref, imag_ref):
    half = real_ref.shape[0]
    tall = (iota((BLOCK, half), 0) % half == iota((BLOCK, half), 1)).astype(jnp.bfloat16)

    def tiled(ref):
        rows = mm(tall, ref[...]).astype(jnp.bfloat16)
        return mm(rows, tall, ((1,), (1,)))

    real, imag = tiled(real_ref), tiled(imag_ref)
    row, col = iota((BLOCK, BLOCK), 0), iota((BLOCK, BLOCK), 1)
    row_real = row % CH < half
    col_real = col % CH < half
    form = jnp.where(row_real == col_real, real, jnp.where(row_real, imag, -imag))
    return jnp.where(row // CH == col // CH, form, 0.0).astype(jnp.bfloat16)


def prep_body(sentinel, near_ref, index_ref, angle_ref, nr, ni, sr, si, gains, mix_ref, form_ref, gain_ref):
    entries, columns = near_ref.shape
    table = angle_ref[...]
    index = index_ref[...]
    phases = []
    for k in range(entries):
        spot = jnp.broadcast_to(index[k : k + 1], (table.shape[0], columns))
        found = jnp.take_along_axis(table, spot % 128, axis=1)
        hit = iota(found.shape, 0) == spot // 128
        phases.append(jnp.sum(jnp.where(hit, found, 0.0), axis=0, keepdims=True))
    phase = jnp.concatenate(phases, axis=0)
    near = near_ref[...]
    present = (near < sentinel).astype(jnp.float32)
    weight = present / jnp.sum(present, axis=0, keepdims=True)
    cosine, sine = jnp.cos(phase) * weight, jnp.sin(phase) * weight
    height = mix_ref.shape[1]
    place = iota((height, columns), 0)
    mix_cos = jnp.zeros((height, columns), jnp.float32)
    mix_sin = jnp.zeros((height, columns), jnp.float32)
    for k in range(entries):
        hit = near[k : k + 1] == place
        mix_cos = mix_cos + jnp.where(hit, cosine[k : k + 1], 0.0)
        mix_sin = mix_sin + jnp.where(hit, sine[k : k + 1], 0.0)
    mix_ref[0] = mix_cos.astype(jnp.bfloat16)
    mix_ref[1] = mix_sin.astype(jnp.bfloat16)
    gain_ref[...] = jnp.concatenate([gains[r : r + 1] for r in range(gains.shape[0])], axis=1)
    form_ref[0] = spread_form(nr, ni)
    form_ref[1] = spread_form(sr, si)


def conv_body(x_ref, inner_ref, outer_ref, mix_ref, form_ref, gain_ref, conv_ref, norm_ref, ext):
    columns, width = x_ref.shape
    border = inner_ref.shape[0]
    odd = lax.axis_index("patch") % 2
    ext[:columns] = x_ref[...]
    ext[pl.ds(pl.multiple_of(columns + border * (1 - odd), 16), border)] = inner_ref[...]
    ext[pl.ds(pl.multiple_of(columns + border * odd, 16), border)] = outer_ref[...]
    rest = ext.shape[0] - columns - 2 * border
    if rest:
        ext[columns + 2 * border :] = jnp.zeros((rest, width), jnp.bfloat16)
    source = ext[...]
    over = ((0,), (0,))
    gathered = mm(mix_ref[0], source, over) + turn(mm(mix_ref[1], source, over))
    gathered = gathered.astype(jnp.bfloat16)
    square = jnp.zeros((columns, BLOCK), jnp.float32)
    for b in range(width // BLOCK):
        at = slice(b * BLOCK, (b + 1) * BLOCK)
        x = x_ref[:, at]
        out = x.astype(jnp.float32) + (mm(gathered[:, at], form_ref[0]) + mm(x, form_ref[1]))
        out = out.astype(jnp.bfloat16)
        conv_ref[:, at] = out
        out = out.astype(jnp.float32)
        square = square + out * out
    scale = lax.rsqrt(jnp.sum(square, axis=1, keepdims=True) / width + 1e-05)
    norm_ref[...] = (conv_ref[...].astype(jnp.float32) * scale * gain_ref[...]).astype(jnp.bfloat16)


def ring_place(group, groups):
    return jnp.where(group % 2 == 0, group // 2, groups - 1 - group // 2)


def ring_group(place, groups):
    return jnp.where(place < groups // 2, 2 * place, 2 * (groups - 1 - place) + 1)


STACK = (1, 3, 0, 2)


def early_body(steps, groups, *refs):
    norms, grads, chunks = refs[:TEAM], refs[TEAM : 2 * TEAM], refs[2 * TEAM : 2 * TEAM + len(steps)]
    ups, pre_ref, back_ref, x_last, g_last, xs, gs, downs = refs[2 * TEAM + len(steps) :]
    columns = norms[0].shape[0]
    span = ups.shape[1]
    me = lax.axis_index("patch")
    group, member = me // TEAM, me % TEAM
    place = ring_place(group, groups)
    for k, m in enumerate(STACK):
        xs[k * columns : (k + 1) * columns] = norms[m][...]
        gs[k * columns : (k + 1) * columns] = grads[m][...]
    for (shift, first), ref in zip(steps, chunks):
        rows = ref.shape[1] // 2
        owner = ring_group((place + shift + groups) % groups, groups)
        for half in range(2):
            at = pl.multiple_of((owner * TEAM + (member ^ (first + half))) * rows, 16)
            part = slice(half * rows, (half + 1) * rows)
            ups[pl.ds(at, rows)] = ref[0, part]
            downs[pl.ds(at, rows)] = ref[1, part]
    owner = ring_group((place + groups // 2) % groups, groups)
    tall = TEAM * rows
    blank = jnp.zeros((tall, span), jnp.bfloat16)
    at = pl.multiple_of(owner * tall, 16)
    ups[pl.ds(at, tall)] = blank
    downs[pl.ds(at, tall)] = blank
    for g in range(groups):

        @pl.when(owner == g)
        def _():
            x_last[...] = xs[:, g * tall : (g + 1) * tall]
            g_last[...] = gs[:, g * tall : (g + 1) * tall]

    pre_ref[...] = mm(xs[...], ups[...])
    back_ref[...] = mm(gs[...], downs[...])


def send_body(groups, ups_in, pre_ref, back_ref, x_last, g_last, first_ref, second_ref, ups, gate_ref, send_ref, up, down):
    me = lax.axis_index("patch")
    group, member = me // TEAM, me % TEAM
    owner = ring_group((ring_place(group, groups) + groups // 2) % groups, groups)
    rows = first_ref.shape[1] // 2
    for k, ref in ((0, first_ref), (2, second_ref)):
        for half in range(2):
            at = pl.multiple_of((member ^ (k + half)) * rows, 16)
            part = slice(half * rows, (half + 1) * rows)
            up[pl.ds(at, rows)] = ref[0, part]
            down[pl.ds(at, rows)] = ref[1, part]
    tall = up.shape[0]
    ups[pl.ds(pl.multiple_of(owner * tall, 16), tall)] = up[...]
    pre_act = pre_ref[...] + mm(x_last[...], up[...])
    back = back_ref[...] + mm(g_last[...], down[...])
    gate = jax.nn.sigmoid(pre_act)
    grad_pre = (back * gate * (1.0 + pre_act * (1.0 - gate))).astype(jnp.bfloat16)
    gate_ref[...] = grad_pre
    columns = send_ref.shape[1]
    rows = mm(grad_pre[: 2 * columns], ups[...], ((1,), (1,))).astype(jnp.bfloat16)
    send_ref[0] = rows[:columns]
    send_ref[1] = rows[columns:]


def keep_body(gate_ref, ups, mine_ref, cross_ref):
    columns = mine_ref.shape[0]
    rows = mm(gate_ref[2 * columns :], ups[...], ((1,), (1,)))
    mine_ref[...] = rows[:columns]
    cross_ref[...] = rows[columns:]


def shifted_back(mix, form, grads):
    spread = mm(mix[0], grads) - turn(mm(mix[1], grads))
    spread = spread.astype(jnp.bfloat16)
    width = grads.shape[1]
    return [
        mm(spread[:, b * BLOCK : (b + 1) * BLOCK], form, ((1,), (1,)))
        for b in range(width // BLOCK)
    ]


def join_body(cross_ref, part_ref, out_ref):
    out_ref[...] = (cross_ref[...] + part_ref[1].astype(jnp.float32)).astype(jnp.bfloat16)


def grad_body(mine_ref, part_ref, cross_ref, conv_ref, cot_ref, gain_ref, mix_ref, form_ref, grad_ref, inner_ref, outer_ref):
    columns, width = conv_ref.shape
    border = inner_ref.shape[0]
    even = is_even()
    grad_normed = mine_ref[...] + part_ref[0].astype(jnp.float32) + cross_ref[...].astype(jnp.float32)
    values = conv_ref[...].astype(jnp.float32)
    scaled = gain_ref[...] * grad_normed
    scale = lax.rsqrt(jnp.sum(values * values, axis=1, keepdims=True) / width + 1e-05)
    mixed = jnp.sum(scaled * values, axis=1, keepdims=True) / width
    grads = cot_ref[...].astype(jnp.float32) + (
        scale * scaled - values * (scale * scale * scale * mixed)
    )
    grads = grads.astype(jnp.bfloat16)
    grad_ref[...] = grads
    outer = [mix_ref[i, columns:] for i in range(2)]
    for b, rows in enumerate(shifted_back(outer, form_ref[0], grads)):
        at = slice(b * BLOCK, (b + 1) * BLOCK)
        rows = rows.astype(jnp.bfloat16)
        prev, later = rows[:border], rows[border : 2 * border]
        inner_ref[:, at] = jnp.where(even, later, prev)
        outer_ref[:, at] = jnp.where(even, prev, later)


def own_body(grad_ref, mix_ref, form_ref, local_ref):
    columns, _ = grad_ref.shape
    grads = grad_ref[...]
    inner = [mix_ref[i, :columns] for i in range(2)]
    for b, rows in enumerate(shifted_back(inner, form_ref[0], grads)):
        at = slice(b * BLOCK, (b + 1) * BLOCK)
        own = grads[:, at]
        local_ref[:, at] = own.astype(jnp.float32) + (mm(own, form_ref[1], ((1,), (1,))) + rows)


def last_body(local_ref, inner_ref, outer_ref, bound_ref, out_ref):
    border = inner_ref.shape[0]
    chosen = picked(bound_ref, local_ref.shape[0]).astype(jnp.float32)
    low, high = chosen[:, :border], chosen[:, border:]
    inner = jnp.where(is_even(), high, low).astype(jnp.bfloat16)
    outer = jnp.where(is_even(), low, high).astype(jnp.bfloat16)
    total = local_ref[...] + mm(inner, inner_ref[...]) + mm(outer, outer_ref[...])
    out_ref[...] = total.astype(jnp.bfloat16)


def per_device(
    layer_input,
    cotangent,
    neighbours,
    boundary,
    gauge_index,
    gauge_angles,
    norm_gain,
    up_weight,
    down_weight,
    self_real,
    self_imag,
    near_real,
    near_imag,
):
    samples, columns, width = layer_input.shape
    devices = lax.axis_size("patch")
    rows, hidden = up_weight.shape
    border = boundary.shape[1] // 2
    span = hidden // TEAM
    fits = (
        lax.axis_size("level") == 1
        and samples == 1
        and devices % (2 * TEAM) == 0
        and width % BLOCK == 0
        and hidden % (TEAM * 128) == 0
        and rows % 16 == 0
        and border % 16 == 0
        and 2 * border <= columns
        and width * span <= 1 << 20
        and gauge_angles.shape[0] % 128 == 0
        and columns == 128
    )
    if not fits:
        return general(
            layer_input,
            cotangent,
            neighbours,
            boundary,
            gauge_index,
            gauge_angles,
            norm_gain,
            up_weight,
            down_weight,
            self_real,
            self_imag,
            near_real,
            near_imag,
        )
    groups = devices // TEAM
    sentinel = columns + 2 * border
    extent = -(-sentinel // 128) * 128
    x = layer_input[0]
    cot = cotangent[0]

    def permute(value, pairs):
        return lax.ppermute(value, "patch", pairs)

    def swap(value, bits):
        return permute(value, [(i, i ^ bits) for i in range(devices)])

    def outer(value):
        return permute(value, [(i, (i - 1 + 2 * (i % 2)) % devices) for i in range(devices)])

    order = list(range(0, groups, 2)) + list(range(groups - 1, 0, -2))

    def around(value, shift):
        pairs = [
            (order[k] * TEAM + j, order[(k + shift) % groups] * TEAM + j)
            for k in range(groups)
            for j in range(TEAM)
        ]
        return permute(value, pairs)

    held = [
        x,
        cot,
        boundary,
        neighbours.T,
        gauge_index.T,
        gauge_angles.reshape(-1, 128),
        near_real,
        near_imag,
        self_real,
        self_imag,
        norm_gain.reshape(-1, 128),
    ]
    loaded = call(
        lambda *refs: load_body(len(held), *refs),
        [struct((2, rows, span))] * TEAM + [struct(value.shape, value.dtype) for value in held],
        [up_weight, down_weight, *held],
        [pltpu.SemaphoreType.DMA((2 * TEAM + len(held),))],
        range(2 + len(held)),
    )
    parts, (x, cot, boundary, *tables) = loaded[:TEAM], loaded[TEAM:]
    near_part = swap(parts[1], 1)
    far_parts = [swap(parts[2], 2), swap(parts[3], 3)]
    first = jnp.concatenate([parts[0], near_part], axis=1)
    second = jnp.concatenate(far_parts, axis=1)
    steps, chunks = [(0, 0), (0, 2)], [first, second]
    forth = [first, second]
    back = [first, second]
    half = groups // 2
    for s in range(1, half + 1):
        for which in range(2):
            if s < half or which == 0:
                forth[which] = around(forth[which], 1)
                steps.append((-s, 2 * which))
                chunks.append(forth[which])
            if s < half or which == 1:
                back[which] = around(back[which], -1)
                steps.append((s, 2 * which))
                chunks.append(back[which])

    inner_rows, outer_rows = call(border_body, [struct((border, width))] * 2, [x, boundary])
    inner_rows = swap(inner_rows, 1)
    outer_rows = outer(outer_rows)
    cot_near = swap(cot, 1)
    cot_far = swap(cot, 2)
    cot_cross = swap(cot_far, 1)

    mix, form, gain = call(
        lambda *refs: prep_body(sentinel, *refs),
        [
            struct((2, extent, columns)),
            struct((2, BLOCK, BLOCK)),
            struct((1, width), jnp.float32),
        ],
        tables,
    )
    conv, norm = call(
        conv_body,
        [struct((columns, width))] * 2,
        [x, inner_rows, outer_rows, mix, form, gain],
        [pltpu.VMEM((extent, width), jnp.bfloat16)],
    )
    norm_near = swap(norm, 1)
    norm_far = swap(norm, 2)
    norm_cross = swap(norm_far, 1)

    wide = struct((columns, width), jnp.float32)
    team = TEAM * columns
    late = len(steps) - 2
    ups, pre, back_sum, x_last, g_last = call(
        lambda *refs: early_body(steps[:late], groups, *refs),
        [struct((width, span))]
        + [struct((team, span), jnp.float32)] * 2
        + [struct((team, TEAM * rows))] * 2,
        [norm, norm_near, norm_far, norm_cross, cot, cot_near, cot_far, cot_cross, *chunks[:late]],
        [
            pltpu.VMEM((team, width), jnp.bfloat16),
            pltpu.VMEM((team, width), jnp.bfloat16),
            pltpu.VMEM((width, span), jnp.bfloat16),
        ],
    )
    ups, gate, send = call(
        lambda *refs: send_body(groups, *refs),
        [struct((width, span)), struct((team, span)), struct((2, columns, width))],
        [ups, pre, back_sum, x_last, g_last, *chunks[late:]],
        [pltpu.VMEM((TEAM * rows, span), jnp.bfloat16)] * 2,
        (),
        ((0, 0),),
    )
    mine, cross = call(keep_body, [wide, wide], [gate, ups])
    received = swap(send, 1)
    crossing = call(join_body, struct((columns, width)), [cross, received])
    crossed = swap(crossing, 2)
    grads, inner_back, outer_back = call(
        grad_body,
        [struct((columns, width)), struct((border, width)), struct((border, width))],
        [mine, received, crossed, conv, cot, gain, mix, form],
    )
    inner_back = swap(inner_back, 1)
    outer_back = outer(outer_back)
    local = call(own_body, wide, [grads, mix, form])
    out = pl.pallas_call(
        last_body, out_shape=jax.ShapeDtypeStruct((columns, width), jnp.bfloat16)
    )(*(pltpu.with_memory_space_constraint(v, pltpu.VMEM) for v in (local, inner_back, outer_back, boundary)))
    return out[None]


def solution(mesh):
    in_specs = (
        P("groups", "patch", "level"),
        P("groups", "patch", "level"),
        P("patch", None),
        P("patch", None),
        P("patch", None),
        P(),
        P(),
        P("patch", "level"),
        P("patch", "level"),
        P(),
        P(),
        P(),
        P(),
    )
    out_specs = P("groups", "patch", "level")

    return jax.shard_map(
        per_device, mesh=mesh, in_specs=in_specs, out_specs=out_specs, check_vma=False
    )
```

```python
import jax
import jax.numpy as jnp
from jax import lax
from jax.experimental import pallas as pl
from jax.experimental.pallas import tpu as pltpu
from jax.sharding import PartitionSpec as P


CH = 64


def padded(shard, sides, width):
    for axis, dim in sides:
        devices, length = (lax.axis_size(axis), shard.shape[dim])
        up = [(i, (i + 1) % devices) for i in range(devices)]
        down = [(j, i) for i, j in up]
        last = lax.slice_in_dim(shard, length - width, length, axis=dim)
        leading = lax.slice_in_dim(shard, 0, width, axis=dim)
        before = lax.ppermute(last, axis, up)
        after = lax.ppermute(leading, axis, down)
        shard = jnp.concatenate([before, shard, after], axis=dim)
    return shard


def real_form(real_part, imag_part):
    upper = jnp.concatenate([real_part, imag_part], axis=1)
    lower = jnp.concatenate([-imag_part, real_part], axis=1)
    return jnp.concatenate([upper, lower], axis=0)


def rotate_quarter(values, channels):
    shape = values.shape
    split = values.reshape(shape[:-1] + (shape[-1] // channels, 2, channels // 2))
    turned = jnp.stack([-split[..., 1, :], split[..., 0, :]], axis=-2)
    return turned.reshape(shape)


def per_level(values, form, channels):
    shape = values.shape
    split = values.reshape(shape[:-1] + (shape[-1] // channels, channels))
    result = jnp.einsum("bclw,wv->bclv", split, form, preferred_element_type=jnp.float32)
    return result.reshape(shape)


def mlp_back(columns_in, grads, norm_gain, up_mat, down_mat):
    values = columns_in.astype(jnp.float32)
    root_scale = lax.rsqrt(jnp.mean(values * values, axis=-1, keepdims=True) + 1e-05)
    normed = (values * root_scale * norm_gain).astype(jnp.bfloat16)
    pre_act = jnp.einsum("brw,wh->brh", normed, up_mat, preferred_element_type=jnp.float32)
    back_hidden = jnp.einsum("brw,wh->brh", grads, down_mat, preferred_element_type=jnp.float32)
    sigmoid_pre = jax.nn.sigmoid(pre_act)
    grad_pre = (back_hidden * sigmoid_pre * (1.0 + pre_act * (1.0 - sigmoid_pre))).astype(
        jnp.bfloat16
    )
    grad_normed = jnp.einsum("brh,wh->brw", grad_pre, up_mat, preferred_element_type=jnp.float32)
    mixed_mean = jnp.mean(norm_gain * grad_normed * values, axis=-1, keepdims=True)
    return (
        root_scale * norm_gain * grad_normed
        - values * root_scale * root_scale * root_scale * mixed_mean
    )


def general(
    layer_input,
    cotangent,
    neighbours,
    boundary,
    gauge_index,
    gauge_angles,
    norm_gain,
    up_weight,
    down_weight,
    self_real,
    self_imag,
    near_real,
    near_imag,
):
    samples, columns, width = layer_input.shape
    border = boundary.shape[1] // 2
    low_rows = boundary[0, :border]
    high_rows = boundary[0, border:]
    sent = jnp.stack([layer_input[:, low_rows], layer_input[:, high_rows]])
    cycle = padded(sent, (("patch", 0),), 1)
    extended = jnp.concatenate(
        [layer_input, cycle[0], cycle[3], jnp.zeros((samples, 1, width), jnp.bfloat16)], axis=1
    )
    sentinel = columns + 2 * border
    present = (neighbours < sentinel).astype(jnp.float32)
    edge_weight = present / jnp.sum(present, axis=1, keepdims=True)
    phase = gauge_angles[gauge_index]
    cosine = jnp.cos(phase)
    sine = jnp.sin(phase)
    near_form = real_form(near_real, near_imag)
    self_form = real_form(self_real, self_imag)
    gathered = jnp.zeros((samples, columns, width), jnp.float32)
    for entry in range(6):
        near = extended[:, neighbours[:, entry]].astype(jnp.float32)
        turned = rotate_quarter(near, CH)
        gathered = (
            gathered
            + (
                cosine[None, :, entry : entry + 1] * near
                + sine[None, :, entry : entry + 1] * turned
            )
            * edge_weight[None, :, entry : entry + 1]
        )
    gathered = gathered.astype(jnp.bfloat16)
    convolved = per_level(gathered, near_form, CH) + per_level(layer_input, self_form, CH)
    conv_out = (layer_input.astype(jnp.float32) + convolved).astype(jnp.bfloat16)
    conv_out = lax.optimization_barrier(conv_out)
    up_part, down_part = (
        lax.all_gather(up_weight, "patch", axis=0, tiled=True),
        lax.all_gather(down_weight, "patch", axis=0, tiled=True),
    )
    up_whole, down_whole = (
        lax.all_gather(up_part, "level", axis=1, tiled=True),
        lax.all_gather(down_part, "level", axis=1, tiled=True),
    )
    half_cols, half_grads = (
        lax.all_to_all(conv_out, "level", split_axis=1, concat_axis=2, tiled=True),
        lax.all_to_all(cotangent, "level", split_axis=1, concat_axis=2, tiled=True),
    )
    terms = mlp_back(half_cols, half_grads, norm_gain, up_whole, down_whole)
    column_grad = (half_grads.astype(jnp.float32) + terms).astype(jnp.bfloat16)
    grad_conv = lax.all_to_all(column_grad, "level", split_axis=2, concat_axis=1, tiled=True)
    grad_conv = lax.optimization_barrier(grad_conv)
    pulled = per_level(grad_conv, near_form.T, CH)
    own_back = per_level(grad_conv, self_form.T, CH)
    pulled_turn = rotate_quarter(pulled, CH)
    spread = jnp.zeros((samples, sentinel + 1, width), jnp.float32)
    for entry in range(6):
        edges = (
            cosine[None, :, entry : entry + 1] * pulled
            - sine[None, :, entry : entry + 1] * pulled_turn
        ) * edge_weight[None, :, entry : entry + 1]
        spread = spread.at[:, neighbours[:, entry]].add(edges)
    back_sent = jnp.stack(
        [spread[:, columns : columns + border], spread[:, columns + border : sentinel]]
    )
    back_cycle = padded(back_sent.astype(jnp.bfloat16), (("patch", 0),), 1).astype(back_sent.dtype)
    local_terms = (
        spread[:, :columns].at[:, low_rows].add(back_cycle[0]).at[:, high_rows].add(back_cycle[3])
    )
    return (grad_conv.astype(jnp.float32) + own_back + local_terms).astype(jnp.bfloat16)


BLOCK = 256
TEAM = 4


def iota(shape, dim):
    return lax.broadcasted_iota(jnp.int32, shape, dim)


def mm(a, b, dims=((1,), (0,))):
    return lax.dot_general(a, b, (dims, ((), ())), preferred_element_type=jnp.float32)


def turn(values):
    width = values.shape[1]
    half = CH // 2
    later = pltpu.roll(values, width - half, 1)
    earlier = pltpu.roll(values, half, 1)
    return jnp.where(iota(values.shape, 1) % CH < half, -later, earlier)


def call(body, outs, args, scratch=(), raw=(), aliases=()):
    vmem = pl.BlockSpec(memory_space=pltpu.VMEM)
    args = [
        pltpu.with_memory_space_constraint(value, pltpu.HBM if i in raw else pltpu.VMEM)
        for i, value in enumerate(args)
    ]
    specs = [pl.BlockSpec(memory_space=pl.ANY) if i in raw else vmem for i in range(len(args))]
    return pl.pallas_call(
        body,
        out_shape=outs,
        in_specs=specs,
        out_specs=jax.tree.map(lambda _: vmem, outs),
        scratch_shapes=scratch,
        input_output_aliases=dict(aliases),
        compiler_params=pltpu.CompilerParams(vmem_limit_bytes=24 << 20),
    )(*args)


def struct(shape, dtype=jnp.bfloat16):
    return pltpu.VMEM(shape, dtype)


def picked(bound_ref, columns):
    count = bound_ref.shape[1]
    return (iota((columns, count), 0) == bound_ref[...]).astype(jnp.bfloat16)


def copy_all(pairs, sem):
    copies = [pltpu.make_async_copy(src, dst, sem.at[i]) for i, (src, dst) in enumerate(pairs)]
    for one in copies:
        one.start()
    for one in copies:
        one.wait()


def weights_body(up_ref, down_ref, *refs):
    *parts, sem = refs
    mine = lax.axis_index("patch") % TEAM
    span = parts[0].shape[2]
    pairs = []
    for k in range(TEAM):
        at = pl.multiple_of((mine ^ k) * span, 128)
        for which, ref in enumerate((up_ref, down_ref)):
            pairs.append((ref.at[:, pl.ds(at, span)], parts[k].at[which]))
    copy_all(pairs, sem)


def load_body(count, *refs):
    copy_all(list(zip(refs[:count], refs[count : 2 * count])), refs[-1])


def is_even():
    return lax.axis_index("patch") % 2 == 0


def border_body(x_ref, bound_ref, inner_ref, outer_ref):
    border = inner_ref.shape[0]
    rows = mm(picked(bound_ref, x_ref.shape[0]), x_ref[...], ((0,), (0,))).astype(jnp.bfloat16)
    low, high = rows[:border], rows[border:]
    inner_ref[...] = jnp.where(is_even(), high, low)
    outer_ref[...] = jnp.where(is_even(), low, high)


def spread_form(real_ref, imag_ref):
    half = real_ref.shape[0]
    tall = (iota((BLOCK, half), 0) % half == iota((BLOCK, half), 1)).astype(jnp.bfloat16)

    def tiled(ref):
        rows = mm(tall, ref[...]).astype(jnp.bfloat16)
        return mm(rows, tall, ((1,), (1,)))

    real, imag = tiled(real_ref), tiled(imag_ref)
    row, col = iota((BLOCK, BLOCK), 0), iota((BLOCK, BLOCK), 1)
    row_real = row % CH < half
    col_real = col % CH < half
    form = jnp.where(row_real == col_real, real, jnp.where(row_real, imag, -imag))
    return jnp.where(row // CH == col // CH, form, 0.0).astype(jnp.bfloat16)


def prep_body(sentinel, near_ref, index_ref, angle_ref, nr, ni, sr, si, gains, mix_ref, form_ref, gain_ref):
    entries, columns = near_ref.shape
    table = angle_ref[...]
    index = index_ref[...]
    phases = []
    for k in range(entries):
        spot = jnp.broadcast_to(index[k : k + 1], (table.shape[0], columns))
        found = jnp.take_along_axis(table, spot % 128, axis=1)
        hit = iota(found.shape, 0) == spot // 128
        phases.append(jnp.sum(jnp.where(hit, found, 0.0), axis=0, keepdims=True))
    phase = jnp.concatenate(phases, axis=0)
    near = near_ref[...]
    present = (near < sentinel).astype(jnp.float32)
    weight = present / jnp.sum(present, axis=0, keepdims=True)
    cosine, sine = jnp.cos(phase) * weight, jnp.sin(phase) * weight
    height = mix_ref.shape[1]
    place = iota((height, columns), 0)
    mix_cos = jnp.zeros((height, columns), jnp.float32)
    mix_sin = jnp.zeros((height, columns), jnp.float32)
    for k in range(entries):
        hit = near[k : k + 1] == place
        mix_cos = mix_cos + jnp.where(hit, cosine[k : k + 1], 0.0)
        mix_sin = mix_sin + jnp.where(hit, sine[k : k + 1], 0.0)
    mix_ref[0] = mix_cos.astype(jnp.bfloat16)
    mix_ref[1] = mix_sin.astype(jnp.bfloat16)
    gain_ref[...] = jnp.concatenate([gains[r : r + 1] for r in range(gains.shape[0])], axis=1)
    form_ref[0] = spread_form(nr, ni)
    form_ref[1] = spread_form(sr, si)


def border_mix(mix_ref, columns, border, which):
    at = pl.multiple_of(columns + border * which, 16)
    return [mix_ref[i, pl.ds(at, border)] for i in range(2)]


def conv_body(x_ref, inner_ref, outer_ref, mix_ref, form_ref, gain_ref, conv_ref, norm_ref, edge_ref, ext):
    columns, width = x_ref.shape
    border = inner_ref.shape[0]
    odd = lax.axis_index("patch") % 2
    ext[:columns] = x_ref[...]
    ext[pl.ds(pl.multiple_of(columns + border * (1 - odd), 16), border)] = inner_ref[...]
    ext[pl.ds(pl.multiple_of(columns + border * odd, 16), border)] = outer_ref[...]
    rest = ext.shape[0] - columns - 2 * border
    if rest:
        ext[columns + 2 * border :] = jnp.zeros((rest, width), jnp.bfloat16)
    source = ext[...]
    over = ((0,), (0,))
    gathered = mm(mix_ref[0], source, over) + turn(mm(mix_ref[1], source, over))
    gathered = gathered.astype(jnp.bfloat16)
    square = jnp.zeros((columns, BLOCK), jnp.float32)
    for b in range(width // BLOCK):
        at = slice(b * BLOCK, (b + 1) * BLOCK)
        x = x_ref[:, at]
        out = x.astype(jnp.float32) + (mm(gathered[:, at], form_ref[0]) + mm(x, form_ref[1]))
        out = out.astype(jnp.bfloat16)
        conv_ref[:, at] = out
        out = out.astype(jnp.float32)
        square = square + out * out
    scale = lax.rsqrt(jnp.sum(square, axis=1, keepdims=True) / width + 1e-05)
    norm_ref[...] = (conv_ref[...].astype(jnp.float32) * scale * gain_ref[...]).astype(jnp.bfloat16)
    across = jnp.broadcast_to(scale, (columns, columns)).T[:1]
    for i, rows in enumerate(border_mix(mix_ref, columns, border, odd)):
        edge_ref[i] = (rows.astype(jnp.float32) * across).astype(jnp.bfloat16)


def ring_place(group, groups):
    return jnp.where(group % 2 == 0, group // 2, groups - 1 - group // 2)


def ring_group(place, groups):
    return jnp.where(place < groups // 2, 2 * place, 2 * (groups - 1 - place) + 1)


STACK = (1, 3, 0, 2)


def far_owner(groups):
    place = ring_place(lax.axis_index("patch") // TEAM, groups)
    return ring_group((place + groups // 2) % groups, groups)


def take_columns(owner, groups, pairs):
    for g in range(groups):

        @pl.when(owner == g)
        def _():
            for source, target in pairs:
                tall = target.shape[1]
                target[...] = source[:, g * tall : (g + 1) * tall]


def early_body(steps, groups, *refs):
    norms, grads, chunks = refs[:2], refs[2 : 2 + TEAM], refs[2 + TEAM : 2 + TEAM + len(steps)]
    ups, pre_ref, back_ref, x_last, g_last, xs, gs, downs = refs[2 + TEAM + len(steps) :]
    columns = norms[0].shape[0]
    span = ups.shape[1]
    me = lax.axis_index("patch")
    group, member = me // TEAM, me % TEAM
    place = ring_place(group, groups)
    for k in range(2):
        xs[k * columns : (k + 1) * columns] = norms[k][...]
    for k, m in enumerate(STACK):
        gs[k * columns : (k + 1) * columns] = grads[m][...]
    for (shift, first), ref in zip(steps, chunks):
        rows = ref.shape[1] // 2
        owner = ring_group((place + shift + groups) % groups, groups)
        for half in range(2):
            at = pl.multiple_of((owner * TEAM + (member ^ (first + half))) * rows, 16)
            part = slice(half * rows, (half + 1) * rows)
            ups[pl.ds(at, rows)] = ref[0, part]
            downs[pl.ds(at, rows)] = ref[1, part]
    owner = far_owner(groups)
    tall = TEAM * rows
    blank = jnp.zeros((tall, span), jnp.bfloat16)
    at = pl.multiple_of(owner * tall, 16)
    ups[pl.ds(at, tall)] = blank
    downs[pl.ds(at, tall)] = blank
    take_columns(owner, groups, ((xs, x_last), (gs, g_last)))
    pre_ref[...] = mm(xs[...], ups[...])
    back_ref[...] = mm(gs[...], downs[...])


def rest_body(groups, cross_ref, far_ref, ups, pre_ref, x_last, xs):
    columns = cross_ref.shape[0]
    xs[:columns] = cross_ref[...]
    xs[columns:] = far_ref[...]
    take_columns(far_owner(groups), groups, ((xs, x_last),))
    pre_ref[...] = mm(xs[...], ups[...])


def send_body(groups, ups_in, pre_a, pre_b, back_ref, xa_last, xb_last, g_last, *refs):
    parts, (ups, gate_ref, send_ref, up, down) = refs[:4], refs[4:]
    member = lax.axis_index("patch") % TEAM
    rows = parts[0].shape[1] // 2
    for k in range(2):
        for half in range(2):
            at = pl.multiple_of((member ^ (2 * k + half)) * rows, 16)
            part = slice(half * rows, (half + 1) * rows)
            up[pl.ds(at, rows)] = parts[2 * k][0, part]
            down[pl.ds(at, rows)] = parts[2 * k + 1][0, part]
    tall = up.shape[0]
    ups[pl.ds(pl.multiple_of(far_owner(groups) * tall, 16), tall)] = up[...]
    columns = send_ref.shape[1]
    first = pre_a[...] + mm(xa_last[...], up[...])
    second = pre_b[...] + mm(xb_last[...], up[...])
    pre_act = jnp.concatenate(
        [first[:columns], second[:columns], first[columns:], second[columns:]], axis=0
    )
    back = back_ref[...] + mm(g_last[...], down[...])
    gate = jax.nn.sigmoid(pre_act)
    grad_pre = (back * gate * (1.0 + pre_act * (1.0 - gate))).astype(jnp.bfloat16)
    gate_ref[...] = grad_pre
    rows = mm(grad_pre[: 2 * columns], ups[...], ((1,), (1,))).astype(jnp.bfloat16)
    send_ref[0] = rows[:columns]
    send_ref[1] = rows[columns:]


def keep_body(gate_ref, ups, mine_ref, cross_ref):
    columns = mine_ref.shape[0]
    rows = mm(gate_ref[2 * columns :], ups[...], ((1,), (1,)))
    mine_ref[...] = rows[:columns]
    cross_ref[...] = rows[columns:]


def shifted_back(mix, form, grads):
    spread = mm(mix[0], grads) - turn(mm(mix[1], grads))
    spread = spread.astype(jnp.bfloat16)
    width = grads.shape[1]
    return [
        mm(spread[:, b * BLOCK : (b + 1) * BLOCK], form, ((1,), (1,)))
        for b in range(width // BLOCK)
    ]


def join_body(cross_ref, part_ref, out_ref):
    out_ref[...] = (cross_ref[...] + part_ref[1].astype(jnp.float32)).astype(jnp.bfloat16)


def column_grad(grad_normed, values, scale, gain):
    scaled = gain * grad_normed
    mixed = jnp.sum(scaled * values, axis=1, keepdims=True) / values.shape[1]
    return scale * scaled - values * (scale * scale * scale * mixed)


def scale_of(values):
    return lax.rsqrt(jnp.sum(values * values, axis=1, keepdims=True) / values.shape[1] + 1e-05)


def edge_body(
    mine_ref, cross_ref, part_ref, conv_ref, cot_ref, far_ref, gain_ref, mix_ref, edge_ref, form_ref, own_ref, other_ref
):
    columns, _ = conv_ref.shape
    border = own_ref.shape[0]
    odd = lax.axis_index("patch") % 2
    values = conv_ref[...].astype(jnp.float32)
    share = mine_ref[...] + part_ref[0].astype(jnp.float32)
    grads = column_grad(share, values, scale_of(values), gain_ref[...])
    grads = (cot_ref[...].astype(jnp.float32) + grads).astype(jnp.bfloat16)
    outer = border_mix(mix_ref, columns, border, odd)
    scaled_values = far_ref[...].astype(jnp.float32) / gain_ref[...]
    share = cross_ref[...] + part_ref[1].astype(jnp.float32)
    others = column_grad(share, scaled_values, 1.0, gain_ref[...]).astype(jnp.bfloat16)
    edge = [edge_ref[i] for i in range(2)]
    for ref, mix, source in ((own_ref, outer, grads), (other_ref, edge, others)):
        for b, rows in enumerate(shifted_back(mix, form_ref[0], source)):
            ref[:, b * BLOCK : (b + 1) * BLOCK] = rows.astype(jnp.bfloat16)


def grad_body(
    mine_ref, part_ref, cross_ref, conv_ref, cot_ref, gain_ref, mix_ref, form_ref, grad_ref, inner_ref
):
    columns, _ = conv_ref.shape
    border = inner_ref.shape[0]
    odd = lax.axis_index("patch") % 2
    grad_normed = mine_ref[...] + part_ref[0].astype(jnp.float32) + cross_ref[...].astype(jnp.float32)
    values = conv_ref[...].astype(jnp.float32)
    grads = column_grad(grad_normed, values, scale_of(values), gain_ref[...])
    grads = (cot_ref[...].astype(jnp.float32) + grads).astype(jnp.bfloat16)
    grad_ref[...] = grads
    inner = border_mix(mix_ref, columns, border, 1 - odd)
    for b, rows in enumerate(shifted_back(inner, form_ref[0], grads)):
        inner_ref[:, b * BLOCK : (b + 1) * BLOCK] = rows.astype(jnp.bfloat16)


def own_body(grad_ref, mix_ref, form_ref, local_ref):
    columns, _ = grad_ref.shape
    grads = grad_ref[...]
    inner = [mix_ref[i, :columns] for i in range(2)]
    for b, rows in enumerate(shifted_back(inner, form_ref[0], grads)):
        at = slice(b * BLOCK, (b + 1) * BLOCK)
        own = grads[:, at]
        local_ref[:, at] = own.astype(jnp.float32) + (mm(own, form_ref[1], ((1,), (1,))) + rows)


def last_body(local_ref, inner_ref, outer_ref, other_ref, bound_ref, out_ref):
    border = inner_ref.shape[0]
    chosen = picked(bound_ref, local_ref.shape[0]).astype(jnp.float32)
    low, high = chosen[:, :border], chosen[:, border:]
    inner = jnp.where(is_even(), high, low).astype(jnp.bfloat16)
    outer = jnp.where(is_even(), low, high).astype(jnp.bfloat16)
    total = local_ref[...] + mm(inner, inner_ref[...])
    total = total + (mm(outer, outer_ref[...]) + mm(outer, other_ref[...]))
    out_ref[...] = total.astype(jnp.bfloat16)


def per_device(
    layer_input,
    cotangent,
    neighbours,
    boundary,
    gauge_index,
    gauge_angles,
    norm_gain,
    up_weight,
    down_weight,
    self_real,
    self_imag,
    near_real,
    near_imag,
):
    samples, columns, width = layer_input.shape
    devices = lax.axis_size("patch")
    rows, hidden = up_weight.shape
    border = boundary.shape[1] // 2
    span = hidden // TEAM
    fits = (
        lax.axis_size("level") == 1
        and samples == 1
        and devices % (2 * TEAM) == 0
        and width % BLOCK == 0
        and hidden % (TEAM * 128) == 0
        and rows % 16 == 0
        and border % 16 == 0
        and 2 * border <= columns
        and width * span <= 1 << 20
        and gauge_angles.shape[0] % 128 == 0
        and columns == 128
    )
    if not fits:
        return general(
            layer_input,
            cotangent,
            neighbours,
            boundary,
            gauge_index,
            gauge_angles,
            norm_gain,
            up_weight,
            down_weight,
            self_real,
            self_imag,
            near_real,
            near_imag,
        )
    groups = devices // TEAM
    sentinel = columns + 2 * border
    extent = -(-sentinel // 128) * 128
    x = layer_input[0]
    cot = cotangent[0]

    def permute(value, pairs):
        return lax.ppermute(value, "patch", pairs)

    def swap(value, bits):
        return permute(value, [(i, i ^ bits) for i in range(devices)])

    def outer(value, bits=0):
        pairs = [(i ^ bits, (i - 1 + 2 * (i % 2)) % devices) for i in range(devices)]
        return permute(value, pairs)

    order = list(range(0, groups, 2)) + list(range(groups - 1, 0, -2))

    def around(value, shift):
        pairs = [
            (order[k] * TEAM + j, order[(k + shift) % groups] * TEAM + j)
            for k in range(groups)
            for j in range(TEAM)
        ]
        return permute(value, pairs)

    held = [
        x,
        cot,
        boundary,
        neighbours.T,
        gauge_index.T,
        gauge_angles.reshape(-1, 128),
        near_real,
        near_imag,
        self_real,
        self_imag,
        norm_gain.reshape(-1, 128),
    ]
    x, cot, boundary, *tables = call(
        lambda *refs: load_body(len(held), *refs),
        [struct(value.shape, value.dtype) for value in held],
        held,
        [pltpu.SemaphoreType.DMA((len(held),))],
        range(len(held)),
    )
    parts = call(
        weights_body,
        [struct((2, rows, span))] * TEAM,
        [up_weight, down_weight],
        [pltpu.SemaphoreType.DMA((2 * TEAM,))],
        (0, 1),
    )
    near_part = swap(parts[1], 1)
    far_parts = [swap(parts[2], 2), swap(parts[3], 3)]
    first = jnp.concatenate([parts[0], near_part], axis=1)
    second = jnp.concatenate(far_parts, axis=1)
    steps, chunks = [(0, 0), (0, 2)], [first, second]
    forth = [first, second]
    back = [first, second]
    half = groups // 2
    for s in range(1, half):
        for which in range(2):
            forth[which] = around(forth[which], 1)
            back[which] = around(back[which], -1)
            steps += [(-s, 2 * which), (s, 2 * which)]
            chunks += [forth[which], back[which]]
    last_chunks = []
    for which in range(2):
        last_chunks += [around(forth[which][:1], 1), around(back[which][1:], -1)]

    inner_rows, outer_rows = call(border_body, [struct((border, width))] * 2, [x, boundary])
    inner_rows = swap(inner_rows, 1)
    outer_rows = outer(outer_rows)
    cot_near = swap(cot, 1)
    cot_far = swap(cot, 2)
    cot_cross = swap(cot_far, 1)

    mix, form, gain = call(
        lambda *refs: prep_body(sentinel, *refs),
        [
            struct((2, extent, columns)),
            struct((2, BLOCK, BLOCK)),
            struct((1, width), jnp.float32),
        ],
        tables,
    )
    conv, norm, edge = call(
        conv_body,
        [struct((columns, width))] * 2 + [struct((2, border, columns))],
        [x, inner_rows, outer_rows, mix, form, gain],
        [pltpu.VMEM((extent, width), jnp.bfloat16)],
    )
    norm_near = swap(norm, 1)
    norm_far = swap(norm, 2)
    norm_cross = swap(norm_far, 1)
    edge = swap(edge, 2)

    wide = struct((columns, width), jnp.float32)
    team = TEAM * columns
    tall = TEAM * rows
    ups, pre_a, back_sum, xa_last, g_last = call(
        lambda *refs: early_body(steps, groups, *refs),
        [
            struct((width, span)),
            struct((team // 2, span), jnp.float32),
            struct((team, span), jnp.float32),
            struct((team // 2, tall)),
            struct((team, tall)),
        ],
        [norm_near, norm, cot, cot_near, cot_far, cot_cross, *chunks],
        [
            pltpu.VMEM((team // 2, width), jnp.bfloat16),
            pltpu.VMEM((team, width), jnp.bfloat16),
            pltpu.VMEM((width, span), jnp.bfloat16),
        ],
    )
    pre_b, xb_last = call(
        lambda *refs: rest_body(groups, *refs),
        [struct((team // 2, span), jnp.float32), struct((team // 2, tall))],
        [norm_cross, norm_far, ups],
        [pltpu.VMEM((team // 2, width), jnp.bfloat16)],
    )
    ups, gate, send = call(
        lambda *refs: send_body(groups, *refs),
        [struct((width, span)), struct((team, span)), struct((2, columns, width))],
        [ups, pre_a, pre_b, back_sum, xa_last, xb_last, g_last, *last_chunks],
        [pltpu.VMEM((tall, span), jnp.bfloat16)] * 2,
        (),
        ((0, 0),),
    )
    mine, cross = call(keep_body, [wide, wide], [gate, ups])
    received = swap(send, 1)
    crossing = call(join_body, struct((columns, width)), [cross, received])
    crossed = swap(crossing, 2)
    own_rows, other_rows = call(
        edge_body,
        [struct((border, width))] * 2,
        [mine, cross, received, conv, cot, norm_far, gain, mix, edge, form],
    )
    own_rows = outer(own_rows)
    other_rows = outer(other_rows, 2)
    grads, inner_back = call(
        grad_body,
        [struct((columns, width)), struct((border, width))],
        [mine, received, crossed, conv, cot, gain, mix, form],
    )
    inner_back = swap(inner_back, 1)
    local = call(own_body, wide, [grads, mix, form])
    out = pl.pallas_call(
        last_body, out_shape=jax.ShapeDtypeStruct((columns, width), jnp.bfloat16)
    )(*(pltpu.with_memory_space_constraint(v, pltpu.VMEM) for v in (local, inner_back, own_rows, other_rows, boundary)))
    return out[None]


def solution(mesh):
    in_specs = (
        P("groups", "patch", "level"),
        P("groups", "patch", "level"),
        P("patch", None),
        P("patch", None),
        P("patch", None),
        P(),
        P(),
        P("patch", "level"),
        P("patch", "level"),
        P(),
        P(),
        P(),
        P(),
    )
    out_specs = P("groups", "patch", "level")

    return jax.shard_map(
        per_device, mesh=mesh, in_specs=in_specs, out_specs=out_specs, check_vma=False
    )
```

```python
import jax
import jax.numpy as jnp
from jax import lax
from jax.experimental import pallas as pl
from jax.experimental.pallas import tpu as pltpu
from jax.sharding import PartitionSpec as P


CH = 64


def padded(shard, sides, width):
    for axis, dim in sides:
        devices, length = (lax.axis_size(axis), shard.shape[dim])
        up = [(i, (i + 1) % devices) for i in range(devices)]
        down = [(j, i) for i, j in up]
        last = lax.slice_in_dim(shard, length - width, length, axis=dim)
        leading = lax.slice_in_dim(shard, 0, width, axis=dim)
        before = lax.ppermute(last, axis, up)
        after = lax.ppermute(leading, axis, down)
        shard = jnp.concatenate([before, shard, after], axis=dim)
    return shard


def real_form(real_part, imag_part):
    upper = jnp.concatenate([real_part, imag_part], axis=1)
    lower = jnp.concatenate([-imag_part, real_part], axis=1)
    return jnp.concatenate([upper, lower], axis=0)


def rotate_quarter(values, channels):
    shape = values.shape
    split = values.reshape(shape[:-1] + (shape[-1] // channels, 2, channels // 2))
    turned = jnp.stack([-split[..., 1, :], split[..., 0, :]], axis=-2)
    return turned.reshape(shape)


def per_level(values, form, channels):
    shape = values.shape
    split = values.reshape(shape[:-1] + (shape[-1] // channels, channels))
    result = jnp.einsum("bclw,wv->bclv", split, form, preferred_element_type=jnp.float32)
    return result.reshape(shape)


def mlp_back(columns_in, grads, norm_gain, up_mat, down_mat):
    values = columns_in.astype(jnp.float32)
    root_scale = lax.rsqrt(jnp.mean(values * values, axis=-1, keepdims=True) + 1e-05)
    normed = (values * root_scale * norm_gain).astype(jnp.bfloat16)
    pre_act = jnp.einsum("brw,wh->brh", normed, up_mat, preferred_element_type=jnp.float32)
    back_hidden = jnp.einsum("brw,wh->brh", grads, down_mat, preferred_element_type=jnp.float32)
    sigmoid_pre = jax.nn.sigmoid(pre_act)
    grad_pre = (back_hidden * sigmoid_pre * (1.0 + pre_act * (1.0 - sigmoid_pre))).astype(
        jnp.bfloat16
    )
    grad_normed = jnp.einsum("brh,wh->brw", grad_pre, up_mat, preferred_element_type=jnp.float32)
    mixed_mean = jnp.mean(norm_gain * grad_normed * values, axis=-1, keepdims=True)
    return (
        root_scale * norm_gain * grad_normed
        - values * root_scale * root_scale * root_scale * mixed_mean
    )


def general(
    layer_input,
    cotangent,
    neighbours,
    boundary,
    gauge_index,
    gauge_angles,
    norm_gain,
    up_weight,
    down_weight,
    self_real,
    self_imag,
    near_real,
    near_imag,
):
    samples, columns, width = layer_input.shape
    border = boundary.shape[1] // 2
    low_rows = boundary[0, :border]
    high_rows = boundary[0, border:]
    sent = jnp.stack([layer_input[:, low_rows], layer_input[:, high_rows]])
    cycle = padded(sent, (("patch", 0),), 1)
    extended = jnp.concatenate(
        [layer_input, cycle[0], cycle[3], jnp.zeros((samples, 1, width), jnp.bfloat16)], axis=1
    )
    sentinel = columns + 2 * border
    present = (neighbours < sentinel).astype(jnp.float32)
    edge_weight = present / jnp.sum(present, axis=1, keepdims=True)
    phase = gauge_angles[gauge_index]
    cosine = jnp.cos(phase)
    sine = jnp.sin(phase)
    near_form = real_form(near_real, near_imag)
    self_form = real_form(self_real, self_imag)
    gathered = jnp.zeros((samples, columns, width), jnp.float32)
    for entry in range(6):
        near = extended[:, neighbours[:, entry]].astype(jnp.float32)
        turned = rotate_quarter(near, CH)
        gathered = (
            gathered
            + (
                cosine[None, :, entry : entry + 1] * near
                + sine[None, :, entry : entry + 1] * turned
            )
            * edge_weight[None, :, entry : entry + 1]
        )
    gathered = gathered.astype(jnp.bfloat16)
    convolved = per_level(gathered, near_form, CH) + per_level(layer_input, self_form, CH)
    conv_out = (layer_input.astype(jnp.float32) + convolved).astype(jnp.bfloat16)
    conv_out = lax.optimization_barrier(conv_out)
    up_part, down_part = (
        lax.all_gather(up_weight, "patch", axis=0, tiled=True),
        lax.all_gather(down_weight, "patch", axis=0, tiled=True),
    )
    up_whole, down_whole = (
        lax.all_gather(up_part, "level", axis=1, tiled=True),
        lax.all_gather(down_part, "level", axis=1, tiled=True),
    )
    half_cols, half_grads = (
        lax.all_to_all(conv_out, "level", split_axis=1, concat_axis=2, tiled=True),
        lax.all_to_all(cotangent, "level", split_axis=1, concat_axis=2, tiled=True),
    )
    terms = mlp_back(half_cols, half_grads, norm_gain, up_whole, down_whole)
    column_grad = (half_grads.astype(jnp.float32) + terms).astype(jnp.bfloat16)
    grad_conv = lax.all_to_all(column_grad, "level", split_axis=2, concat_axis=1, tiled=True)
    grad_conv = lax.optimization_barrier(grad_conv)
    pulled = per_level(grad_conv, near_form.T, CH)
    own_back = per_level(grad_conv, self_form.T, CH)
    pulled_turn = rotate_quarter(pulled, CH)
    spread = jnp.zeros((samples, sentinel + 1, width), jnp.float32)
    for entry in range(6):
        edges = (
            cosine[None, :, entry : entry + 1] * pulled
            - sine[None, :, entry : entry + 1] * pulled_turn
        ) * edge_weight[None, :, entry : entry + 1]
        spread = spread.at[:, neighbours[:, entry]].add(edges)
    back_sent = jnp.stack(
        [spread[:, columns : columns + border], spread[:, columns + border : sentinel]]
    )
    back_cycle = padded(back_sent.astype(jnp.bfloat16), (("patch", 0),), 1).astype(back_sent.dtype)
    local_terms = (
        spread[:, :columns].at[:, low_rows].add(back_cycle[0]).at[:, high_rows].add(back_cycle[3])
    )
    return (grad_conv.astype(jnp.float32) + own_back + local_terms).astype(jnp.bfloat16)


BLOCK = 256
TEAM = 4


def iota(shape, dim):
    return lax.broadcasted_iota(jnp.int32, shape, dim)


def mm(a, b, dims=((1,), (0,))):
    return lax.dot_general(a, b, (dims, ((), ())), preferred_element_type=jnp.float32)


def turn(values):
    width = values.shape[1]
    half = CH // 2
    later = pltpu.roll(values, width - half, 1)
    earlier = pltpu.roll(values, half, 1)
    return jnp.where(iota(values.shape, 1) % CH < half, -later, earlier)


def call(body, outs, args, scratch=(), raw=(), aliases=()):
    vmem = pl.BlockSpec(memory_space=pltpu.VMEM)
    args = [
        pltpu.with_memory_space_constraint(value, pltpu.HBM if i in raw else pltpu.VMEM)
        for i, value in enumerate(args)
    ]
    specs = [pl.BlockSpec(memory_space=pl.ANY) if i in raw else vmem for i in range(len(args))]
    return pl.pallas_call(
        body,
        out_shape=outs,
        in_specs=specs,
        out_specs=jax.tree.map(lambda _: vmem, outs),
        scratch_shapes=scratch,
        input_output_aliases=dict(aliases),
        compiler_params=pltpu.CompilerParams(vmem_limit_bytes=24 << 20),
    )(*args)


def struct(shape, dtype=jnp.bfloat16):
    return pltpu.VMEM(shape, dtype)


def picked(bound_ref, columns):
    count = bound_ref.shape[1]
    return (iota((columns, count), 0) == bound_ref[...]).astype(jnp.bfloat16)


def copy_all(pairs, sem):
    copies = [pltpu.make_async_copy(src, dst, sem.at[i]) for i, (src, dst) in enumerate(pairs)]
    for one in copies:
        one.start()
    for one in copies:
        one.wait()


def weights_body(up_ref, down_ref, *refs):
    *parts, sem = refs
    mine = lax.axis_index("patch") % TEAM
    span = parts[0].shape[2]
    pairs = []
    for k in range(TEAM):
        at = pl.multiple_of((mine ^ k) * span, 128)
        for which, ref in enumerate((up_ref, down_ref)):
            pairs.append((ref.at[:, pl.ds(at, span)], parts[k].at[which]))
    copy_all(pairs, sem)


def load_body(count, *refs):
    copy_all(list(zip(refs[:count], refs[count : 2 * count])), refs[-1])


def is_even():
    return lax.axis_index("patch") % 2 == 0


def border_body(x_ref, bound_ref, inner_ref, outer_ref):
    border = inner_ref.shape[0]
    rows = mm(picked(bound_ref, x_ref.shape[0]), x_ref[...], ((0,), (0,))).astype(jnp.bfloat16)
    low, high = rows[:border], rows[border:]
    inner_ref[...] = jnp.where(is_even(), high, low)
    outer_ref[...] = jnp.where(is_even(), low, high)


def spread_form(real_ref, imag_ref):
    half = real_ref.shape[0]
    tall = (iota((BLOCK, half), 0) % half == iota((BLOCK, half), 1)).astype(jnp.bfloat16)

    def tiled(ref):
        rows = mm(tall, ref[...]).astype(jnp.bfloat16)
        return mm(rows, tall, ((1,), (1,)))

    real, imag = tiled(real_ref), tiled(imag_ref)
    row, col = iota((BLOCK, BLOCK), 0), iota((BLOCK, BLOCK), 1)
    row_real = row % CH < half
    col_real = col % CH < half
    form = jnp.where(row_real == col_real, real, jnp.where(row_real, imag, -imag))
    return jnp.where(row // CH == col // CH, form, 0.0).astype(jnp.bfloat16)


def prep_body(sentinel, near_ref, index_ref, angle_ref, nr, ni, sr, si, gains, mix_ref, form_ref, gain_ref):
    entries, columns = near_ref.shape
    table = angle_ref[...]
    index = index_ref[...]
    phases = []
    for k in range(entries):
        spot = jnp.broadcast_to(index[k : k + 1], (table.shape[0], columns))
        found = jnp.take_along_axis(table, spot % 128, axis=1)
        hit = iota(found.shape, 0) == spot // 128
        phases.append(jnp.sum(jnp.where(hit, found, 0.0), axis=0, keepdims=True))
    phase = jnp.concatenate(phases, axis=0)
    near = near_ref[...]
    present = (near < sentinel).astype(jnp.float32)
    weight = present / jnp.sum(present, axis=0, keepdims=True)
    cosine, sine = jnp.cos(phase) * weight, jnp.sin(phase) * weight
    height = mix_ref.shape[1]
    place = iota((height, columns), 0)
    mix_cos = jnp.zeros((height, columns), jnp.float32)
    mix_sin = jnp.zeros((height, columns), jnp.float32)
    for k in range(entries):
        hit = near[k : k + 1] == place
        mix_cos = mix_cos + jnp.where(hit, cosine[k : k + 1], 0.0)
        mix_sin = mix_sin + jnp.where(hit, sine[k : k + 1], 0.0)
    mix_ref[0] = mix_cos.astype(jnp.bfloat16)
    mix_ref[1] = mix_sin.astype(jnp.bfloat16)
    gain_ref[...] = jnp.concatenate([gains[r : r + 1] for r in range(gains.shape[0])], axis=1)
    form_ref[0] = spread_form(nr, ni)
    form_ref[1] = spread_form(sr, si)


def border_mix(mix_ref, columns, border, which):
    at = pl.multiple_of(columns + border * which, 16)
    return [mix_ref[i, pl.ds(at, border)] for i in range(2)]


def conv_body(x_ref, inner_ref, outer_ref, mix_ref, form_ref, gain_ref, conv_ref, norm_ref, edge_ref, scale_ref, ext):
    columns, width = x_ref.shape
    border = inner_ref.shape[0]
    odd = lax.axis_index("patch") % 2
    ext[:columns] = x_ref[...]
    ext[pl.ds(pl.multiple_of(columns + border * (1 - odd), 16), border)] = inner_ref[...]
    ext[pl.ds(pl.multiple_of(columns + border * odd, 16), border)] = outer_ref[...]
    rest = ext.shape[0] - columns - 2 * border
    if rest:
        ext[columns + 2 * border :] = jnp.zeros((rest, width), jnp.bfloat16)
    source = ext[...]
    over = ((0,), (0,))
    gathered = mm(mix_ref[0], source, over) + turn(mm(mix_ref[1], source, over))
    gathered = gathered.astype(jnp.bfloat16)
    square = jnp.zeros((columns, BLOCK), jnp.float32)
    for b in range(width // BLOCK):
        at = slice(b * BLOCK, (b + 1) * BLOCK)
        x = x_ref[:, at]
        out = x.astype(jnp.float32) + (mm(gathered[:, at], form_ref[0]) + mm(x, form_ref[1]))
        out = out.astype(jnp.bfloat16)
        conv_ref[:, at] = out
        out = out.astype(jnp.float32)
        square = square + out * out
    scale = lax.rsqrt(jnp.sum(square, axis=1, keepdims=True) / width + 1e-05)
    norm_ref[...] = (conv_ref[...].astype(jnp.float32) * scale * gain_ref[...]).astype(jnp.bfloat16)
    scale_ref[...] = jnp.broadcast_to(scale, scale_ref.shape)
    across = jnp.broadcast_to(scale, (columns, columns)).T[:1]
    for i, rows in enumerate(border_mix(mix_ref, columns, border, odd)):
        edge_ref[i] = (rows.astype(jnp.float32) * across).astype(jnp.bfloat16)


def ring_place(group, groups):
    return jnp.where(group % 2 == 0, group // 2, groups - 1 - group // 2)


def ring_group(place, groups):
    return jnp.where(place < groups // 2, 2 * place, 2 * (groups - 1 - place) + 1)


STACK = (3, 2, 1, 0)


def far_owner(groups):
    place = ring_place(lax.axis_index("patch") // TEAM, groups)
    return ring_group((place + groups // 2) % groups, groups)


def take_columns(owner, groups, pairs):
    for g in range(groups):

        @pl.when(owner == g)
        def _():
            for source, target in pairs:
                tall = target.shape[1]
                target[...] = source[:, g * tall : (g + 1) * tall]


def early_body(steps, groups, *refs):
    norms, grads, chunks = refs[:2], refs[2 : 2 + TEAM], refs[2 + TEAM : 2 + TEAM + len(steps)]
    ups, pre_ref, back_ref, x_last, g_last, xs, gs, downs = refs[2 + TEAM + len(steps) :]
    columns = norms[0].shape[0]
    span = ups.shape[1]
    me = lax.axis_index("patch")
    group, member = me // TEAM, me % TEAM
    place = ring_place(group, groups)
    for k in range(2):
        xs[k * columns : (k + 1) * columns] = norms[k][...]
    for k, m in enumerate(STACK):
        gs[k * columns : (k + 1) * columns] = grads[m][...]
    for (shift, first), ref in zip(steps, chunks):
        rows = ref.shape[1] // 2
        owner = ring_group((place + shift + groups) % groups, groups)
        for half in range(2):
            at = pl.multiple_of((owner * TEAM + (member ^ (first + half))) * rows, 16)
            part = slice(half * rows, (half + 1) * rows)
            ups[pl.ds(at, rows)] = ref[0, part]
            downs[pl.ds(at, rows)] = ref[1, part]
    owner = far_owner(groups)
    tall = TEAM * rows
    blank = jnp.zeros((tall, span), jnp.bfloat16)
    at = pl.multiple_of(owner * tall, 16)
    ups[pl.ds(at, tall)] = blank
    downs[pl.ds(at, tall)] = blank
    take_columns(owner, groups, ((xs, x_last), (gs, g_last)))
    pre_ref[...] = mm(xs[...], ups[...])
    back_ref[...] = mm(gs[...], downs[...])


def rest_body(groups, cross_ref, far_ref, ups, pre_ref, x_last, xs):
    columns = cross_ref.shape[0]
    xs[:columns] = cross_ref[...]
    xs[columns:] = far_ref[...]
    take_columns(far_owner(groups), groups, ((xs, x_last),))
    pre_ref[...] = mm(xs[...], ups[...])


def gated(pre_act, back):
    gate = jax.nn.sigmoid(pre_act)
    return (back * gate * (1.0 + pre_act * (1.0 - gate))).astype(jnp.bfloat16)


def send_body(groups, ups_in, pre_ref, back_ref, x_last, g_last, *refs):
    parts, (ups, up, down, gate_ref, send_ref) = refs[:4], refs[4:]
    member = lax.axis_index("patch") % TEAM
    rows = parts[0].shape[1] // 2
    for k in range(2):
        for half in range(2):
            at = pl.multiple_of((member ^ (2 * k + half)) * rows, 16)
            part = slice(half * rows, (half + 1) * rows)
            up[pl.ds(at, rows)] = parts[2 * k][0, part]
            down[pl.ds(at, rows)] = parts[2 * k + 1][0, part]
    tall = up.shape[0]
    ups[pl.ds(pl.multiple_of(far_owner(groups) * tall, 16), tall)] = up[...]
    columns = send_ref.shape[0]
    two = slice(0, 2 * columns)
    pre_act = pre_ref[...] + mm(x_last[...], up[...])
    grad_pre = gated(pre_act, back_ref[two] + mm(g_last[two], down[...]))
    gate_ref[...] = grad_pre[columns:]
    send_ref[...] = mm(grad_pre[:columns], ups[...], ((1,), (1,))).astype(jnp.bfloat16)


def cross_body(gate_ref, ups, cross_ref):
    cross_ref[...] = mm(gate_ref[...], ups[...], ((1,), (1,)))


def keep_body(ups, up, down, pre_ref, back_ref, x_last, g_last, mine_ref, send_ref):
    columns = mine_ref.shape[0]
    two = slice(2 * columns, 4 * columns)
    pre_act = pre_ref[...] + mm(x_last[...], up[...])
    grad_pre = gated(pre_act, back_ref[two] + mm(g_last[two], down[...]))
    rows = mm(grad_pre, ups[...], ((1,), (1,)))
    send_ref[...] = rows[:columns].astype(jnp.bfloat16)
    mine_ref[...] = rows[columns:]


def shifted_back(mix, form, grads):
    spread = mm(mix[0], grads) - turn(mm(mix[1], grads))
    spread = spread.astype(jnp.bfloat16)
    width = grads.shape[1]
    return [
        mm(spread[:, b * BLOCK : (b + 1) * BLOCK], form, ((1,), (1,)))
        for b in range(width // BLOCK)
    ]


def join_body(cross_ref, part_ref, out_ref):
    out_ref[...] = (cross_ref[...] + part_ref[...].astype(jnp.float32)).astype(jnp.bfloat16)


def column_grad(grad_normed, values, scale, gain):
    scaled = gain * grad_normed
    mixed = jnp.sum(scaled * values, axis=1, keepdims=True) / values.shape[1]
    return scale * scaled - values * (scale * scale * scale * mixed)


def put_back(target, mix, form, grads):
    for b, rows in enumerate(shifted_back(mix, form, grads)):
        target[:, b * BLOCK : (b + 1) * BLOCK] = rows.astype(jnp.bfloat16)


def other_body(cross_ref, part_ref, far_ref, gain_ref, edge_ref, form_ref, out_ref):
    scaled_values = far_ref[...].astype(jnp.float32) / gain_ref[...]
    share = cross_ref[...] + part_ref[...].astype(jnp.float32)
    grads = column_grad(share, scaled_values, 1.0, gain_ref[...]).astype(jnp.bfloat16)
    put_back(out_ref, [edge_ref[i] for i in range(2)], form_ref[0], grads)


def edge_body(mine_ref, part_ref, conv_ref, cot_ref, scale_ref, gain_ref, mix_ref, form_ref, base_ref, out_ref):
    values = conv_ref[...].astype(jnp.float32)
    share = mine_ref[...] + part_ref[...].astype(jnp.float32)
    grads = column_grad(share, values, scale_ref[:, :1], gain_ref[...])
    grads = cot_ref[...].astype(jnp.float32) + grads
    base_ref[...] = grads
    odd = lax.axis_index("patch") % 2
    mix = border_mix(mix_ref, conv_ref.shape[0], out_ref.shape[0], odd)
    put_back(out_ref, mix, form_ref[0], grads.astype(jnp.bfloat16))


def grad_body(base_ref, cross_ref, conv_ref, scale_ref, gain_ref, mix_ref, form_ref, grad_ref, inner_ref):
    values = conv_ref[...].astype(jnp.float32)
    share = cross_ref[...].astype(jnp.float32)
    grads = column_grad(share, values, scale_ref[:, :1], gain_ref[...])
    grads = (base_ref[...] + grads).astype(jnp.bfloat16)
    grad_ref[...] = grads
    odd = lax.axis_index("patch") % 2
    mix = border_mix(mix_ref, conv_ref.shape[0], inner_ref.shape[0], 1 - odd)
    put_back(inner_ref, mix, form_ref[0], grads)


def parity_rows(bound_ref, columns, border):
    chosen = picked(bound_ref, columns).astype(jnp.float32)
    low, high = chosen[:, :border], chosen[:, border:]
    inner = jnp.where(is_even(), high, low).astype(jnp.bfloat16)
    outer = jnp.where(is_even(), low, high).astype(jnp.bfloat16)
    return inner, outer


def own_body(grad_ref, mix_ref, form_ref, local_ref):
    columns, _ = grad_ref.shape
    grads = grad_ref[...]
    mix = [mix_ref[i, :columns] for i in range(2)]
    for b, rows in enumerate(shifted_back(mix, form_ref[0], grads)):
        at = slice(b * BLOCK, (b + 1) * BLOCK)
        own = grads[:, at]
        rows = rows + mm(own, form_ref[1], ((1,), (1,)))
        local_ref[:, at] = own.astype(jnp.float32) + rows


def last_body(local_ref, inner_ref, outer_ref, other_ref, bound_ref, out_ref, held, sem):
    columns, width = local_ref.shape
    inner, outer = parity_rows(bound_ref, columns, inner_ref.shape[0])
    pick = jnp.concatenate([inner, outer, outer], axis=1)
    copies = []
    for b in range(width // BLOCK // 2):
        at = slice(2 * b * BLOCK, 2 * (b + 1) * BLOCK)
        rows = jnp.concatenate([inner_ref[:, at], outer_ref[:, at], other_ref[:, at]], axis=0)
        held[:, at] = (local_ref[:, at] + mm(pick, rows)).astype(jnp.bfloat16)
        copies.append(pltpu.make_async_copy(held.at[:, at], out_ref.at[:, at], sem.at[b]))
        copies[-1].start()
    for one in copies:
        one.wait()


def per_device(
    layer_input,
    cotangent,
    neighbours,
    boundary,
    gauge_index,
    gauge_angles,
    norm_gain,
    up_weight,
    down_weight,
    self_real,
    self_imag,
    near_real,
    near_imag,
):
    samples, columns, width = layer_input.shape
    devices = lax.axis_size("patch")
    rows, hidden = up_weight.shape
    border = boundary.shape[1] // 2
    span = hidden // TEAM
    fits = (
        lax.axis_size("level") == 1
        and samples == 1
        and devices % (2 * TEAM) == 0
        and width % (2 * BLOCK) == 0
        and hidden % (TEAM * 128) == 0
        and rows % 16 == 0
        and border % 16 == 0
        and 2 * border <= columns
        and width * span <= 1 << 20
        and gauge_angles.shape[0] % 128 == 0
        and columns == 128
    )
    if not fits:
        return general(
            layer_input,
            cotangent,
            neighbours,
            boundary,
            gauge_index,
            gauge_angles,
            norm_gain,
            up_weight,
            down_weight,
            self_real,
            self_imag,
            near_real,
            near_imag,
        )
    groups = devices // TEAM
    sentinel = columns + 2 * border
    extent = -(-sentinel // 128) * 128
    x = layer_input[0]
    cot = cotangent[0]

    def permute(value, pairs):
        return lax.ppermute(value, "patch", pairs)

    def swap(value, bits):
        return permute(value, [(i, i ^ bits) for i in range(devices)])

    def outer(value, bits=0):
        pairs = [(i ^ bits, (i - 1 + 2 * (i % 2)) % devices) for i in range(devices)]
        return permute(value, pairs)

    order = list(range(0, groups, 2)) + list(range(groups - 1, 0, -2))

    def around(value, shift):
        pairs = [
            (order[k] * TEAM + j, order[(k + shift) % groups] * TEAM + j)
            for k in range(groups)
            for j in range(TEAM)
        ]
        return permute(value, pairs)

    held = [
        x,
        cot,
        boundary,
        neighbours.T,
        gauge_index.T,
        gauge_angles.reshape(-1, 128),
        near_real,
        near_imag,
        self_real,
        self_imag,
        norm_gain.reshape(-1, 128),
    ]
    x, cot, boundary, *tables = call(
        lambda *refs: load_body(len(held), *refs),
        [struct(value.shape, value.dtype) for value in held],
        held,
        [pltpu.SemaphoreType.DMA((len(held),))],
        range(len(held)),
    )
    parts = call(
        weights_body,
        [struct((2, rows, span))] * TEAM,
        [up_weight, down_weight],
        [pltpu.SemaphoreType.DMA((2 * TEAM,))],
        (0, 1),
    )
    near_part = swap(parts[1], 1)
    far_parts = [swap(parts[2], 2), swap(parts[3], 3)]
    first = jnp.concatenate([parts[0], near_part], axis=1)
    second = jnp.concatenate(far_parts, axis=1)
    steps, chunks = [(0, 0), (0, 2)], [first, second]
    forth = [first, second]
    back = [first, second]
    half = groups // 2
    for s in range(1, half):
        for which in range(2):
            forth[which] = around(forth[which], 1)
            back[which] = around(back[which], -1)
            steps += [(-s, 2 * which), (s, 2 * which)]
            chunks += [forth[which], back[which]]
    last_chunks = []
    for which in range(2):
        last_chunks += [around(forth[which][:1], 1), around(back[which][1:], -1)]

    inner_rows, outer_rows = call(border_body, [struct((border, width))] * 2, [x, boundary])
    inner_rows = swap(inner_rows, 1)
    outer_rows = outer(outer_rows)
    cot_near = swap(cot, 1)
    cot_far = swap(cot, 2)
    cot_cross = swap(cot_far, 1)

    mix, form, gain = call(
        lambda *refs: prep_body(sentinel, *refs),
        [
            struct((2, extent, columns)),
            struct((2, BLOCK, BLOCK)),
            struct((1, width), jnp.float32),
        ],
        tables,
    )
    conv, norm, edge, scale = call(
        conv_body,
        [
            *[struct((columns, width))] * 2,
            struct((2, border, columns)),
            struct((columns, 128), jnp.float32),
        ],
        [x, inner_rows, outer_rows, mix, form, gain],
        [pltpu.VMEM((extent, width), jnp.bfloat16)],
    )
    norm_near = swap(norm, 1)
    norm_far = swap(norm, 2)
    norm_cross = swap(norm_far, 1)
    edge = swap(edge, 2)

    wide = struct((columns, width), jnp.float32)
    team = TEAM * columns
    tall = TEAM * rows
    ups, pre_a, back_sum, xa_last, g_last = call(
        lambda *refs: early_body(steps, groups, *refs),
        [
            struct((width, span)),
            struct((team // 2, span), jnp.float32),
            struct((team, span), jnp.float32),
            struct((team // 2, tall)),
            struct((team, tall)),
        ],
        [norm_near, norm, cot, cot_near, cot_far, cot_cross, *chunks],
        [
            pltpu.VMEM((team // 2, width), jnp.bfloat16),
            pltpu.VMEM((team, width), jnp.bfloat16),
            pltpu.VMEM((width, span), jnp.bfloat16),
        ],
    )
    pre_b, xb_last = call(
        lambda *refs: rest_body(groups, *refs),
        [struct((team // 2, span), jnp.float32), struct((team // 2, tall))],
        [norm_cross, norm_far, ups],
        [pltpu.VMEM((team // 2, width), jnp.bfloat16)],
    )
    ups, up_last, down_last, gate, send_cross = call(
        lambda *refs: send_body(groups, *refs),
        [
            struct((width, span)),
            *[struct((tall, span))] * 2,
            struct((columns, span)),
            struct((columns, width)),
        ],
        [ups, pre_b, back_sum, xb_last, g_last, *last_chunks],
        (),
        (),
        ((0, 0),),
    )
    received_cross = swap(send_cross, 1)
    cross = call(cross_body, wide, [gate, ups])
    crossing = call(join_body, struct((columns, width)), [cross, received_cross])
    crossed = swap(crossing, 2)
    mine, send = call(
        keep_body,
        [wide, struct((columns, width))],
        [ups, up_last, down_last, pre_a, back_sum, xa_last, g_last],
    )
    received = swap(send, 1)
    other_rows = call(
        other_body, struct((border, width)), [cross, received_cross, norm_far, gain, edge, form]
    )
    other_rows = outer(other_rows, 2)
    base, own_rows = call(
        edge_body,
        [wide, struct((border, width))],
        [mine, received, conv, cot, scale, gain, mix, form],
    )
    own_rows = outer(own_rows)
    grads, inner_back = call(
        grad_body,
        [struct((columns, width)), struct((border, width))],
        [base, crossed, conv, scale, gain, mix, form],
    )
    inner_back = swap(inner_back, 1)
    local = call(own_body, wide, [grads, mix, form])
    pieces = width // BLOCK // 2
    out = pl.pallas_call(
        last_body,
        out_shape=jax.ShapeDtypeStruct((columns, width), jnp.bfloat16),
        out_specs=pl.BlockSpec(memory_space=pl.ANY),
        scratch_shapes=[
            pltpu.VMEM((columns, width), jnp.bfloat16),
            pltpu.SemaphoreType.DMA((pieces,)),
        ],
    )(
        *(
            pltpu.with_memory_space_constraint(value, pltpu.VMEM)
            for value in (local, inner_back, own_rows, other_rows, boundary)
        )
    )
    return out[None]


def solution(mesh):
    in_specs = (
        P("groups", "patch", "level"),
        P("groups", "patch", "level"),
        P("patch", None),
        P("patch", None),
        P("patch", None),
        P(),
        P(),
        P("patch", "level"),
        P("patch", "level"),
        P(),
        P(),
        P(),
        P(),
    )
    out_specs = P("groups", "patch", "level")

    return jax.shard_map(
        per_device, mesh=mesh, in_specs=in_specs, out_specs=out_specs, check_vma=False
    )
```

```python
import jax
import jax.numpy as jnp
from jax import lax
from jax.experimental import pallas as pl
from jax.experimental.pallas import tpu as pltpu
from jax.sharding import PartitionSpec as P


CH = 64


def padded(shard, sides, width):
    for axis, dim in sides:
        devices, length = (lax.axis_size(axis), shard.shape[dim])
        up = [(i, (i + 1) % devices) for i in range(devices)]
        down = [(j, i) for i, j in up]
        last = lax.slice_in_dim(shard, length - width, length, axis=dim)
        leading = lax.slice_in_dim(shard, 0, width, axis=dim)
        before = lax.ppermute(last, axis, up)
        after = lax.ppermute(leading, axis, down)
        shard = jnp.concatenate([before, shard, after], axis=dim)
    return shard


def real_form(real_part, imag_part):
    upper = jnp.concatenate([real_part, imag_part], axis=1)
    lower = jnp.concatenate([-imag_part, real_part], axis=1)
    return jnp.concatenate([upper, lower], axis=0)


def rotate_quarter(values, channels):
    shape = values.shape
    split = values.reshape(shape[:-1] + (shape[-1] // channels, 2, channels // 2))
    turned = jnp.stack([-split[..., 1, :], split[..., 0, :]], axis=-2)
    return turned.reshape(shape)


def per_level(values, form, channels):
    shape = values.shape
    split = values.reshape(shape[:-1] + (shape[-1] // channels, channels))
    result = jnp.einsum("bclw,wv->bclv", split, form, preferred_element_type=jnp.float32)
    return result.reshape(shape)


def mlp_back(columns_in, grads, norm_gain, up_mat, down_mat):
    values = columns_in.astype(jnp.float32)
    root_scale = lax.rsqrt(jnp.mean(values * values, axis=-1, keepdims=True) + 1e-05)
    normed = (values * root_scale * norm_gain).astype(jnp.bfloat16)
    pre_act = jnp.einsum("brw,wh->brh", normed, up_mat, preferred_element_type=jnp.float32)
    back_hidden = jnp.einsum("brw,wh->brh", grads, down_mat, preferred_element_type=jnp.float32)
    sigmoid_pre = jax.nn.sigmoid(pre_act)
    grad_pre = (back_hidden * sigmoid_pre * (1.0 + pre_act * (1.0 - sigmoid_pre))).astype(
        jnp.bfloat16
    )
    grad_normed = jnp.einsum("brh,wh->brw", grad_pre, up_mat, preferred_element_type=jnp.float32)
    mixed_mean = jnp.mean(norm_gain * grad_normed * values, axis=-1, keepdims=True)
    return (
        root_scale * norm_gain * grad_normed
        - values * root_scale * root_scale * root_scale * mixed_mean
    )


def general(
    layer_input,
    cotangent,
    neighbours,
    boundary,
    gauge_index,
    gauge_angles,
    norm_gain,
    up_weight,
    down_weight,
    self_real,
    self_imag,
    near_real,
    near_imag,
):
    samples, columns, width = layer_input.shape
    border = boundary.shape[1] // 2
    low_rows = boundary[0, :border]
    high_rows = boundary[0, border:]
    sent = jnp.stack([layer_input[:, low_rows], layer_input[:, high_rows]])
    cycle = padded(sent, (("patch", 0),), 1)
    extended = jnp.concatenate(
        [layer_input, cycle[0], cycle[3], jnp.zeros((samples, 1, width), jnp.bfloat16)], axis=1
    )
    sentinel = columns + 2 * border
    present = (neighbours < sentinel).astype(jnp.float32)
    edge_weight = present / jnp.sum(present, axis=1, keepdims=True)
    phase = gauge_angles[gauge_index]
    cosine = jnp.cos(phase)
    sine = jnp.sin(phase)
    near_form = real_form(near_real, near_imag)
    self_form = real_form(self_real, self_imag)
    gathered = jnp.zeros((samples, columns, width), jnp.float32)
    for entry in range(6):
        near = extended[:, neighbours[:, entry]].astype(jnp.float32)
        turned = rotate_quarter(near, CH)
        gathered = (
            gathered
            + (
                cosine[None, :, entry : entry + 1] * near
                + sine[None, :, entry : entry + 1] * turned
            )
            * edge_weight[None, :, entry : entry + 1]
        )
    gathered = gathered.astype(jnp.bfloat16)
    convolved = per_level(gathered, near_form, CH) + per_level(layer_input, self_form, CH)
    conv_out = (layer_input.astype(jnp.float32) + convolved).astype(jnp.bfloat16)
    conv_out = lax.optimization_barrier(conv_out)
    up_part, down_part = (
        lax.all_gather(up_weight, "patch", axis=0, tiled=True),
        lax.all_gather(down_weight, "patch", axis=0, tiled=True),
    )
    up_whole, down_whole = (
        lax.all_gather(up_part, "level", axis=1, tiled=True),
        lax.all_gather(down_part, "level", axis=1, tiled=True),
    )
    half_cols, half_grads = (
        lax.all_to_all(conv_out, "level", split_axis=1, concat_axis=2, tiled=True),
        lax.all_to_all(cotangent, "level", split_axis=1, concat_axis=2, tiled=True),
    )
    terms = mlp_back(half_cols, half_grads, norm_gain, up_whole, down_whole)
    column_grad = (half_grads.astype(jnp.float32) + terms).astype(jnp.bfloat16)
    grad_conv = lax.all_to_all(column_grad, "level", split_axis=2, concat_axis=1, tiled=True)
    grad_conv = lax.optimization_barrier(grad_conv)
    pulled = per_level(grad_conv, near_form.T, CH)
    own_back = per_level(grad_conv, self_form.T, CH)
    pulled_turn = rotate_quarter(pulled, CH)
    spread = jnp.zeros((samples, sentinel + 1, width), jnp.float32)
    for entry in range(6):
        edges = (
            cosine[None, :, entry : entry + 1] * pulled
            - sine[None, :, entry : entry + 1] * pulled_turn
        ) * edge_weight[None, :, entry : entry + 1]
        spread = spread.at[:, neighbours[:, entry]].add(edges)
    back_sent = jnp.stack(
        [spread[:, columns : columns + border], spread[:, columns + border : sentinel]]
    )
    back_cycle = padded(back_sent.astype(jnp.bfloat16), (("patch", 0),), 1).astype(back_sent.dtype)
    local_terms = (
        spread[:, :columns].at[:, low_rows].add(back_cycle[0]).at[:, high_rows].add(back_cycle[3])
    )
    return (grad_conv.astype(jnp.float32) + own_back + local_terms).astype(jnp.bfloat16)


BLOCK = 256
TEAM = 4


def iota(shape, dim):
    return lax.broadcasted_iota(jnp.int32, shape, dim)


def mm(a, b, dims=((1,), (0,))):
    return lax.dot_general(a, b, (dims, ((), ())), preferred_element_type=jnp.float32)


def turn(values):
    width = values.shape[1]
    half = CH // 2
    later = pltpu.roll(values, width - half, 1)
    earlier = pltpu.roll(values, half, 1)
    return jnp.where(iota(values.shape, 1) % CH < half, -later, earlier)


def stacked(values):
    width = values.shape[1]
    return jnp.concatenate([values[:, at : at + BLOCK] for at in range(0, width, BLOCK)], axis=0)


def unstacked(values, rows):
    count = values.shape[0]
    return jnp.concatenate([values[at : at + rows] for at in range(0, count, rows)], axis=1)


def call(body, outs, args, scratch=(), raw=(), aliases=()):
    vmem = pl.BlockSpec(memory_space=pltpu.VMEM)
    args = [
        pltpu.with_memory_space_constraint(value, pltpu.HBM if i in raw else pltpu.VMEM)
        for i, value in enumerate(args)
    ]
    specs = [pl.BlockSpec(memory_space=pl.ANY) if i in raw else vmem for i in range(len(args))]
    return pl.pallas_call(
        body,
        out_shape=outs,
        in_specs=specs,
        out_specs=jax.tree.map(lambda _: vmem, outs),
        scratch_shapes=scratch,
        input_output_aliases=dict(aliases),
        compiler_params=pltpu.CompilerParams(vmem_limit_bytes=24 << 20),
    )(*args)


def struct(shape, dtype=jnp.bfloat16):
    return pltpu.VMEM(shape, dtype)


def picked(bound_ref, columns):
    count = bound_ref.shape[1]
    return (iota((columns, count), 0) == bound_ref[...]).astype(jnp.bfloat16)


def copy_all(pairs, sem):
    copies = [pltpu.make_async_copy(src, dst, sem.at[i]) for i, (src, dst) in enumerate(pairs)]
    for one in copies:
        one.start()
    for one in copies:
        one.wait()


def weights_body(up_ref, down_ref, *refs):
    *parts, sem = refs
    mine = lax.axis_index("patch") % TEAM
    span = parts[0].shape[2]
    pairs = []
    for k in range(TEAM):
        at = pl.multiple_of((mine ^ k) * span, 128)
        for which, ref in enumerate((up_ref, down_ref)):
            pairs.append((ref.at[:, pl.ds(at, span)], parts[k].at[which]))
    copy_all(pairs, sem)


def load_body(count, *refs):
    copy_all(list(zip(refs[:count], refs[count : 2 * count])), refs[-1])


def is_even():
    return lax.axis_index("patch") % 2 == 0


def border_body(x_ref, bound_ref, inner_ref, outer_ref):
    border = inner_ref.shape[0]
    rows = mm(picked(bound_ref, x_ref.shape[0]), x_ref[...], ((0,), (0,))).astype(jnp.bfloat16)
    low, high = rows[:border], rows[border:]
    inner_ref[...] = jnp.where(is_even(), high, low)
    outer_ref[...] = jnp.where(is_even(), low, high)


def spread_form(real_ref, imag_ref):
    half = real_ref.shape[0]
    tall = (iota((BLOCK, half), 0) % half == iota((BLOCK, half), 1)).astype(jnp.bfloat16)

    def tiled(ref):
        rows = mm(tall, ref[...]).astype(jnp.bfloat16)
        return mm(rows, tall, ((1,), (1,)))

    real, imag = tiled(real_ref), tiled(imag_ref)
    row, col = iota((BLOCK, BLOCK), 0), iota((BLOCK, BLOCK), 1)
    row_real = row % CH < half
    col_real = col % CH < half
    form = jnp.where(row_real == col_real, real, jnp.where(row_real, imag, -imag))
    return jnp.where(row // CH == col // CH, form, 0.0).astype(jnp.bfloat16)


def prep_body(sentinel, near_ref, index_ref, angle_ref, nr, ni, sr, si, gains, mix_ref, form_ref, gain_ref):
    entries, columns = near_ref.shape
    table = angle_ref[...]
    index = index_ref[...]
    phases = []
    for k in range(entries):
        spot = jnp.broadcast_to(index[k : k + 1], (table.shape[0], columns))
        found = jnp.take_along_axis(table, spot % 128, axis=1)
        hit = iota(found.shape, 0) == spot // 128
        phases.append(jnp.sum(jnp.where(hit, found, 0.0), axis=0, keepdims=True))
    phase = jnp.concatenate(phases, axis=0)
    near = near_ref[...]
    present = (near < sentinel).astype(jnp.float32)
    weight = present / jnp.sum(present, axis=0, keepdims=True)
    cosine, sine = jnp.cos(phase) * weight, jnp.sin(phase) * weight
    height = mix_ref.shape[1]
    place = iota((height, columns), 0)
    mix_cos = jnp.zeros((height, columns), jnp.float32)
    mix_sin = jnp.zeros((height, columns), jnp.float32)
    for k in range(entries):
        hit = near[k : k + 1] == place
        mix_cos = mix_cos + jnp.where(hit, cosine[k : k + 1], 0.0)
        mix_sin = mix_sin + jnp.where(hit, sine[k : k + 1], 0.0)
    mix_ref[0] = mix_cos.astype(jnp.bfloat16)
    mix_ref[1] = mix_sin.astype(jnp.bfloat16)
    gain_ref[...] = jnp.concatenate([gains[r : r + 1] for r in range(gains.shape[0])], axis=1)
    form_ref[0] = spread_form(nr, ni)
    form_ref[1] = spread_form(sr, si)


def border_mix(mix_ref, columns, border, which):
    at = pl.multiple_of(columns + border * which, 16)
    return [mix_ref[i, pl.ds(at, border)] for i in range(2)]


def conv_body(x_ref, inner_ref, outer_ref, mix_ref, form_ref, gain_ref, conv_ref, norm_ref, edge_ref, scale_ref, ext):
    columns, width = x_ref.shape
    border = inner_ref.shape[0]
    odd = lax.axis_index("patch") % 2
    ext[:columns] = x_ref[...]
    ext[pl.ds(pl.multiple_of(columns + border * (1 - odd), 16), border)] = inner_ref[...]
    ext[pl.ds(pl.multiple_of(columns + border * odd, 16), border)] = outer_ref[...]
    rest = ext.shape[0] - columns - 2 * border
    if rest:
        ext[columns + 2 * border :] = jnp.zeros((rest, width), jnp.bfloat16)
    source = ext[...]
    gathered = mm(jnp.concatenate([mix_ref[0], mix_ref[1]], axis=1), source, ((0,), (0,)))
    gathered = (gathered[:columns] + turn(gathered[columns:])).astype(jnp.bfloat16)
    x = x_ref[...]
    folded = mm(stacked(gathered), form_ref[0]) + mm(stacked(x), form_ref[1])
    out = (x.astype(jnp.float32) + unstacked(folded, columns)).astype(jnp.bfloat16)
    conv_ref[...] = out
    out = out.astype(jnp.float32)
    square = out * out
    scale = lax.rsqrt(jnp.sum(square, axis=1, keepdims=True) / width + 1e-05)
    norm_ref[...] = (conv_ref[...].astype(jnp.float32) * scale * gain_ref[...]).astype(jnp.bfloat16)
    scale_ref[...] = jnp.broadcast_to(scale, scale_ref.shape)
    across = jnp.broadcast_to(scale, (columns, columns)).T[:1]
    for i, rows in enumerate(border_mix(mix_ref, columns, border, odd)):
        edge_ref[i] = (rows.astype(jnp.float32) * across).astype(jnp.bfloat16)


def ring_place(group, groups):
    return jnp.where(group % 2 == 0, group // 2, groups - 1 - group // 2)


def ring_group(place, groups):
    return jnp.where(place < groups // 2, 2 * place, 2 * (groups - 1 - place) + 1)


STACK = (3, 2, 1, 0)


def far_owner(groups):
    place = ring_place(lax.axis_index("patch") // TEAM, groups)
    return ring_group((place + groups // 2) % groups, groups)


def take_columns(owner, groups, pairs):
    for g in range(groups):

        @pl.when(owner == g)
        def _():
            for source, target in pairs:
                tall = target.shape[1]
                target[...] = source[:, g * tall : (g + 1) * tall]


def early_body(steps, groups, *refs):
    norms, grads, chunks = refs[:2], refs[2 : 2 + TEAM], refs[2 + TEAM : 2 + TEAM + len(steps)]
    ups, pre_ref, back_ref, x_last, g_last, xs, gs, downs = refs[2 + TEAM + len(steps) :]
    columns = norms[0].shape[0]
    span = ups.shape[1]
    me = lax.axis_index("patch")
    group, member = me // TEAM, me % TEAM
    place = ring_place(group, groups)
    for k in range(2):
        xs[k * columns : (k + 1) * columns] = norms[k][...]
    for k, m in enumerate(STACK):
        gs[k * columns : (k + 1) * columns] = grads[m][...]
    for (shift, first), ref in zip(steps, chunks):
        rows = ref.shape[1] // 2
        owner = ring_group((place + shift + groups) % groups, groups)
        for half in range(2):
            at = pl.multiple_of((owner * TEAM + (member ^ (first + half))) * rows, 16)
            part = slice(half * rows, (half + 1) * rows)
            ups[pl.ds(at, rows)] = ref[0, part]
            downs[pl.ds(at, rows)] = ref[1, part]
    owner = far_owner(groups)
    tall = TEAM * rows
    blank = jnp.zeros((tall, span), jnp.bfloat16)
    at = pl.multiple_of(owner * tall, 16)
    ups[pl.ds(at, tall)] = blank
    downs[pl.ds(at, tall)] = blank
    take_columns(owner, groups, ((xs, x_last), (gs, g_last)))
    pre_ref[...] = mm(xs[...], ups[...])
    back_ref[...] = mm(gs[...], downs[...])


def rest_body(groups, cross_ref, far_ref, ups, pre_ref, x_last, xs):
    columns = cross_ref.shape[0]
    xs[:columns] = cross_ref[...]
    xs[columns:] = far_ref[...]
    take_columns(far_owner(groups), groups, ((xs, x_last),))
    pre_ref[...] = mm(xs[...], ups[...])


def gated(pre_act, back):
    gate = jax.nn.sigmoid(pre_act)
    return (back * gate * (1.0 + pre_act * (1.0 - gate))).astype(jnp.bfloat16)


def send_body(groups, ups_in, pre_ref, back_ref, x_last, g_last, *refs):
    parts, (ups, up, down, gate_ref, send_ref) = refs[:4], refs[4:]
    member = lax.axis_index("patch") % TEAM
    rows = parts[0].shape[1] // 2
    for k in range(2):
        for half in range(2):
            at = pl.multiple_of((member ^ (2 * k + half)) * rows, 16)
            part = slice(half * rows, (half + 1) * rows)
            up[pl.ds(at, rows)] = parts[2 * k][0, part]
            down[pl.ds(at, rows)] = parts[2 * k + 1][0, part]
    tall = up.shape[0]
    ups[pl.ds(pl.multiple_of(far_owner(groups) * tall, 16), tall)] = up[...]
    columns = send_ref.shape[0]
    two = slice(0, 2 * columns)
    pre_act = pre_ref[...] + mm(x_last[...], up[...])
    grad_pre = gated(pre_act, back_ref[two] + mm(g_last[two], down[...]))
    gate_ref[...] = grad_pre[columns:]
    send_ref[...] = mm(grad_pre[:columns], ups[...], ((1,), (1,))).astype(jnp.bfloat16)


def cross_body(gate_ref, ups, cross_ref):
    cross_ref[...] = mm(gate_ref[...], ups[...], ((1,), (1,)))


def keep_body(ups, up, down, pre_ref, back_ref, x_last, g_last, mine_ref, send_ref):
    columns = mine_ref.shape[0]
    two = slice(2 * columns, 4 * columns)
    pre_act = pre_ref[...] + mm(x_last[...], up[...])
    grad_pre = gated(pre_act, back_ref[two] + mm(g_last[two], down[...]))
    rows = mm(grad_pre, ups[...], ((1,), (1,)))
    send_ref[...] = rows[:columns].astype(jnp.bfloat16)
    mine_ref[...] = rows[columns:]


def shifted_back(mix, grads):
    rows = mix[0].shape[0]
    spread = mm(jnp.concatenate(mix, axis=0), grads)
    return (spread[:rows] - turn(spread[rows:])).astype(jnp.bfloat16)


def join_body(cross_ref, part_ref, out_ref):
    out_ref[...] = (cross_ref[...] + part_ref[...].astype(jnp.float32)).astype(jnp.bfloat16)


def column_grad(grad_normed, values, scale, gain):
    scaled = gain * grad_normed
    mixed = jnp.sum(scaled * values, axis=1, keepdims=True) / values.shape[1]
    return scale * scaled - values * (scale * scale * scale * mixed)


def put_back(target, mix, form, grads):
    rows = mm(stacked(shifted_back(mix, grads)), form, ((1,), (1,))).astype(jnp.bfloat16)
    target[...] = unstacked(rows, target.shape[0])


def other_body(cross_ref, part_ref, far_ref, gain_ref, edge_ref, form_ref, out_ref):
    scaled_values = far_ref[...].astype(jnp.float32) / gain_ref[...]
    share = cross_ref[...] + part_ref[...].astype(jnp.float32)
    grads = column_grad(share, scaled_values, 1.0, gain_ref[...]).astype(jnp.bfloat16)
    put_back(out_ref, [edge_ref[i] for i in range(2)], form_ref[0], grads)


def edge_body(mine_ref, part_ref, conv_ref, cot_ref, scale_ref, gain_ref, mix_ref, form_ref, base_ref, out_ref):
    values = conv_ref[...].astype(jnp.float32)
    share = mine_ref[...] + part_ref[...].astype(jnp.float32)
    grads = column_grad(share, values, scale_ref[:, :1], gain_ref[...])
    grads = cot_ref[...].astype(jnp.float32) + grads
    base_ref[...] = grads
    odd = lax.axis_index("patch") % 2
    mix = border_mix(mix_ref, conv_ref.shape[0], out_ref.shape[0], odd)
    put_back(out_ref, mix, form_ref[0], grads.astype(jnp.bfloat16))


def grad_body(base_ref, cross_ref, conv_ref, scale_ref, gain_ref, mix_ref, form_ref, grad_ref, inner_ref):
    values = conv_ref[...].astype(jnp.float32)
    share = cross_ref[...].astype(jnp.float32)
    grads = column_grad(share, values, scale_ref[:, :1], gain_ref[...])
    grads = (base_ref[...] + grads).astype(jnp.bfloat16)
    grad_ref[...] = grads
    odd = lax.axis_index("patch") % 2
    mix = border_mix(mix_ref, conv_ref.shape[0], inner_ref.shape[0], 1 - odd)
    put_back(inner_ref, mix, form_ref[0], grads)


def parity_rows(bound_ref, columns, border):
    chosen = picked(bound_ref, columns).astype(jnp.float32)
    low, high = chosen[:, :border], chosen[:, border:]
    inner = jnp.where(is_even(), high, low).astype(jnp.bfloat16)
    outer = jnp.where(is_even(), low, high).astype(jnp.bfloat16)
    return inner, outer


def own_body(grad_ref, mix_ref, form_ref, local_ref):
    columns = grad_ref.shape[0]
    grads = grad_ref[...]
    spread = shifted_back([mix_ref[i, :columns] for i in range(2)], grads)
    across = ((1,), (1,))
    rows = mm(stacked(spread), form_ref[0], across) + mm(stacked(grads), form_ref[1], across)
    local_ref[...] = grads.astype(jnp.float32) + unstacked(rows, columns)


def last_body(local_ref, inner_ref, outer_ref, other_ref, bound_ref, out_ref, held, sem):
    columns, width = local_ref.shape
    inner, outer = parity_rows(bound_ref, columns, inner_ref.shape[0])
    pick = jnp.concatenate([inner, outer, outer], axis=1)
    copies = []
    for b in range(width // BLOCK // 2):
        at = slice(2 * b * BLOCK, 2 * (b + 1) * BLOCK)
        rows = jnp.concatenate([inner_ref[:, at], outer_ref[:, at], other_ref[:, at]], axis=0)
        held[:, at] = (local_ref[:, at] + mm(pick, rows)).astype(jnp.bfloat16)
        copies.append(pltpu.make_async_copy(held.at[:, at], out_ref.at[:, at], sem.at[b]))
        copies[-1].start()
    for one in copies:
        one.wait()


def per_device(
    layer_input,
    cotangent,
    neighbours,
    boundary,
    gauge_index,
    gauge_angles,
    norm_gain,
    up_weight,
    down_weight,
    self_real,
    self_imag,
    near_real,
    near_imag,
):
    samples, columns, width = layer_input.shape
    devices = lax.axis_size("patch")
    rows, hidden = up_weight.shape
    border = boundary.shape[1] // 2
    span = hidden // TEAM
    fits = (
        lax.axis_size("level") == 1
        and samples == 1
        and devices % (2 * TEAM) == 0
        and width % (2 * BLOCK) == 0
        and hidden % (TEAM * 128) == 0
        and rows % 16 == 0
        and border % 16 == 0
        and 2 * border <= columns
        and width * span <= 1 << 20
        and gauge_angles.shape[0] % 128 == 0
        and columns == 128
    )
    if not fits:
        return general(
            layer_input,
            cotangent,
            neighbours,
            boundary,
            gauge_index,
            gauge_angles,
            norm_gain,
            up_weight,
            down_weight,
            self_real,
            self_imag,
            near_real,
            near_imag,
        )
    groups = devices // TEAM
    sentinel = columns + 2 * border
    extent = -(-sentinel // 128) * 128
    x = layer_input[0]
    cot = cotangent[0]

    def permute(value, pairs):
        return lax.ppermute(value, "patch", pairs)

    def swap(value, bits):
        return permute(value, [(i, i ^ bits) for i in range(devices)])

    def outer(value, bits=0):
        pairs = [(i ^ bits, (i - 1 + 2 * (i % 2)) % devices) for i in range(devices)]
        return permute(value, pairs)

    order = list(range(0, groups, 2)) + list(range(groups - 1, 0, -2))

    def around(value, shift):
        pairs = [
            (order[k] * TEAM + j, order[(k + shift) % groups] * TEAM + j)
            for k in range(groups)
            for j in range(TEAM)
        ]
        return permute(value, pairs)

    held = [
        x,
        cot,
        boundary,
        neighbours.T,
        gauge_index.T,
        gauge_angles.reshape(-1, 128),
        near_real,
        near_imag,
        self_real,
        self_imag,
        norm_gain.reshape(-1, 128),
    ]
    x, cot, boundary, *tables = call(
        lambda *refs: load_body(len(held), *refs),
        [struct(value.shape, value.dtype) for value in held],
        held,
        [pltpu.SemaphoreType.DMA((len(held),))],
        range(len(held)),
    )
    parts = call(
        weights_body,
        [struct((2, rows, span))] * TEAM,
        [up_weight, down_weight],
        [pltpu.SemaphoreType.DMA((2 * TEAM,))],
        (0, 1),
    )
    near_part = swap(parts[1], 1)
    far_parts = [swap(parts[2], 2), swap(parts[3], 3)]
    first = jnp.concatenate([parts[0], near_part], axis=1)
    second = jnp.concatenate(far_parts, axis=1)
    steps, chunks = [(0, 0), (0, 2)], [first, second]
    forth = [first, second]
    back = [first, second]
    half = groups // 2
    for s in range(1, half):
        for which in range(2):
            forth[which] = around(forth[which], 1)
            back[which] = around(back[which], -1)
            steps += [(-s, 2 * which), (s, 2 * which)]
            chunks += [forth[which], back[which]]
    last_chunks = []
    for which in range(2):
        last_chunks += [around(forth[which][:1], 1), around(back[which][1:], -1)]

    inner_rows, outer_rows = call(border_body, [struct((border, width))] * 2, [x, boundary])
    inner_rows = swap(inner_rows, 1)
    outer_rows = outer(outer_rows)
    cot_near = swap(cot, 1)
    cot_far = swap(cot, 2)
    cot_cross = swap(cot_far, 1)

    mix, form, gain = call(
        lambda *refs: prep_body(sentinel, *refs),
        [
            struct((2, extent, columns)),
            struct((2, BLOCK, BLOCK)),
            struct((1, width), jnp.float32),
        ],
        tables,
    )
    conv, norm, edge, scale = call(
        conv_body,
        [
            *[struct((columns, width))] * 2,
            struct((2, border, columns)),
            struct((columns, 128), jnp.float32),
        ],
        [x, inner_rows, outer_rows, mix, form, gain],
        [pltpu.VMEM((extent, width), jnp.bfloat16)],
    )
    norm_near = swap(norm, 1)
    norm_far = swap(norm, 2)
    norm_cross = swap(norm_far, 1)
    edge = swap(edge, 2)

    wide = struct((columns, width), jnp.float32)
    team = TEAM * columns
    tall = TEAM * rows
    ups, pre_a, back_sum, xa_last, g_last = call(
        lambda *refs: early_body(steps, groups, *refs),
        [
            struct((width, span)),
            struct((team // 2, span), jnp.float32),
            struct((team, span), jnp.float32),
            struct((team // 2, tall)),
            struct((team, tall)),
        ],
        [norm_near, norm, cot, cot_near, cot_far, cot_cross, *chunks],
        [
            pltpu.VMEM((team // 2, width), jnp.bfloat16),
            pltpu.VMEM((team, width), jnp.bfloat16),
            pltpu.VMEM((width, span), jnp.bfloat16),
        ],
    )
    pre_b, xb_last = call(
        lambda *refs: rest_body(groups, *refs),
        [struct((team // 2, span), jnp.float32), struct((team // 2, tall))],
        [norm_cross, norm_far, ups],
        [pltpu.VMEM((team // 2, width), jnp.bfloat16)],
    )
    ups, up_last, down_last, gate, send_cross = call(
        lambda *refs: send_body(groups, *refs),
        [
            struct((width, span)),
            *[struct((tall, span))] * 2,
            struct((columns, span)),
            struct((columns, width)),
        ],
        [ups, pre_b, back_sum, xb_last, g_last, *last_chunks],
        (),
        (),
        ((0, 0),),
    )
    received_cross = swap(send_cross, 1)
    cross = call(cross_body, wide, [gate, ups])
    crossing = call(join_body, struct((columns, width)), [cross, received_cross])
    crossed = swap(crossing, 2)
    mine, send = call(
        keep_body,
        [wide, struct((columns, width))],
        [ups, up_last, down_last, pre_a, back_sum, xa_last, g_last],
    )
    received = swap(send, 1)
    other_rows = call(
        other_body, struct((border, width)), [cross, received_cross, norm_far, gain, edge, form]
    )
    other_rows = outer(other_rows, 2)
    base, own_rows = call(
        edge_body,
        [wide, struct((border, width))],
        [mine, received, conv, cot, scale, gain, mix, form],
    )
    own_rows = outer(own_rows)
    grads, inner_back = call(
        grad_body,
        [struct((columns, width)), struct((border, width))],
        [base, crossed, conv, scale, gain, mix, form],
    )
    inner_back = swap(inner_back, 1)
    local = call(own_body, wide, [grads, mix, form])
    pieces = width // BLOCK // 2
    out = pl.pallas_call(
        last_body,
        out_shape=jax.ShapeDtypeStruct((columns, width), jnp.bfloat16),
        out_specs=pl.BlockSpec(memory_space=pl.ANY),
        scratch_shapes=[
            pltpu.VMEM((columns, width), jnp.bfloat16),
            pltpu.SemaphoreType.DMA((pieces,)),
        ],
    )(
        *(
            pltpu.with_memory_space_constraint(value, pltpu.VMEM)
            for value in (local, inner_back, own_rows, other_rows, boundary)
        )
    )
    return out[None]


def solution(mesh):
    in_specs = (
        P("groups", "patch", "level"),
        P("groups", "patch", "level"),
        P("patch", None),
        P("patch", None),
        P("patch", None),
        P(),
        P(),
        P("patch", "level"),
        P("patch", "level"),
        P(),
        P(),
        P(),
        P(),
    )
    out_specs = P("groups", "patch", "level")

    return jax.shard_map(
        per_device, mesh=mesh, in_specs=in_specs, out_specs=out_specs, check_vma=False
    )
```

```python
import jax
import jax.numpy as jnp
from jax import lax
from jax.experimental import pallas as pl
from jax.experimental.pallas import tpu as pltpu
from jax.sharding import PartitionSpec as P


CH = 64


def padded(shard, sides, width):
    for axis, dim in sides:
        devices, length = (lax.axis_size(axis), shard.shape[dim])
        up = [(i, (i + 1) % devices) for i in range(devices)]
        down = [(j, i) for i, j in up]
        last = lax.slice_in_dim(shard, length - width, length, axis=dim)
        leading = lax.slice_in_dim(shard, 0, width, axis=dim)
        before = lax.ppermute(last, axis, up)
        after = lax.ppermute(leading, axis, down)
        shard = jnp.concatenate([before, shard, after], axis=dim)
    return shard


def real_form(real_part, imag_part):
    upper = jnp.concatenate([real_part, imag_part], axis=1)
    lower = jnp.concatenate([-imag_part, real_part], axis=1)
    return jnp.concatenate([upper, lower], axis=0)


def rotate_quarter(values, channels):
    shape = values.shape
    split = values.reshape(shape[:-1] + (shape[-1] // channels, 2, channels // 2))
    turned = jnp.stack([-split[..., 1, :], split[..., 0, :]], axis=-2)
    return turned.reshape(shape)


def per_level(values, form, channels):
    shape = values.shape
    split = values.reshape(shape[:-1] + (shape[-1] // channels, channels))
    result = jnp.einsum("bclw,wv->bclv", split, form, preferred_element_type=jnp.float32)
    return result.reshape(shape)


def mlp_back(columns_in, grads, norm_gain, up_mat, down_mat):
    values = columns_in.astype(jnp.float32)
    root_scale = lax.rsqrt(jnp.mean(values * values, axis=-1, keepdims=True) + 1e-05)
    normed = (values * root_scale * norm_gain).astype(jnp.bfloat16)
    pre_act = jnp.einsum("brw,wh->brh", normed, up_mat, preferred_element_type=jnp.float32)
    back_hidden = jnp.einsum("brw,wh->brh", grads, down_mat, preferred_element_type=jnp.float32)
    sigmoid_pre = jax.nn.sigmoid(pre_act)
    grad_pre = (back_hidden * sigmoid_pre * (1.0 + pre_act * (1.0 - sigmoid_pre))).astype(
        jnp.bfloat16
    )
    grad_normed = jnp.einsum("brh,wh->brw", grad_pre, up_mat, preferred_element_type=jnp.float32)
    mixed_mean = jnp.mean(norm_gain * grad_normed * values, axis=-1, keepdims=True)
    return (
        root_scale * norm_gain * grad_normed
        - values * root_scale * root_scale * root_scale * mixed_mean
    )


def general(
    layer_input,
    cotangent,
    neighbours,
    boundary,
    gauge_index,
    gauge_angles,
    norm_gain,
    up_weight,
    down_weight,
    self_real,
    self_imag,
    near_real,
    near_imag,
):
    samples, columns, width = layer_input.shape
    border = boundary.shape[1] // 2
    low_rows = boundary[0, :border]
    high_rows = boundary[0, border:]
    sent = jnp.stack([layer_input[:, low_rows], layer_input[:, high_rows]])
    cycle = padded(sent, (("patch", 0),), 1)
    extended = jnp.concatenate(
        [layer_input, cycle[0], cycle[3], jnp.zeros((samples, 1, width), jnp.bfloat16)], axis=1
    )
    sentinel = columns + 2 * border
    present = (neighbours < sentinel).astype(jnp.float32)
    edge_weight = present / jnp.sum(present, axis=1, keepdims=True)
    phase = gauge_angles[gauge_index]
    cosine = jnp.cos(phase)
    sine = jnp.sin(phase)
    near_form = real_form(near_real, near_imag)
    self_form = real_form(self_real, self_imag)
    gathered = jnp.zeros((samples, columns, width), jnp.float32)
    for entry in range(6):
        near = extended[:, neighbours[:, entry]].astype(jnp.float32)
        turned = rotate_quarter(near, CH)
        gathered = (
            gathered
            + (
                cosine[None, :, entry : entry + 1] * near
                + sine[None, :, entry : entry + 1] * turned
            )
            * edge_weight[None, :, entry : entry + 1]
        )
    gathered = gathered.astype(jnp.bfloat16)
    convolved = per_level(gathered, near_form, CH) + per_level(layer_input, self_form, CH)
    conv_out = (layer_input.astype(jnp.float32) + convolved).astype(jnp.bfloat16)
    conv_out = lax.optimization_barrier(conv_out)
    up_part, down_part = (
        lax.all_gather(up_weight, "patch", axis=0, tiled=True),
        lax.all_gather(down_weight, "patch", axis=0, tiled=True),
    )
    up_whole, down_whole = (
        lax.all_gather(up_part, "level", axis=1, tiled=True),
        lax.all_gather(down_part, "level", axis=1, tiled=True),
    )
    half_cols, half_grads = (
        lax.all_to_all(conv_out, "level", split_axis=1, concat_axis=2, tiled=True),
        lax.all_to_all(cotangent, "level", split_axis=1, concat_axis=2, tiled=True),
    )
    terms = mlp_back(half_cols, half_grads, norm_gain, up_whole, down_whole)
    column_grad = (half_grads.astype(jnp.float32) + terms).astype(jnp.bfloat16)
    grad_conv = lax.all_to_all(column_grad, "level", split_axis=2, concat_axis=1, tiled=True)
    grad_conv = lax.optimization_barrier(grad_conv)
    pulled = per_level(grad_conv, near_form.T, CH)
    own_back = per_level(grad_conv, self_form.T, CH)
    pulled_turn = rotate_quarter(pulled, CH)
    spread = jnp.zeros((samples, sentinel + 1, width), jnp.float32)
    for entry in range(6):
        edges = (
            cosine[None, :, entry : entry + 1] * pulled
            - sine[None, :, entry : entry + 1] * pulled_turn
        ) * edge_weight[None, :, entry : entry + 1]
        spread = spread.at[:, neighbours[:, entry]].add(edges)
    back_sent = jnp.stack(
        [spread[:, columns : columns + border], spread[:, columns + border : sentinel]]
    )
    back_cycle = padded(back_sent.astype(jnp.bfloat16), (("patch", 0),), 1).astype(back_sent.dtype)
    local_terms = (
        spread[:, :columns].at[:, low_rows].add(back_cycle[0]).at[:, high_rows].add(back_cycle[3])
    )
    return (grad_conv.astype(jnp.float32) + own_back + local_terms).astype(jnp.bfloat16)


BLOCK = 256
TEAM = 4


def iota(shape, dim):
    return lax.broadcasted_iota(jnp.int32, shape, dim)


def mm(a, b, dims=((1,), (0,))):
    return lax.dot_general(a, b, (dims, ((), ())), preferred_element_type=jnp.float32)


def turn(values):
    width = values.shape[1]
    half = CH // 2
    later = pltpu.roll(values, width - half, 1)
    earlier = pltpu.roll(values, half, 1)
    return jnp.where(iota(values.shape, 1) % CH < half, -later, earlier)


def stacked(values):
    width = values.shape[1]
    return jnp.concatenate([values[:, at : at + BLOCK] for at in range(0, width, BLOCK)], axis=0)


def unstacked(values, rows):
    count = values.shape[0]
    return jnp.concatenate([values[at : at + rows] for at in range(0, count, rows)], axis=1)


def call(body, outs, args, scratch=(), raw=(), aliases=()):
    vmem = pl.BlockSpec(memory_space=pltpu.VMEM)
    args = [
        pltpu.with_memory_space_constraint(value, pltpu.HBM if i in raw else pltpu.VMEM)
        for i, value in enumerate(args)
    ]
    specs = [pl.BlockSpec(memory_space=pl.ANY) if i in raw else vmem for i in range(len(args))]
    return pl.pallas_call(
        body,
        out_shape=outs,
        in_specs=specs,
        out_specs=jax.tree.map(lambda _: vmem, outs),
        scratch_shapes=scratch,
        input_output_aliases=dict(aliases),
        compiler_params=pltpu.CompilerParams(vmem_limit_bytes=24 << 20),
    )(*args)


def struct(shape, dtype=jnp.bfloat16):
    return pltpu.VMEM(shape, dtype)


def picked(bound_ref, columns):
    count = bound_ref.shape[1]
    return (iota((columns, count), 0) == bound_ref[...]).astype(jnp.bfloat16)


def copy_all(pairs, sem):
    copies = [pltpu.make_async_copy(src, dst, sem.at[i]) for i, (src, dst) in enumerate(pairs)]
    for one in copies:
        one.start()
    for one in copies:
        one.wait()


def weights_body(up_ref, down_ref, *refs):
    *parts, sem = refs
    mine = lax.axis_index("patch") % TEAM
    span = parts[0].shape[2]
    pairs = []
    for k in range(TEAM):
        at = pl.multiple_of((mine ^ k) * span, 128)
        for which, ref in enumerate((up_ref, down_ref)):
            pairs.append((ref.at[:, pl.ds(at, span)], parts[k].at[which]))
    copy_all(pairs, sem)


def load_body(count, *refs):
    copy_all(list(zip(refs[:count], refs[count : 2 * count])), refs[-1])


def is_even():
    return lax.axis_index("patch") % 2 == 0


def border_body(x_ref, bound_ref, inner_ref, outer_ref):
    border = inner_ref.shape[0]
    rows = mm(picked(bound_ref, x_ref.shape[0]), x_ref[...], ((0,), (0,))).astype(jnp.bfloat16)
    low, high = rows[:border], rows[border:]
    inner_ref[...] = jnp.where(is_even(), high, low)
    outer_ref[...] = jnp.where(is_even(), low, high)


def spread_form(real_ref, imag_ref):
    half = real_ref.shape[0]
    tall = (iota((BLOCK, half), 0) % half == iota((BLOCK, half), 1)).astype(jnp.bfloat16)

    def tiled(ref):
        rows = mm(tall, ref[...]).astype(jnp.bfloat16)
        return mm(rows, tall, ((1,), (1,)))

    real, imag = tiled(real_ref), tiled(imag_ref)
    row, col = iota((BLOCK, BLOCK), 0), iota((BLOCK, BLOCK), 1)
    row_real = row % CH < half
    col_real = col % CH < half
    form = jnp.where(row_real == col_real, real, jnp.where(row_real, imag, -imag))
    return jnp.where(row // CH == col // CH, form, 0.0).astype(jnp.bfloat16)


def prep_body(sentinel, near_ref, index_ref, angle_ref, nr, ni, sr, si, gains, mix_ref, form_ref, gain_ref):
    entries, columns = near_ref.shape
    table = angle_ref[...]
    index = index_ref[...]
    phases = []
    for k in range(entries):
        spot = jnp.broadcast_to(index[k : k + 1], (table.shape[0], columns))
        found = jnp.take_along_axis(table, spot % 128, axis=1)
        hit = iota(found.shape, 0) == spot // 128
        phases.append(jnp.sum(jnp.where(hit, found, 0.0), axis=0, keepdims=True))
    phase = jnp.concatenate(phases, axis=0)
    near = near_ref[...]
    present = (near < sentinel).astype(jnp.float32)
    weight = present / jnp.sum(present, axis=0, keepdims=True)
    cosine, sine = jnp.cos(phase) * weight, jnp.sin(phase) * weight
    height = mix_ref.shape[1]
    place = iota((height, columns), 0)
    mix_cos = jnp.zeros((height, columns), jnp.float32)
    mix_sin = jnp.zeros((height, columns), jnp.float32)
    for k in range(entries):
        hit = near[k : k + 1] == place
        mix_cos = mix_cos + jnp.where(hit, cosine[k : k + 1], 0.0)
        mix_sin = mix_sin + jnp.where(hit, sine[k : k + 1], 0.0)
    mix_ref[0] = mix_cos.astype(jnp.bfloat16)
    mix_ref[1] = mix_sin.astype(jnp.bfloat16)
    gain_ref[...] = jnp.concatenate([gains[r : r + 1] for r in range(gains.shape[0])], axis=1)
    form_ref[0] = spread_form(nr, ni)
    form_ref[1] = spread_form(sr, si)


def border_mix(mix_ref, columns, border, which):
    at = pl.multiple_of(columns + border * which, 16)
    return [mix_ref[i, pl.ds(at, border)] for i in range(2)]


def conv_body(x_ref, inner_ref, outer_ref, mix_ref, form_ref, gain_ref, conv_ref, norm_ref, edge_ref, scale_ref, ext):
    columns, width = x_ref.shape
    border = inner_ref.shape[0]
    odd = lax.axis_index("patch") % 2
    ext[:columns] = x_ref[...]
    ext[pl.ds(pl.multiple_of(columns + border * (1 - odd), 16), border)] = inner_ref[...]
    ext[pl.ds(pl.multiple_of(columns + border * odd, 16), border)] = outer_ref[...]
    rest = ext.shape[0] - columns - 2 * border
    if rest:
        ext[columns + 2 * border :] = jnp.zeros((rest, width), jnp.bfloat16)
    source = ext[...]
    gathered = mm(jnp.concatenate([mix_ref[0], mix_ref[1]], axis=1), source, ((0,), (0,)))
    gathered = (gathered[:columns] + turn(gathered[columns:])).astype(jnp.bfloat16)
    x = x_ref[...]
    folded = mm(stacked(gathered), form_ref[0]) + mm(stacked(x), form_ref[1])
    out = (x.astype(jnp.float32) + unstacked(folded, columns)).astype(jnp.bfloat16)
    conv_ref[...] = out
    out = out.astype(jnp.float32)
    square = out * out
    scale = lax.rsqrt(jnp.sum(square, axis=1, keepdims=True) / width + 1e-05)
    norm_ref[...] = (conv_ref[...].astype(jnp.float32) * scale * gain_ref[...]).astype(jnp.bfloat16)
    scale_ref[...] = jnp.broadcast_to(scale, scale_ref.shape)
    across = jnp.broadcast_to(scale, (columns, columns)).T[:1]
    for i, rows in enumerate(border_mix(mix_ref, columns, border, odd)):
        edge_ref[i] = (rows.astype(jnp.float32) * across).astype(jnp.bfloat16)


def ring_place(group, groups):
    return jnp.where(group % 2 == 0, group // 2, groups - 1 - group // 2)


def ring_group(place, groups):
    return jnp.where(place < groups // 2, 2 * place, 2 * (groups - 1 - place) + 1)


STACK = (3, 2, 1, 0)


def far_owner(groups):
    place = ring_place(lax.axis_index("patch") // TEAM, groups)
    return ring_group((place + groups // 2) % groups, groups)


def take_columns(owner, groups, pairs):
    for g in range(groups):

        @pl.when(owner == g)
        def _():
            for source, target in pairs:
                tall = target.shape[1]
                target[...] = source[:, g * tall : (g + 1) * tall]


def early_body(steps, groups, *refs):
    norms, grads, chunks = refs[:2], refs[2 : 2 + TEAM], refs[2 + TEAM : 2 + TEAM + len(steps)]
    ups, pre_ref, back_ref, x_last, g_last, xs, gs, downs = refs[2 + TEAM + len(steps) :]
    columns = norms[0].shape[0]
    span = ups.shape[1]
    me = lax.axis_index("patch")
    group, member = me // TEAM, me % TEAM
    place = ring_place(group, groups)
    for k in range(2):
        xs[k * columns : (k + 1) * columns] = norms[k][...]
    for k, m in enumerate(STACK):
        gs[k * columns : (k + 1) * columns] = grads[m][...]
    for (shift, first), ref in zip(steps, chunks):
        rows = ref.shape[1] // 2
        owner = ring_group((place + shift + groups) % groups, groups)
        for half in range(2):
            at = pl.multiple_of((owner * TEAM + (member ^ (first + half))) * rows, 16)
            part = slice(half * rows, (half + 1) * rows)
            ups[pl.ds(at, rows)] = ref[0, part]
            downs[pl.ds(at, rows)] = ref[1, part]
    owner = far_owner(groups)
    tall = TEAM * rows
    blank = jnp.zeros((tall, span), jnp.bfloat16)
    at = pl.multiple_of(owner * tall, 16)
    ups[pl.ds(at, tall)] = blank
    downs[pl.ds(at, tall)] = blank
    take_columns(owner, groups, ((xs, x_last), (gs, g_last)))
    pre_ref[...] = mm(xs[...], ups[...])
    back_ref[...] = mm(gs[...], downs[...])


def rest_body(groups, cross_ref, far_ref, ups, pre_ref, x_last, xs):
    columns = cross_ref.shape[0]
    xs[:columns] = cross_ref[...]
    xs[columns:] = far_ref[...]
    take_columns(far_owner(groups), groups, ((xs, x_last),))
    pre_ref[...] = mm(xs[...], ups[...])


def gated(pre_act, back):
    gate = jax.nn.sigmoid(pre_act)
    return (back * gate * (1.0 + pre_act * (1.0 - gate))).astype(jnp.bfloat16)


def send_body(groups, ups_in, pre_ref, back_ref, x_last, g_last, *refs):
    parts, (ups, up, down, send_ref) = refs[:4], refs[4:]
    member = lax.axis_index("patch") % TEAM
    rows = parts[0].shape[1] // 2
    for k in range(2):
        for half in range(2):
            at = pl.multiple_of((member ^ (2 * k + half)) * rows, 16)
            part = slice(half * rows, (half + 1) * rows)
            up[pl.ds(at, rows)] = parts[2 * k][0, part]
            down[pl.ds(at, rows)] = parts[2 * k + 1][0, part]
    tall = up.shape[0]
    ups[pl.ds(pl.multiple_of(far_owner(groups) * tall, 16), tall)] = up[...]
    columns = send_ref.shape[0]
    one = slice(0, columns)
    pre_act = pre_ref[one] + mm(x_last[one], up[...])
    grad_pre = gated(pre_act, back_ref[one] + mm(g_last[one], down[...]))
    send_ref[...] = mm(grad_pre, ups[...], ((1,), (1,))).astype(jnp.bfloat16)


def cross_body(ups, up, down, pre_ref, back_ref, x_last, g_last, cross_ref):
    columns = cross_ref.shape[0]
    one = slice(columns, 2 * columns)
    pre_act = pre_ref[one] + mm(x_last[one], up[...])
    grad_pre = gated(pre_act, back_ref[one] + mm(g_last[one], down[...]))
    cross_ref[...] = mm(grad_pre, ups[...], ((1,), (1,)))


def keep_body(ups, up, down, pre_ref, back_ref, x_last, g_last, mine_ref, send_ref):
    columns = mine_ref.shape[0]
    two = slice(2 * columns, 4 * columns)
    pre_act = pre_ref[...] + mm(x_last[...], up[...])
    grad_pre = gated(pre_act, back_ref[two] + mm(g_last[two], down[...]))
    rows = mm(grad_pre, ups[...], ((1,), (1,)))
    send_ref[...] = rows[:columns].astype(jnp.bfloat16)
    mine_ref[...] = rows[columns:]


def shifted_back(mix, grads):
    rows = mix[0].shape[0]
    spread = mm(jnp.concatenate(mix, axis=0), grads)
    return (spread[:rows] - turn(spread[rows:])).astype(jnp.bfloat16)


def join_body(cross_ref, part_ref, out_ref):
    out_ref[...] = (cross_ref[...] + part_ref[...].astype(jnp.float32)).astype(jnp.bfloat16)


def column_grad(grad_normed, values, scale, gain):
    scaled = gain * grad_normed
    mixed = jnp.sum(scaled * values, axis=1, keepdims=True) / values.shape[1]
    return scale * scaled - values * (scale * scale * scale * mixed)


def put_back(target, mix, form, grads):
    rows = mm(stacked(shifted_back(mix, grads)), form, ((1,), (1,))).astype(jnp.bfloat16)
    target[...] = unstacked(rows, target.shape[0])


def other_body(cross_ref, part_ref, far_ref, gain_ref, edge_ref, form_ref, out_ref):
    scaled_values = far_ref[...].astype(jnp.float32) / gain_ref[...]
    share = cross_ref[...] + part_ref[...].astype(jnp.float32)
    grads = column_grad(share, scaled_values, 1.0, gain_ref[...]).astype(jnp.bfloat16)
    put_back(out_ref, [edge_ref[i] for i in range(2)], form_ref[0], grads)


def edge_body(mine_ref, part_ref, conv_ref, cot_ref, scale_ref, gain_ref, mix_ref, form_ref, base_ref, out_ref):
    values = conv_ref[...].astype(jnp.float32)
    share = mine_ref[...] + part_ref[...].astype(jnp.float32)
    grads = column_grad(share, values, scale_ref[:, :1], gain_ref[...])
    grads = cot_ref[...].astype(jnp.float32) + grads
    base_ref[...] = grads
    odd = lax.axis_index("patch") % 2
    mix = border_mix(mix_ref, conv_ref.shape[0], out_ref.shape[0], odd)
    put_back(out_ref, mix, form_ref[0], grads.astype(jnp.bfloat16))


def grad_body(base_ref, cross_ref, conv_ref, scale_ref, gain_ref, mix_ref, form_ref, grad_ref, inner_ref):
    values = conv_ref[...].astype(jnp.float32)
    share = cross_ref[...].astype(jnp.float32)
    grads = column_grad(share, values, scale_ref[:, :1], gain_ref[...])
    grads = (base_ref[...] + grads).astype(jnp.bfloat16)
    grad_ref[...] = grads
    odd = lax.axis_index("patch") % 2
    mix = border_mix(mix_ref, conv_ref.shape[0], inner_ref.shape[0], 1 - odd)
    put_back(inner_ref, mix, form_ref[0], grads)


def parity_rows(bound_ref, columns, border):
    chosen = picked(bound_ref, columns).astype(jnp.float32)
    low, high = chosen[:, :border], chosen[:, border:]
    inner = jnp.where(is_even(), high, low).astype(jnp.bfloat16)
    outer = jnp.where(is_even(), low, high).astype(jnp.bfloat16)
    return inner, outer


def own_body(grad_ref, mix_ref, form_ref, local_ref):
    columns = grad_ref.shape[0]
    grads = grad_ref[...]
    spread = shifted_back([mix_ref[i, :columns] for i in range(2)], grads)
    across = ((1,), (1,))
    rows = mm(stacked(spread), form_ref[0], across) + mm(stacked(grads), form_ref[1], across)
    local_ref[...] = grads.astype(jnp.float32) + unstacked(rows, columns)


def last_body(local_ref, inner_ref, outer_ref, other_ref, bound_ref, out_ref, held, sem):
    columns, width = local_ref.shape
    inner, outer = parity_rows(bound_ref, columns, inner_ref.shape[0])
    pick = jnp.concatenate([inner, outer, outer], axis=1)
    copies = []
    for b in range(width // BLOCK // 2):
        at = slice(2 * b * BLOCK, 2 * (b + 1) * BLOCK)
        rows = jnp.concatenate([inner_ref[:, at], outer_ref[:, at], other_ref[:, at]], axis=0)
        held[:, at] = (local_ref[:, at] + mm(pick, rows)).astype(jnp.bfloat16)
        copies.append(pltpu.make_async_copy(held.at[:, at], out_ref.at[:, at], sem.at[b]))
        copies[-1].start()
    for one in copies:
        one.wait()


def per_device(
    layer_input,
    cotangent,
    neighbours,
    boundary,
    gauge_index,
    gauge_angles,
    norm_gain,
    up_weight,
    down_weight,
    self_real,
    self_imag,
    near_real,
    near_imag,
):
    samples, columns, width = layer_input.shape
    devices = lax.axis_size("patch")
    rows, hidden = up_weight.shape
    border = boundary.shape[1] // 2
    span = hidden // TEAM
    fits = (
        lax.axis_size("level") == 1
        and samples == 1
        and devices % (2 * TEAM) == 0
        and width % (2 * BLOCK) == 0
        and hidden % (TEAM * 128) == 0
        and rows % 16 == 0
        and border % 16 == 0
        and 2 * border <= columns
        and width * span <= 1 << 20
        and gauge_angles.shape[0] % 128 == 0
        and columns == 128
    )
    if not fits:
        return general(
            layer_input,
            cotangent,
            neighbours,
            boundary,
            gauge_index,
            gauge_angles,
            norm_gain,
            up_weight,
            down_weight,
            self_real,
            self_imag,
            near_real,
            near_imag,
        )
    groups = devices // TEAM
    sentinel = columns + 2 * border
    extent = -(-sentinel // 128) * 128
    x = layer_input[0]
    cot = cotangent[0]

    def permute(value, pairs):
        return lax.ppermute(value, "patch", pairs)

    def swap(value, bits):
        return permute(value, [(i, i ^ bits) for i in range(devices)])

    def outer(value, bits=0):
        pairs = [(i ^ bits, (i - 1 + 2 * (i % 2)) % devices) for i in range(devices)]
        return permute(value, pairs)

    order = list(range(0, groups, 2)) + list(range(groups - 1, 0, -2))

    def around(value, shift):
        pairs = [
            (order[k] * TEAM + j, order[(k + shift) % groups] * TEAM + j)
            for k in range(groups)
            for j in range(TEAM)
        ]
        return permute(value, pairs)

    held = [
        x,
        cot,
        boundary,
        neighbours.T,
        gauge_index.T,
        gauge_angles.reshape(-1, 128),
        near_real,
        near_imag,
        self_real,
        self_imag,
        norm_gain.reshape(-1, 128),
    ]
    x, cot, boundary, *tables = call(
        lambda *refs: load_body(len(held), *refs),
        [struct(value.shape, value.dtype) for value in held],
        held,
        [pltpu.SemaphoreType.DMA((len(held),))],
        range(len(held)),
    )
    parts = call(
        weights_body,
        [struct((2, rows, span))] * TEAM,
        [up_weight, down_weight],
        [pltpu.SemaphoreType.DMA((2 * TEAM,))],
        (0, 1),
    )
    near_part = swap(parts[1], 1)
    far_parts = [swap(parts[2], 2), swap(parts[3], 3)]
    first = jnp.concatenate([parts[0], near_part], axis=1)
    second = jnp.concatenate(far_parts, axis=1)
    steps, chunks = [(0, 0), (0, 2)], [first, second]
    forth = [first, second]
    back = [first, second]
    half = groups // 2
    for s in range(1, half):
        for which in range(2):
            forth[which] = around(forth[which], 1)
            back[which] = around(back[which], -1)
            steps += [(-s, 2 * which), (s, 2 * which)]
            chunks += [forth[which], back[which]]
    last_chunks = []
    for which in range(2):
        last_chunks += [around(forth[which][:1], 1), around(back[which][1:], -1)]

    inner_rows, outer_rows = call(border_body, [struct((border, width))] * 2, [x, boundary])
    inner_rows = swap(inner_rows, 1)
    outer_rows = outer(outer_rows)
    cot_near = swap(cot, 1)
    cot_far = swap(cot, 2)
    cot_cross = swap(cot_far, 1)

    mix, form, gain = call(
        lambda *refs: prep_body(sentinel, *refs),
        [
            struct((2, extent, columns)),
            struct((2, BLOCK, BLOCK)),
            struct((1, width), jnp.float32),
        ],
        tables,
    )
    conv, norm, edge, scale = call(
        conv_body,
        [
            *[struct((columns, width))] * 2,
            struct((2, border, columns)),
            struct((columns, 128), jnp.float32),
        ],
        [x, inner_rows, outer_rows, mix, form, gain],
        [pltpu.VMEM((extent, width), jnp.bfloat16)],
    )
    norm_near = swap(norm, 1)
    norm_far = swap(norm, 2)
    norm_cross = swap(norm_far, 1)
    edge = swap(edge, 2)

    wide = struct((columns, width), jnp.float32)
    team = TEAM * columns
    tall = TEAM * rows
    ups, pre_a, back_sum, xa_last, g_last = call(
        lambda *refs: early_body(steps, groups, *refs),
        [
            struct((width, span)),
            struct((team // 2, span), jnp.float32),
            struct((team, span), jnp.float32),
            struct((team // 2, tall)),
            struct((team, tall)),
        ],
        [norm_near, norm, cot, cot_near, cot_far, cot_cross, *chunks],
        [
            pltpu.VMEM((team // 2, width), jnp.bfloat16),
            pltpu.VMEM((team, width), jnp.bfloat16),
            pltpu.VMEM((width, span), jnp.bfloat16),
        ],
    )
    pre_b, xb_last = call(
        lambda *refs: rest_body(groups, *refs),
        [struct((team // 2, span), jnp.float32), struct((team // 2, tall))],
        [norm_cross, norm_far, ups],
        [pltpu.VMEM((team // 2, width), jnp.bfloat16)],
    )
    ups, up_last, down_last, send_cross = call(
        lambda *refs: send_body(groups, *refs),
        [
            struct((width, span)),
            *[struct((tall, span))] * 2,
            struct((columns, width)),
        ],
        [ups, pre_b, back_sum, xb_last, g_last, *last_chunks],
        (),
        (),
        ((0, 0),),
    )
    received_cross = swap(send_cross, 1)
    cross = call(cross_body, wide, [ups, up_last, down_last, pre_b, back_sum, xb_last, g_last])
    crossing = call(join_body, struct((columns, width)), [cross, received_cross])
    crossed = swap(crossing, 2)
    mine, send = call(
        keep_body,
        [wide, struct((columns, width))],
        [ups, up_last, down_last, pre_a, back_sum, xa_last, g_last],
    )
    received = swap(send, 1)
    other_rows = call(
        other_body, struct((border, width)), [cross, received_cross, norm_far, gain, edge, form]
    )
    other_rows = outer(other_rows, 2)
    base, own_rows = call(
        edge_body,
        [wide, struct((border, width))],
        [mine, received, conv, cot, scale, gain, mix, form],
    )
    own_rows = outer(own_rows)
    grads, inner_back = call(
        grad_body,
        [struct((columns, width)), struct((border, width))],
        [base, crossed, conv, scale, gain, mix, form],
    )
    inner_back = swap(inner_back, 1)
    local = call(own_body, wide, [grads, mix, form])
    pieces = width // BLOCK // 2
    out = pl.pallas_call(
        last_body,
        out_shape=jax.ShapeDtypeStruct((columns, width), jnp.bfloat16),
        out_specs=pl.BlockSpec(memory_space=pl.ANY),
        scratch_shapes=[
            pltpu.VMEM((columns, width), jnp.bfloat16),
            pltpu.SemaphoreType.DMA((pieces,)),
        ],
    )(
        *(
            pltpu.with_memory_space_constraint(value, pltpu.VMEM)
            for value in (local, inner_back, own_rows, other_rows, boundary)
        )
    )
    return out[None]


def solution(mesh):
    in_specs = (
        P("groups", "patch", "level"),
        P("groups", "patch", "level"),
        P("patch", None),
        P("patch", None),
        P("patch", None),
        P(),
        P(),
        P("patch", "level"),
        P("patch", "level"),
        P(),
        P(),
        P(),
        P(),
    )
    out_specs = P("groups", "patch", "level")

    return jax.shard_map(
        per_device, mesh=mesh, in_specs=in_specs, out_specs=out_specs, check_vma=False
    )
```
